128 devices in a mesh: slab: 16 (over y, z), chan: 8 (over x, core).
Axes of the slice: x: 4, y: 4, z: 4, core: 2. Of those that a mesh axis runs over, the one named last changes fastest.
Arguments:
- field: bfloat16 [32, 256, 256, 256], P('chan', 'slab'), may hold values from -6 to 6
- forcing: bfloat16 [256, 256, 256], P('slab', 'chan'), may hold values from -6 to 6
- slot_column: int32 [16, 128], replicated, may hold values from -1 to 1023, as said below
- w_spec: bfloat16 [2, 32, 32, 32768], P(None, 'chan', None, 'slab'), may hold values from -12 to 12
- skip_gain: float32 [32], P('chan'), may hold values from 0.5 to 1.5
- bias: float32 [32], P('chan'), may hold values from -3 to 3
Outputs:
- output: bfloat16 [32, 256, 256, 256], P('chan', 'slab')
- gradient: bfloat16 [32, 256, 256, 256], P('chan', 'slab')
The draws below stay inside these ranges and needn't reach their ends.
Inputs may be any that keep to these rules, and one draw needn't show every extreme that they name: `slot_column`: every kept pair index 0 to 1023 appears exactly once in the table; empty slots hold -1; the busiest slab device fills all 128 of its slots.
All inputs are finite; a program needn't handle non-finite values.
Results may differ from the reference program's by a relative error of at most 0.022.
Values may be sent and summed in bfloat16 or wider, within the bound.
A program may use at most 128 MiB of HBM per device.

```python
import math
import jax
import jax.numpy as jnp
from jax import lax

GRID = 256
CH = 32
KXY = 32
KZ = 16
CAP = 128
N_SLAB = 16


def draw_slot_column(key, part):
    columns = KXY * KXY
    slabs = 2 * columns // CAP
    average = columns // slabs
    key_delta = jax.random.fold_in(key, 11)
    key_order = jax.random.fold_in(key, 23)
    key_cols = jax.random.fold_in(key, 37)
    deltas = jax.random.randint(key_delta, (slabs // 2,), 0, average // 2 + 1).astype(jnp.int32)
    deltas = deltas.at[0].set(average)
    paired = jnp.stack([average + deltas, average - deltas], axis=1).reshape(slabs)
    order = jax.random.permutation(key_order, slabs)
    counts = jnp.zeros((slabs,), jnp.int32).at[order].set(paired)
    offsets = jnp.cumsum(counts) - counts
    shuffled = jax.random.permutation(key_cols, columns).astype(jnp.int32)
    slot_ids = jnp.arange(CAP, dtype=jnp.int32)
    wanted = offsets[:, None] + slot_ids[None, :]
    occupied = slot_ids[None, :] < counts[:, None]
    picked = shuffled[jnp.clip(wanted, 0, columns - 1)]
    return jnp.where(occupied, picked, -1).astype(jnp.int32)


def shard_levels(stream_key, shape, shards, low, top_value):
    factor_of = 1.0
    for axis_at, shards_of in shards:
        steps = jax.random.uniform(jax.random.fold_in(jax.random.fold_in(stream_key, 6), axis_at), (shards_of,), jnp.float32, low / len(shards), top_value / len(shards))
        factor_of = factor_of * jnp.repeat(jnp.exp(steps), shape[axis_at] // shards_of).reshape((-1,) + (1,) * (len(shape) - 1 - axis_at))
    return factor_of


def noise(rng, dims, deviation, most, split=(), held_as=jnp.bfloat16):
    values = deviation * jax.random.normal(rng, dims, jnp.float32)
    if split:
        values = values * shard_levels(rng, dims, split, -0.22, 0.18)
    return jnp.clip(values, -most, most).astype(held_as)


def setup_inputs(seed: int = 0) -> dict:
    splits = jax.random.split(jax.random.key(seed), 7)
    field = noise(splits[0], (CH, GRID, GRID, GRID), 1.0, 6.0, ((0, 8), (1, 16)))
    forcing = noise(splits[1], (GRID, GRID, GRID), 1.0, 6.0, ((0, 16), (1, 8)))
    slot_column = draw_slot_column(jax.random.fold_in(splits[6], 71), 0)
    w_spec = noise(splits[3], (2, CH, CH, N_SLAB * CAP * KZ), 2.0, 12.0, ((1, 8), (3, 16)))
    skip_gain = jnp.clip(0.5 + 1.0 * jax.random.uniform(splits[4], (CH,), jnp.float32) ** shard_levels(splits[4], (CH,), ((0, 8),), -0.2, 0.2), 0.5, 1.5)
    bias = noise(splits[5], (CH,), 0.5, 3.0, ((0, 8),), jnp.float32)
    return {"field": field, "forcing": forcing, "slot_column": slot_column, "w_spec": w_spec, "skip_gain": skip_gain, "bias": bias}


def angle_pair(freqs, coords, grid_len):
    turns = freqs[:, None] * coords[None, :] % grid_len
    angle = turns.astype(jnp.float32) * (2.0 * math.pi / grid_len)
    return (jnp.cos(angle), jnp.sin(angle))

def plane_tables(kept, grid_len):
    freqs = jnp.arange(kept, dtype=jnp.int32) - kept // 2
    coords = jnp.arange(grid_len, dtype=jnp.int32)
    cosine, sine = angle_pair(freqs, coords, grid_len)
    row_table = jnp.concatenate([cosine.T, -sine.T], axis=1).astype(jnp.bfloat16)
    col_table = jnp.stack([cosine, sine]).astype(jnp.bfloat16)
    return (row_table, col_table)

def depth_table(kept_z, start, count, grid_len):
    freqs = jnp.arange(kept_z, dtype=jnp.int32)
    coords = start + jnp.arange(count, dtype=jnp.int32)
    cosine, sine = angle_pair(freqs, coords, grid_len)
    return jnp.stack([cosine, sine]).astype(jnp.float32)

def slot_positions(slot_column, columns):
    flat_slots = slot_column.reshape(-1)
    slot_ids = jnp.arange(flat_slots.shape[0], dtype=jnp.int32)
    matches = flat_slots[None, :] == jnp.arange(columns, dtype=jnp.int32)[:, None]
    return lax.optimization_barrier(jnp.sum(jnp.where(matches, slot_ids[None, :], 0), axis=1)).astype(jnp.int32)

def gelu_parts(preact):
    coeff = math.sqrt(2.0 / math.pi)
    inner = coeff * (preact + 0.044715 * preact ** 3)
    tangent = jnp.tanh(inner)
    value = 0.5 * preact * (1.0 + tangent)
    slope = 0.5 * (1.0 + tangent) + 0.5 * preact * (1.0 - tangent * tangent) * coeff * (1.0 + 3.0 * 0.044715 * preact * preact)
    return (value, slope)

def reference(field, forcing, slot_column, w_spec, skip_gain, bias):
    grid_len = GRID
    kept = KXY
    columns = KXY * KXY
    factor = grid_len ** (-1.5)
    highest = lax.Precision.HIGHEST
    row_table, col_table = plane_tables(kept, grid_len)
    col_wide = col_table.astype(jnp.float32)
    depth = depth_table(KZ, 0, grid_len, grid_len)
    position = slot_positions(slot_column, columns)

    def analyse(volume):
        rows_done = jnp.dot(volume, row_table, preferred_element_type=jnp.float32).astype(jnp.bfloat16)
        mixed_x = jnp.einsum('tkx,zxj->tkjz', col_wide, rows_done.astype(jnp.float32))
        real_part = mixed_x[0, :, :kept] + mixed_x[1, :, kept:]
        imag_part = mixed_x[0, :, kept:] - mixed_x[1, :, :kept]
        pencils = jnp.stack([real_part, imag_part], 2).reshape(columns, 2, grid_len)
        terms = jnp.einsum('tfz,qrz->trqf', depth, pencils, precision=highest)
        return jnp.stack([terms[0, 0] + terms[1, 1], terms[0, 1] - terms[1, 0]], 1) * factor

    def synthesise(spectra):
        terms = jnp.einsum('tfz,qrf->tqrz', depth, spectra, precision=highest)
        planes = jnp.stack([terms[0, :, 0] - terms[1, :, 1], terms[1, :, 0] + terms[0, :, 1]], 1)
        planes = planes.astype(jnp.bfloat16).reshape(kept, kept, 2, grid_len)
        mixed_x = jnp.einsum('tkx,kjrz->trzxj', col_wide, planes.astype(jnp.float32))
        joined = jnp.concatenate([mixed_x[0, 0] - mixed_x[1, 1], mixed_x[1, 0] + mixed_x[0, 1]], -1).astype(jnp.bfloat16)
        return jnp.dot(joined, row_table.T, preferred_element_type=jnp.float32) * factor

    def merge_one(volume):
        return (volume.astype(jnp.float32) + forcing.astype(jnp.float32)).astype(jnp.bfloat16)
    coeffs = lax.map(lambda volume: analyse(merge_one(volume)), field)
    weights = jnp.take(w_spec.reshape(2, CH, CH, N_SLAB * CAP, KZ), position, axis=3).astype(jnp.float32)
    w_real, w_imag = (weights[0], weights[1])
    doubling = jnp.where(jnp.arange(KZ) == 0, 1.0, 2.0).astype(jnp.float32)
    u_real, u_imag = (coeffs[:, :, 0], coeffs[:, :, 1])
    out_real = jnp.einsum('cokf,ckf->okf', w_real, u_real, precision=highest) - jnp.einsum('cokf,ckf->okf', w_imag, u_imag, precision=highest)
    out_imag = jnp.einsum('cokf,ckf->okf', w_imag, u_real, precision=highest) + jnp.einsum('cokf,ckf->okf', w_real, u_imag, precision=highest)
    mixed = jnp.stack([out_real, out_imag], 2) * doubling

    def forward_one(items):
        volume, spectra, gain, shift = items
        merged = merge_one(volume)
        preact = synthesise(spectra) + gain * merged.astype(jnp.float32) + shift
        value, slope = gelu_parts(preact)
        output = value.astype(jnp.bfloat16)
        return (output, output.astype(jnp.float32) * slope)
    output, grad_pre = lax.map(forward_one, (field, mixed, skip_gain, bias))
    back = lax.map(lambda volume: analyse(volume.astype(jnp.bfloat16)), grad_pre) * doubling
    g_real, g_imag = (back[:, :, 0], back[:, :, 1])
    adj_real = jnp.einsum('cokf,okf->ckf', w_real, g_real, precision=highest) + jnp.einsum('cokf,okf->ckf', w_imag, g_imag, precision=highest)
    adj_imag = jnp.einsum('cokf,okf->ckf', w_real, g_imag, precision=highest) - jnp.einsum('cokf,okf->ckf', w_imag, g_real, precision=highest)
    adjoint = jnp.stack([adj_real, adj_imag], 2)

    def backward_one(items):
        spectra, grad_one, gain = items
        return (synthesise(spectra) + gain * grad_one).astype(jnp.bfloat16)
    gradient = lax.map(backward_one, (adjoint, grad_pre, skip_gain))
    return (output, gradient)
```

```python
import functools
import math

import jax
import jax.numpy as jnp
import ml_dtypes
import numpy as np
from jax import lax
from jax.experimental import pallas as pl
from jax.experimental.pallas import tpu as pltpu
from jax.sharding import PartitionSpec as P

KXY = 32
KZ = 16
MESH = pl.DeviceIdType.MESH
BF = jnp.bfloat16
F32 = jnp.float32
LANES = 128
GROUP = LANES // KXY


def bf16_table(values):
    return np.asarray(values, np.float32).astype(ml_dtypes.bfloat16)


def trig(freqs, coords, grid_len):
    angle = (np.outer(freqs, coords) % grid_len) * (2.0 * math.pi / grid_len)
    return np.cos(angle), np.sin(angle)


def plane_tables(grid_len):
    freqs = np.arange(KXY) - KXY // 2
    cos, sin = trig(freqs, np.arange(grid_len), grid_len)
    groups = KXY // GROUP
    scale = float(grid_len) ** -1.5
    x_down = np.zeros((GROUP, 2, groups, grid_len))
    x_up = np.zeros((grid_len, GROUP, 2, groups))
    y_down = np.zeros((GROUP, 2, grid_len, 2, GROUP, KXY))
    y_up = np.zeros((2, GROUP, KXY, GROUP, 2, grid_len))
    for k in range(GROUP):
        for g in range(groups):
            jx = g * GROUP + k
            x_down[k, 0, g], x_down[k, 1, g] = cos[jx], sin[jx]
            x_up[:, k, 0, g], x_up[:, k, 1, g] = scale * cos[jx], -scale * sin[jx]
        y_down[k, 0, :, 0, k], y_down[k, 1, :, 0, k] = cos.T, -sin.T
        y_down[k, 0, :, 1, k], y_down[k, 1, :, 1, k] = -sin.T, -cos.T
        y_up[0, k, :, k, 0], y_up[1, k, :, k, 0] = cos, -sin
        y_up[0, k, :, k, 1], y_up[1, k, :, k, 1] = sin, cos
    rows = 2 * KXY
    return (
        bf16_table(x_down.reshape(rows, grid_len)),
        bf16_table(x_up.reshape(grid_len, rows)),
        bf16_table(y_down.reshape(2 * GROUP * grid_len, 2 * LANES)),
        bf16_table(y_up.reshape(2 * LANES, 2 * GROUP * grid_len)),
    )


def depth_tables(channels, planes, slabs, grid_len):
    scale = float(grid_len) ** -1.5
    down, up = [], []
    eye = np.eye(channels)
    for s in range(slabs):
        cos, sin = trig(np.arange(KZ), s * planes + np.arange(planes), grid_len)
        parts = [[cos, sin], [-sin, cos]]
        full = np.zeros((2, channels, KZ, 2, channels, planes))
        for q in range(2):
            for r in range(2):
                full[q, :, :, r] = np.einsum("cd,mz->cmdz", eye, parts[q][r])
        full = full.reshape(2 * channels * KZ, 2 * channels * planes)
        for store, table in ((down, full * scale), (up, full.T)):
            high = bf16_table(table)
            low = bf16_table(table - high.astype(np.float64))
            store.append(np.concatenate([high, low], axis=1))
    return np.stack(down), np.stack(up)


def dot(a, b):
    return jnp.dot(a, b, preferred_element_type=F32)


def dot_nt(a, b):
    return lax.dot_general(a, b, (((1,), (1,)), ((), ())), preferred_element_type=F32)


def twice(block):
    return jnp.concatenate([block, block], axis=0)


def keep_x_rows(xs_ref, plane, planes_all, value):
    groups = KXY // GROUP
    width = value.shape[1]
    tiles = width // LANES
    for kp in range(2 * GROUP):
        for h in range(tiles):
            xs_ref[kp * tiles + h, pl.ds(plane, groups, stride=planes_all), :] = value[
                kp * groups : (kp + 1) * groups, h * LANES : (h + 1) * LANES
            ]


def plane_rows(ws_ref, plane, planes_all, width):
    groups = KXY // GROUP
    tiles = width // LANES
    columns = []
    for h in range(tiles):
        parts = [ws_ref[kp * tiles + h, pl.ds(plane, groups, stride=planes_all), :] for kp in range(2 * GROUP)]
        columns.append(jnp.concatenate(parts, axis=0))
    return jnp.concatenate(columns, axis=1)


def analysis_tail(xs_ref, y_down_ref, z_down_ref, slot_ref, zt_ref, packed_ref):
    planes_all = xs_ref.shape[1] * GROUP // KXY
    lhs = jnp.concatenate([xs_ref[j].astype(BF) for j in range(xs_ref.shape[0])], axis=1)
    spectra = dot(lhs, y_down_ref[...])
    for g in range(KXY // GROUP):
        for q in range(2):
            zt_ref[q * planes_all : (q + 1) * planes_all, g * LANES : (g + 1) * LANES] = spectra[
                g * planes_all : (g + 1) * planes_all, q * LANES : (q + 1) * LANES
            ].astype(BF)
    coeffs = dot(z_down_ref[0], twice(zt_ref[...])).astype(BF)
    columns = coeffs.shape[1]
    slots = slot_ref.shape[1]
    capacity = packed_ref.shape[2]
    chunk = 2 * capacity
    column = lax.broadcasted_iota(jnp.int32, (columns, chunk), 0)
    for n in range(slots // chunk):
        pick = (column == slot_ref[0:1, n * chunk : (n + 1) * chunk]).astype(F32).astype(BF)
        part = dot(coeffs, pick).astype(BF)
        packed_ref[2 * n] = part[:, :capacity]
        packed_ref[2 * n + 1] = part[:, capacity:]


def synthesis_head(recv_ref, slot_ref, z_up_ref, y_up_ref, zt_ref, ws_ref):
    planes_all = ws_ref.shape[1] * GROUP // KXY
    slabs = recv_ref.shape[0]
    by_slot = jnp.concatenate([recv_ref[s] for s in range(slabs)], axis=1)
    slots = by_slot.shape[1]
    chunk = 2 * LANES
    column = lax.broadcasted_iota(jnp.int32, (chunk, slots), 0)
    for n in range(KXY * KXY // chunk):
        pick = (column + n * chunk == slot_ref[0:1, :]).astype(F32).astype(BF)
        spectra = dot_nt(by_slot, pick).astype(BF)
        zt_ref[:, n * chunk : (n + 1) * chunk] = dot(z_up_ref[0], twice(spectra)).astype(BF)
    rows = []
    for g in range(KXY // GROUP):
        at = slice(g * LANES, (g + 1) * LANES)
        rows.append(jnp.concatenate([zt_ref[:planes_all, at], zt_ref[planes_all:, at]], axis=1))
    lhs = jnp.concatenate(rows, axis=0)
    chunk = 2 * LANES
    for j in range(ws_ref.shape[0] // 2):
        wide = dot(lhs, y_up_ref[:, j * chunk : (j + 1) * chunk])
        ws_ref[2 * j] = wide[:, :LANES]
        ws_ref[2 * j + 1] = wide[:, LANES:]


def gelu_pair(preact):
    coeff = math.sqrt(2.0 / math.pi)
    square = preact * preact
    tangent = jnp.tanh(preact * (coeff + (coeff * 0.044715) * square))
    half = 0.5 * preact
    above = 1.0 + tangent
    value = half * above
    slope = above * (0.5 + half * (1.0 - tangent) * (coeff + (3.0 * 0.044715 * coeff) * square))
    return value, slope


def analyse_kernel(per_step, slab_ref, field_ref, plane_ref, slot_ref, x_down_ref, y_down_ref, z_down_ref, packed_ref, xs_ref, zt_ref):
    step = pl.program_id(0)
    channels = field_ref.shape[0]
    planes_all = xs_ref.shape[1] * GROUP // KXY
    planes = planes_all // channels
    for zz in range(per_step):
        shift = plane_ref[zz].astype(F32)
        for c in range(channels):
            merged = (field_ref[c, zz].astype(F32) + shift).astype(BF)
            keep_x_rows(xs_ref, c * planes + step * per_step + zz, planes_all, dot(x_down_ref[...], merged))

    @pl.when(step == pl.num_programs(0) - 1)
    def _():
        analysis_tail(xs_ref, y_down_ref, z_down_ref, slot_ref, zt_ref, packed_ref)


def middle_kernel(per_step, rows, slab_ref, gain_ref, bias_ref, field_ref, plane_ref, recv_ref, slot_ref, x_down_ref, x_up_ref, y_down_ref, y_up_ref, z_down_ref, z_up_ref, out_ref, grad_ref, packed_ref, xs_ref, ws_ref, zt_ref):
    step = pl.program_id(0)
    channels, _, grid_len, _ = field_ref.shape
    planes_all = xs_ref.shape[1] * GROUP // KXY
    planes = planes_all // channels

    @pl.when(step == 0)
    def _():
        synthesis_head(recv_ref, slot_ref, z_up_ref, y_up_ref, zt_ref, ws_ref)

    for zz in range(per_step):
        for c in range(channels):
            plane = c * planes + step * per_step + zz
            wp = plane_rows(ws_ref, plane, planes_all, grid_len).astype(BF)
            gain, bias = gain_ref[c], bias_ref[c]
            for at in range(0, grid_len, rows):
                span = slice(at, at + rows)
                merged = (field_ref[c, zz, span, :].astype(F32) + plane_ref[zz, span, :].astype(F32)).astype(BF)
                preact = dot(x_up_ref[span, :], wp) + (gain * merged.astype(F32) + bias)
                value, slope = gelu_pair(preact)
                value = value.astype(BF)
                out_ref[c, zz, span, :] = value
                grad_ref[c, zz, span, :] = (value.astype(F32) * slope).astype(BF)
            keep_x_rows(xs_ref, plane, planes_all, dot(x_down_ref[...], grad_ref[c, zz]))

    @pl.when(step == pl.num_programs(0) - 1)
    def _():
        analysis_tail(xs_ref, y_down_ref, z_down_ref, slot_ref, zt_ref, packed_ref)


def final_kernel(per_step, rows, slab_ref, gain_ref, grad_ref, recv_ref, slot_ref, x_up_ref, y_up_ref, z_up_ref, out_ref, ws_ref, zt_ref):
    step = pl.program_id(0)
    channels, _, grid_len, _ = grad_ref.shape
    planes_all = ws_ref.shape[1] * GROUP // KXY
    planes = planes_all // channels

    @pl.when(step == 0)
    def _():
        synthesis_head(recv_ref, slot_ref, z_up_ref, y_up_ref, zt_ref, ws_ref)

    for zz in range(per_step):
        for c in range(channels):
            wp = plane_rows(ws_ref, c * planes + step * per_step + zz, planes_all, grid_len).astype(BF)
            gain = gain_ref[c]
            for at in range(0, grid_len, rows):
                span = slice(at, at + rows)
                grad = dot(x_up_ref[span, :], wp) + gain * grad_ref[c, zz, span, :].astype(F32)
                out_ref[c, zz, span, :] = grad.astype(BF)


def entry_barrier(targets):
    barrier = pltpu.get_barrier_semaphore()
    for target in targets:
        pl.semaphore_signal(barrier, inc=1, device_id=target, device_id_type=MESH)
    pl.semaphore_wait(barrier, len(targets))


def spread(block, start, width):
    slots = block.shape[1]
    lane = lax.broadcasted_iota(jnp.int32, (slots, width), 1) + start
    row = lax.broadcasted_iota(jnp.int32, (slots, width), 0)
    expand = (lane // KZ == row).astype(F32).astype(BF)
    high = block.astype(BF)
    low = (block - high.astype(F32)).astype(BF)
    wide = dot(high, expand) + dot(low, expand)
    pairs = wide.shape[0] // KZ
    wide = wide.reshape(pairs, KZ, width)
    m_row = lax.broadcasted_iota(jnp.int32, wide.shape, 1)
    m_lane = lax.broadcasted_iota(jnp.int32, wide.shape, 2) % KZ
    return jnp.sum(jnp.where(m_row == m_lane, wide, 0.0), axis=1)


def unspread(pairs, start, slots):
    count, width = pairs.shape
    shape = (count, KZ, width)
    m_row = lax.broadcasted_iota(jnp.int32, shape, 1)
    m_lane = lax.broadcasted_iota(jnp.int32, shape, 2) % KZ
    wide = jnp.where(m_row == m_lane, jnp.broadcast_to(pairs[:, None, :], shape), 0.0)
    wide = wide.reshape(count * KZ, width).astype(BF)
    lane = lax.broadcasted_iota(jnp.int32, (slots, width), 1) + start
    row = lax.broadcasted_iota(jnp.int32, (slots, width), 0)
    collect = (lane // KZ == row).astype(F32).astype(BF)
    return dot_nt(wide, collect)


def mix_kernel(slabs, groups, forward, packed_ref, w_ref, recv_ref, rx, sums, tx2, rx2, mine, s_send, s_recv, c_send, c_recv, g_send, g_recv):
    slab, chan = lax.axis_index("slab"), lax.axis_index("chan")
    slab_peer = [(lax.rem(slab + d, slabs), chan) for d in range(1, slabs)]
    chan_peer = [(slab, lax.rem(chan + d, groups)) for d in range(1, groups)]
    entry_barrier(slab_peer + chan_peer)
    first = []
    for d in range(1, slabs):
        copy = pltpu.make_async_remote_copy(
            src_ref=packed_ref.at[slab_peer[d - 1][0]], dst_ref=rx.at[d - 1], send_sem=s_send.at[d - 1], recv_sem=s_recv.at[d - 1],
            device_id=slab_peer[d - 1], device_id_type=MESH,
        )
        copy.start()
        first.append(copy)
    total = packed_ref[slab].astype(F32)
    for d in range(1, slabs):
        first[d - 1].wait_recv()
        total = total + rx[d - 1].astype(F32)
    slots = total.shape[1]
    wide = slots * KZ
    chunk = 512
    own = rx2.shape[1] // 2
    outputs = own * groups
    if forward:
        for start in range(0, wide, chunk):
            at = slice(start, start + chunk)
            u = spread(total, start, chunk)
            real = jnp.zeros((outputs, chunk), F32)
            imag = jnp.zeros((outputs, chunk), F32)
            for c in range(own):
                w0, w1 = w_ref[0, c, :, at].astype(F32), w_ref[1, c, :, at].astype(F32)
                ur, ui = u[c : c + 1], u[own + c : own + c + 1]
                real = real + (w0 * ur - w1 * ui)
                imag = imag + (w1 * ur + w0 * ui)
            for e in range(groups):
                rows = slice(e * own, (e + 1) * own)
                tx2[e, :, at] = jnp.concatenate([real[rows], imag[rows]], axis=0).astype(BF)
    else:
        for start in range(0, wide, chunk):
            at = slice(start, start + chunk)
            lane = lax.broadcasted_iota(jnp.int32, (2 * own, chunk), 1)
            double = jnp.where(lane % KZ == 0, 1.0, 2.0)
            tx2[0, :, at] = (spread(total, start, chunk) * double).astype(BF)
    second = []
    for d in range(1, groups):
        peer = chan_peer[d - 1]
        copy = pltpu.make_async_remote_copy(
            src_ref=tx2.at[peer[1]] if forward else tx2.at[0], dst_ref=rx2.at[chan], send_sem=c_send.at[d - 1], recv_sem=c_recv.at[d - 1],
            device_id=peer, device_id_type=MESH,
        )
        copy.start()
        second.append(copy)
    rx2[chan] = tx2[chan] if forward else tx2[0]
    for copy in second:
        copy.wait_recv()
    result = jnp.zeros((2 * own * KZ, slots), F32)
    for start in range(0, wide, chunk):
        at = slice(start, start + chunk)
        if forward:
            pairs = rx2[0, :, at].astype(F32)
            for e in range(1, groups):
                pairs = pairs + rx2[e, :, at].astype(F32)
            lane = lax.broadcasted_iota(jnp.int32, (2 * own, chunk), 1)
            pairs = pairs * jnp.where(lane % KZ == 0, 1.0, 2.0)
        else:
            blocks = [rx2[e, :, at].astype(F32) for e in range(groups)]
            real = jnp.concatenate([b[:own] for b in blocks], axis=0)
            imag = jnp.concatenate([b[own:] for b in blocks], axis=0)
            reals, imags = [], []
            for c in range(own):
                w0, w1 = w_ref[0, c, :, at].astype(F32), w_ref[1, c, :, at].astype(F32)
                reals.append(jnp.sum(w0 * real + w1 * imag, axis=0, keepdims=True))
                imags.append(jnp.sum(w0 * imag - w1 * real, axis=0, keepdims=True))
            pairs = jnp.concatenate(reals + imags, axis=0)
        result = result + unspread(pairs, start, slots)
    mine[...] = result.astype(BF)
    third = []
    for d in range(1, slabs):
        copy = pltpu.make_async_remote_copy(
            src_ref=mine, dst_ref=recv_ref.at[slab], send_sem=g_send.at[d - 1], recv_sem=g_recv.at[d - 1],
            device_id=slab_peer[d - 1], device_id_type=MESH,
        )
        copy.start()
        third.append(copy)
    recv_ref[slab] = mine[...]
    for copy in third:
        copy.wait_recv()
    for copy in first + second + third:
        copy.wait_send()


def gather_kernel(chips, block_ref, plane_ref, own_sem, x_send, x_recv, p_send, p_recv):
    slab, chan = lax.axis_index("slab"), lax.axis_index("chan")
    height = block_ref.shape[1]
    chip, core = chan // 2, lax.rem(chan, 2)
    partner = (slab, chan + 1 - 2 * core)
    peers = [(slab, 2 * lax.rem(chip + t, chips) + core) for t in range(1, chips)]
    entry_barrier(peers + [partner])

    def rows(index):
        return plane_ref.at[:, pl.ds(pl.multiple_of(index * height, height), height), :]

    own = pltpu.make_async_copy(block_ref, rows(chan), own_sem)
    own.start()
    across = []
    for t in range(1, chips):
        across.append(pltpu.make_async_remote_copy(
            src_ref=block_ref, dst_ref=rows(chan), send_sem=x_send.at[t - 1], recv_sem=x_recv.at[t - 1],
            device_id=peers[t - 1], device_id_type=MESH,
        ))
    order = [1, 3, 2]
    for t in order:
        across[t - 1].start()
    local = [pltpu.make_async_remote_copy(
        src_ref=block_ref, dst_ref=rows(chan), send_sem=p_send.at[0], recv_sem=p_recv.at[0], device_id=partner, device_id_type=MESH,
    )]
    local[0].start()
    for t in order:
        across[t - 1].wait_recv()
        source = 2 * lax.rem(chip + chips - t, chips) + core
        copy = pltpu.make_async_remote_copy(
            src_ref=rows(source), dst_ref=rows(source), send_sem=p_send.at[t], recv_sem=p_recv.at[t], device_id=partner, device_id_type=MESH,
        )
        copy.start()
        local.append(copy)
    own.wait()
    for copy in local:
        copy.wait_recv()
    for copy in across + local:
        copy.wait_send()


def whole(shape):
    zeros = (0,) * len(shape)
    return pl.BlockSpec(shape, lambda *_: zeros, pipeline_mode=pl.Buffered(1))


def per_device(slabs, groups, field, forcing, slot_column, w_spec, skip_gain, bias):
    channels, planes, grid_len, _ = field.shape
    capacity = slot_column.shape[1]
    planes_all = channels * planes
    columns = KXY * KXY
    x_down, x_up, y_down, y_up = [jnp.asarray(t) for t in plane_tables(grid_len)]
    z_down, z_up = [jnp.asarray(t) for t in depth_tables(channels, planes, slabs, grid_len)]
    slots = slot_column.reshape(1, slabs * capacity)
    where = lax.axis_index("slab").astype(jnp.int32).reshape(1)
    chips = groups // 2

    plane = pl.pallas_call(
        functools.partial(gather_kernel, chips),
        out_shape=jax.ShapeDtypeStruct((planes, grid_len, grid_len), BF),
        in_specs=[pl.BlockSpec(memory_space=pl.ANY)],
        out_specs=pl.BlockSpec(memory_space=pl.ANY),
        scratch_shapes=[pltpu.SemaphoreType.DMA] + [pltpu.SemaphoreType.DMA((chips - 1,))] * 2 + [pltpu.SemaphoreType.DMA((chips,))] * 2,
        compiler_params=pltpu.CompilerParams(collective_id=0, has_side_effects=True),
        name="gather_forcing",
    )(forcing)

    per_step = 2
    steps = planes // per_step
    field_spec = pl.BlockSpec((channels, per_step, grid_len, grid_len), lambda i, s: (0, i, 0, 0))
    plane_spec = pl.BlockSpec((per_step, grid_len, grid_len), lambda i, s: (i, 0, 0))
    z_spec = pl.BlockSpec((1,) + z_down.shape[1:], lambda i, s: (s[0], 0, 0), pipeline_mode=pl.Buffered(1))
    packed_shape = (slabs, 2 * channels * KZ, capacity)
    volume = jax.ShapeDtypeStruct(field.shape, BF)
    packed_out = jax.ShapeDtypeStruct(packed_shape, BF)
    packed_spec = pl.BlockSpec(packed_shape, lambda i, s: (0, 0, 0))
    wide_scratch = pltpu.VMEM((2 * GROUP * grid_len // LANES, planes_all * KXY // GROUP, LANES), F32)
    zt_scratch = pltpu.VMEM((2 * planes_all, columns), BF)
    big = pltpu.CompilerParams(dimension_semantics=("arbitrary",), vmem_limit_bytes=56 << 20)
    smem = pl.BlockSpec(memory_space=pltpu.SMEM)

    packed = pl.pallas_call(
        functools.partial(analyse_kernel, per_step),
        out_shape=packed_out,
        grid_spec=pltpu.PrefetchScalarGridSpec(
            num_scalar_prefetch=1, grid=(steps,),
            in_specs=[field_spec, plane_spec, whole(slots.shape), whole(x_down.shape), whole(y_down.shape), z_spec],
            out_specs=packed_spec,
            scratch_shapes=[wide_scratch, zt_scratch],
        ),
        compiler_params=big,
        name="analyse",
    )(where, field, plane, slots, x_down, y_down, z_down)

    vmem = pl.BlockSpec(memory_space=pltpu.VMEM)

    def exchange(values, forward):
        block = packed_shape[1:]
        pair = (groups, 2 * channels, capacity * KZ)
        return pl.pallas_call(
            functools.partial(mix_kernel, slabs, groups, forward),
            out_shape=packed_out,
            in_specs=[vmem, vmem],
            out_specs=vmem,
            scratch_shapes=[
                pltpu.VMEM((slabs - 1,) + block, BF),
                pltpu.VMEM(block, F32),
                pltpu.VMEM(pair, BF),
                pltpu.VMEM(pair, BF),
                pltpu.VMEM(block, BF),
            ]
            + [pltpu.SemaphoreType.DMA((slabs - 1,))] * 2
            + [pltpu.SemaphoreType.DMA((groups - 1,))] * 2
            + [pltpu.SemaphoreType.DMA((slabs - 1,))] * 2,
            compiler_params=pltpu.CompilerParams(collective_id=1 if forward else 2, has_side_effects=True, vmem_limit_bytes=32 << 20),
            name="mix_forward" if forward else "mix_adjoint",
        )(values, w_spec)

    spectra = exchange(packed, True)
    output, grad_pre, packed_back = pl.pallas_call(
        functools.partial(middle_kernel, per_step, 64),
        out_shape=(volume, volume, packed_out),
        grid_spec=pltpu.PrefetchScalarGridSpec(
            num_scalar_prefetch=1, grid=(steps,),
            in_specs=[smem, smem, field_spec, plane_spec, whole(packed_shape), whole(slots.shape), whole(x_down.shape), whole(x_up.shape), whole(y_down.shape), whole(y_up.shape), z_spec, z_spec],
            out_specs=(field_spec, field_spec, packed_spec),
            scratch_shapes=[wide_scratch, wide_scratch, zt_scratch],
        ),
        compiler_params=big,
        name="synth_gelu_analyse",
    )(where, skip_gain, bias, field, plane, spectra, slots, x_down, x_up, y_down, y_up, z_down, z_up)

    adjoint = exchange(packed_back, False)
    gradient = pl.pallas_call(
        functools.partial(final_kernel, per_step, 64),
        out_shape=volume,
        grid_spec=pltpu.PrefetchScalarGridSpec(
            num_scalar_prefetch=1, grid=(steps,),
            in_specs=[smem, field_spec, whole(packed_shape), whole(slots.shape), whole(x_up.shape), whole(y_up.shape), z_spec],
            out_specs=field_spec,
            scratch_shapes=[wide_scratch, zt_scratch],
        ),
        compiler_params=big,
        name="synth_gradient",
    )(where, skip_gain, grad_pre, adjoint, slots, x_up, y_up, z_up)
    return (output, gradient)


def solution(mesh):
    placed = (
        P("chan", "slab", None, None),
        P("slab", "chan", None),
        P(),
        P(None, "chan", None, "slab"),
        P("chan"),
        P("chan"),
    )
    slabs, groups = mesh.shape["slab"], mesh.shape["chan"]
    return jax.shard_map(
        functools.partial(per_device, slabs, groups),
        mesh=mesh,
        in_specs=placed,
        out_specs=(P("chan", "slab", None, None), P("chan", "slab", None, None)),
        check_vma=False,
    )
```

```python
import functools
import math

import jax
import jax.numpy as jnp
import ml_dtypes
import numpy as np
from jax import lax
from jax.experimental import pallas as pl
from jax.experimental.pallas import tpu as pltpu
from jax.sharding import PartitionSpec as P

KXY = 32
KZ = 16
MESH = pl.DeviceIdType.MESH
BF = jnp.bfloat16
F32 = jnp.float32
LANES = 128
GROUP = LANES // KXY


def bf16_table(values):
    return np.asarray(values, np.float32).astype(ml_dtypes.bfloat16)


def trig(freqs, coords, grid_len):
    angle = (np.outer(freqs, coords) % grid_len) * (2.0 * math.pi / grid_len)
    return np.cos(angle), np.sin(angle)


def plane_tables(grid_len):
    freqs = np.arange(KXY) - KXY // 2
    cos, sin = trig(freqs, np.arange(grid_len), grid_len)
    groups = KXY // GROUP
    scale = float(grid_len) ** -1.5
    x_down = np.zeros((GROUP, 2, groups, grid_len))
    x_up = np.zeros((grid_len, GROUP, 2, groups))
    y_down = np.zeros((GROUP, 2, grid_len, 2, GROUP, KXY))
    y_up = np.zeros((2, GROUP, KXY, GROUP, 2, grid_len))
    for k in range(GROUP):
        for g in range(groups):
            jx = g * GROUP + k
            x_down[k, 0, g], x_down[k, 1, g] = cos[jx], sin[jx]
            x_up[:, k, 0, g], x_up[:, k, 1, g] = scale * cos[jx], -scale * sin[jx]
        y_down[k, 0, :, 0, k], y_down[k, 1, :, 0, k] = cos.T, -sin.T
        y_down[k, 0, :, 1, k], y_down[k, 1, :, 1, k] = -sin.T, -cos.T
        y_up[0, k, :, k, 0], y_up[1, k, :, k, 0] = cos, -sin
        y_up[0, k, :, k, 1], y_up[1, k, :, k, 1] = sin, cos
    rows = 2 * KXY
    return (
        bf16_table(x_down.reshape(rows, grid_len)),
        bf16_table(x_up.reshape(grid_len, rows)),
        bf16_table(y_down.reshape(2 * GROUP * grid_len, 2 * LANES)),
        bf16_table(y_up.reshape(2 * LANES, 2 * GROUP * grid_len)),
    )


def depth_tables(channels, planes, slabs, grid_len):
    scale = float(grid_len) ** -1.5
    down, up = [], []
    eye = np.eye(channels)
    for s in range(slabs):
        cos, sin = trig(np.arange(KZ), s * planes + np.arange(planes), grid_len)
        parts = [[cos, sin], [-sin, cos]]
        full = np.zeros((2, channels, KZ, 2, channels, planes))
        for q in range(2):
            for r in range(2):
                full[q, :, :, r] = np.einsum("cd,mz->cmdz", eye, parts[q][r])
        full = full.reshape(2 * channels * KZ, 2 * channels * planes)
        for store, table in ((down, full * scale), (up, full.T)):
            high = bf16_table(table)
            low = bf16_table(table - high.astype(np.float64))
            store.append(np.concatenate([high, low], axis=1))
    return np.stack(down), np.stack(up)


def dot(a, b):
    return jnp.dot(a, b, preferred_element_type=F32)


def dot_nt(a, b):
    return lax.dot_general(a, b, (((1,), (1,)), ((), ())), preferred_element_type=F32)


def twice(block):
    return jnp.concatenate([block, block], axis=0)


def keep_x_rows(xs_ref, plane, planes_all, value):
    groups = KXY // GROUP
    width = value.shape[1]
    tiles = width // LANES
    for kp in range(2 * GROUP):
        for h in range(tiles):
            xs_ref[kp * tiles + h, pl.ds(plane, groups, stride=planes_all), :] = value[
                kp * groups : (kp + 1) * groups, h * LANES : (h + 1) * LANES
            ]


def plane_rows(ws_ref, plane, planes_all, width):
    groups = KXY // GROUP
    tiles = width // LANES
    columns = []
    for h in range(tiles):
        parts = [ws_ref[kp * tiles + h, pl.ds(plane, groups, stride=planes_all), :] for kp in range(2 * GROUP)]
        columns.append(jnp.concatenate(parts, axis=0))
    return jnp.concatenate(columns, axis=1)


def analysis_tail(xs_ref, y_down_ref, z_down_ref, slot_ref, zt_ref, packed_ref):
    planes_all = xs_ref.shape[1] * GROUP // KXY
    lhs = jnp.concatenate([xs_ref[j].astype(BF) for j in range(xs_ref.shape[0])], axis=1)
    spectra = dot(lhs, y_down_ref[...])
    for g in range(KXY // GROUP):
        for q in range(2):
            zt_ref[q * planes_all : (q + 1) * planes_all, g * LANES : (g + 1) * LANES] = spectra[
                g * planes_all : (g + 1) * planes_all, q * LANES : (q + 1) * LANES
            ].astype(BF)
    coeffs = dot(z_down_ref[0], twice(zt_ref[...])).astype(BF)
    columns = coeffs.shape[1]
    slots = slot_ref.shape[1]
    capacity = packed_ref.shape[2]
    chunk = 2 * capacity
    column = lax.broadcasted_iota(jnp.int32, (columns, chunk), 0)
    for n in range(slots // chunk):
        pick = (column == slot_ref[0:1, n * chunk : (n + 1) * chunk]).astype(F32).astype(BF)
        part = dot(coeffs, pick).astype(BF)
        packed_ref[2 * n] = part[:, :capacity]
        packed_ref[2 * n + 1] = part[:, capacity:]


def synthesis_head(recv_ref, slot_ref, z_up_ref, y_up_ref, zt_ref, ws_ref):
    planes_all = ws_ref.shape[1] * GROUP // KXY
    slabs = recv_ref.shape[0]
    by_slot = jnp.concatenate([recv_ref[s] for s in range(slabs)], axis=1)
    slots = by_slot.shape[1]
    chunk = 2 * LANES
    column = lax.broadcasted_iota(jnp.int32, (chunk, slots), 0)
    for n in range(KXY * KXY // chunk):
        pick = (column + n * chunk == slot_ref[0:1, :]).astype(F32).astype(BF)
        spectra = dot_nt(by_slot, pick).astype(BF)
        zt_ref[:, n * chunk : (n + 1) * chunk] = dot(z_up_ref[0], twice(spectra)).astype(BF)
    rows = []
    for g in range(KXY // GROUP):
        at = slice(g * LANES, (g + 1) * LANES)
        rows.append(jnp.concatenate([zt_ref[:planes_all, at], zt_ref[planes_all:, at]], axis=1))
    lhs = jnp.concatenate(rows, axis=0)
    chunk = 2 * LANES
    for j in range(ws_ref.shape[0] // 2):
        wide = dot(lhs, y_up_ref[:, j * chunk : (j + 1) * chunk])
        ws_ref[2 * j] = wide[:, :LANES]
        ws_ref[2 * j + 1] = wide[:, LANES:]


def gelu_pair(half):
    coeff = math.sqrt(2.0 / math.pi)
    square = half * half
    tangent = jnp.tanh(half * (2.0 * coeff + (8.0 * 0.044715 * coeff) * square))
    above = 1.0 + tangent
    value = half * above
    slope = above * (0.5 + (half * (1.0 - tangent)) * (coeff + (12.0 * 0.044715 * coeff) * square))
    return value, slope


class Planes:
    def __init__(self, step, per_step, channels, planes):
        self.step, self.per_step, self.count = step, per_step, per_step * channels
        self.planes, self.planes_all = planes, planes * channels

    def place(self, t):
        c = t // self.per_step
        zz = t - c * self.per_step
        return c, zz, c * self.planes + self.step * self.per_step + zz


def analyse_kernel(per_step, slab_ref, field_ref, plane_ref, slot_ref, x_down_ref, y_down_ref, z_down_ref, packed_ref, merged_ref, xs_ref, zt_ref):
    step = pl.program_id(0)
    channels = field_ref.shape[0]
    at = Planes(step, per_step, channels, xs_ref.shape[1] * GROUP // KXY // channels)

    def body(zz, carry):
        for c in range(channels):
            merged = field_ref[c, zz] + plane_ref[zz]
            merged_ref[c, step * per_step + zz] = merged
            keep_x_rows(xs_ref, c * at.planes + step * per_step + zz, at.planes_all, dot(x_down_ref[...], merged))
        return carry

    lax.fori_loop(0, per_step, body, 0)

    @pl.when(step == pl.num_programs(0) - 1)
    def _():
        analysis_tail(xs_ref, y_down_ref, z_down_ref, slot_ref, zt_ref, packed_ref)


def middle_kernel(per_step, rows, slab_ref, gain_ref, bias_ref, merged_ref, recv_ref, slot_ref, x_down_ref, x_up_ref, y_down_ref, y_up_ref, z_down_ref, z_up_ref, out_ref, grad_ref, packed_ref, xs_ref, ws_ref, zt_ref, sa_ref, sb_ref):
    step = pl.program_id(0)
    channels, _, grid_len, _ = merged_ref.shape
    at = Planes(step, per_step, channels, xs_ref.shape[1] * GROUP // KXY // channels)

    @pl.when(step == 0)
    def _():
        synthesis_head(recv_ref, slot_ref, z_up_ref, y_up_ref, zt_ref, ws_ref)

    def synth(t, s_ref):
        wp = plane_rows(ws_ref, at.place(t)[2], at.planes_all, grid_len).astype(BF)
        s_ref[...] = dot(x_up_ref[...], wp)

    def point(t, s_ref):
        c, zz, _ = at.place(t)
        zz_all = step * per_step + zz
        gain, bias = 0.5 * gain_ref[c], 0.5 * bias_ref[c]
        for start in range(0, grid_len, rows):
            span = slice(start, start + rows)
            merged = merged_ref[c, zz_all, span, :]
            value, slope = gelu_pair(0.5 * s_ref[span, :] + (gain * merged.astype(F32) + bias))
            out_ref[c, zz, span, :] = value.astype(BF)
            grad_ref[c, zz_all, span, :] = (value * slope).astype(BF)

    def down(t):
        c, zz, plane = at.place(t)
        keep_x_rows(xs_ref, plane, at.planes_all, dot(x_down_ref[...], grad_ref[c, step * per_step + zz]))

    synth(0, sa_ref)

    def body(j, carry):
        t = 2 * j
        synth(t + 1, sb_ref)
        down(jnp.maximum(t - 1, 0))
        point(t, sa_ref)
        synth(jnp.minimum(t + 2, at.count - 1), sa_ref)
        down(t)
        point(t + 1, sb_ref)
        return carry

    lax.fori_loop(0, at.count // 2, body, 0)
    down(at.count - 1)

    @pl.when(step == pl.num_programs(0) - 1)
    def _():
        analysis_tail(xs_ref, y_down_ref, z_down_ref, slot_ref, zt_ref, packed_ref)


def final_kernel(per_step, rows, slab_ref, gain_ref, grad_ref, recv_ref, slot_ref, x_up_ref, y_up_ref, z_up_ref, out_ref, ws_ref, zt_ref):
    step = pl.program_id(0)
    channels, _, grid_len, _ = grad_ref.shape
    at = Planes(step, per_step, channels, ws_ref.shape[1] * GROUP // KXY // channels)

    @pl.when(step == 0)
    def _():
        synthesis_head(recv_ref, slot_ref, z_up_ref, y_up_ref, zt_ref, ws_ref)

    def body(zz, carry):
        for c in range(channels):
            wp = plane_rows(ws_ref, c * at.planes + step * per_step + zz, at.planes_all, grid_len).astype(BF)
            out_ref[c, zz] = (dot(x_up_ref[...], wp) + gain_ref[c] * grad_ref[c, step * per_step + zz].astype(F32)).astype(BF)
        return carry

    lax.fori_loop(0, per_step, body, 0)


def entry_barrier(targets):
    barrier = pltpu.get_barrier_semaphore()
    for target in targets:
        pl.semaphore_signal(barrier, inc=1, device_id=target, device_id_type=MESH)
    pl.semaphore_wait(barrier, len(targets))


def spread(block, start, width):
    slots = block.shape[1]
    lane = lax.broadcasted_iota(jnp.int32, (slots, width), 1) + start
    row = lax.broadcasted_iota(jnp.int32, (slots, width), 0)
    expand = (lane // KZ == row).astype(F32).astype(BF)
    high = block.astype(BF)
    low = (block - high.astype(F32)).astype(BF)
    wide = dot(high, expand) + dot(low, expand)
    pairs = wide.shape[0] // KZ
    wide = wide.reshape(pairs, KZ, width)
    m_row = lax.broadcasted_iota(jnp.int32, wide.shape, 1)
    m_lane = lax.broadcasted_iota(jnp.int32, wide.shape, 2) % KZ
    return jnp.sum(jnp.where(m_row == m_lane, wide, 0.0), axis=1)


def unspread(pairs, start, slots):
    count, width = pairs.shape
    shape = (count, KZ, width)
    m_row = lax.broadcasted_iota(jnp.int32, shape, 1)
    m_lane = lax.broadcasted_iota(jnp.int32, shape, 2) % KZ
    wide = jnp.where(m_row == m_lane, jnp.broadcast_to(pairs[:, None, :], shape), 0.0)
    wide = wide.reshape(count * KZ, width).astype(BF)
    lane = lax.broadcasted_iota(jnp.int32, (slots, width), 1) + start
    row = lax.broadcasted_iota(jnp.int32, (slots, width), 0)
    collect = (lane // KZ == row).astype(F32).astype(BF)
    return dot_nt(wide, collect)


def mix_kernel(slabs, groups, forward, packed_ref, w_ref, recv_ref, rx, sums, tx2, rx2, mine, s_send, s_recv, c_send, c_recv, g_send, g_recv):
    slab, chan = lax.axis_index("slab"), lax.axis_index("chan")
    slab_peer = [(lax.rem(slab + d, slabs), chan) for d in range(1, slabs)]
    chan_peer = [(slab, lax.rem(chan + d, groups)) for d in range(1, groups)]
    entry_barrier(slab_peer + chan_peer)
    first = []
    for d in range(1, slabs):
        copy = pltpu.make_async_remote_copy(
            src_ref=packed_ref.at[slab_peer[d - 1][0]], dst_ref=rx.at[d - 1], send_sem=s_send.at[d - 1], recv_sem=s_recv.at[d - 1],
            device_id=slab_peer[d - 1], device_id_type=MESH,
        )
        copy.start()
        first.append(copy)
    total = packed_ref[slab].astype(F32)
    for d in range(1, slabs):
        first[d - 1].wait_recv()
        total = total + rx[d - 1].astype(F32)
    slots = total.shape[1]
    wide = slots * KZ
    chunk = 512
    own = rx2.shape[1] // 2
    outputs = own * groups
    if forward:
        for start in range(0, wide, chunk):
            at = slice(start, start + chunk)
            u = spread(total, start, chunk)
            real = jnp.zeros((outputs, chunk), F32)
            imag = jnp.zeros((outputs, chunk), F32)
            for c in range(own):
                w0, w1 = w_ref[0, c, :, at].astype(F32), w_ref[1, c, :, at].astype(F32)
                ur, ui = u[c : c + 1], u[own + c : own + c + 1]
                real = real + (w0 * ur - w1 * ui)
                imag = imag + (w1 * ur + w0 * ui)
            for e in range(groups):
                rows = slice(e * own, (e + 1) * own)
                tx2[e, :, at] = jnp.concatenate([real[rows], imag[rows]], axis=0).astype(BF)
    else:
        for start in range(0, wide, chunk):
            at = slice(start, start + chunk)
            lane = lax.broadcasted_iota(jnp.int32, (2 * own, chunk), 1)
            double = jnp.where(lane % KZ == 0, 1.0, 2.0)
            tx2[0, :, at] = (spread(total, start, chunk) * double).astype(BF)
    second = []
    for d in range(1, groups):
        peer = chan_peer[d - 1]
        copy = pltpu.make_async_remote_copy(
            src_ref=tx2.at[peer[1]] if forward else tx2.at[0], dst_ref=rx2.at[chan], send_sem=c_send.at[d - 1], recv_sem=c_recv.at[d - 1],
            device_id=peer, device_id_type=MESH,
        )
        copy.start()
        second.append(copy)
    rx2[chan] = tx2[chan] if forward else tx2[0]
    for copy in second:
        copy.wait_recv()
    result = jnp.zeros((2 * own * KZ, slots), F32)
    for start in range(0, wide, chunk):
        at = slice(start, start + chunk)
        if forward:
            pairs = rx2[0, :, at].astype(F32)
            for e in range(1, groups):
                pairs = pairs + rx2[e, :, at].astype(F32)
            lane = lax.broadcasted_iota(jnp.int32, (2 * own, chunk), 1)
            pairs = pairs * jnp.where(lane % KZ == 0, 1.0, 2.0)
        else:
            blocks = [rx2[e, :, at].astype(F32) for e in range(groups)]
            real = jnp.concatenate([b[:own] for b in blocks], axis=0)
            imag = jnp.concatenate([b[own:] for b in blocks], axis=0)
            reals, imags = [], []
            for c in range(own):
                w0, w1 = w_ref[0, c, :, at].astype(F32), w_ref[1, c, :, at].astype(F32)
                reals.append(jnp.sum(w0 * real + w1 * imag, axis=0, keepdims=True))
                imags.append(jnp.sum(w0 * imag - w1 * real, axis=0, keepdims=True))
            pairs = jnp.concatenate(reals + imags, axis=0)
        result = result + unspread(pairs, start, slots)
    mine[...] = result.astype(BF)
    third = []
    for d in range(1, slabs):
        copy = pltpu.make_async_remote_copy(
            src_ref=mine, dst_ref=recv_ref.at[slab], send_sem=g_send.at[d - 1], recv_sem=g_recv.at[d - 1],
            device_id=slab_peer[d - 1], device_id_type=MESH,
        )
        copy.start()
        third.append(copy)
    recv_ref[slab] = mine[...]
    for copy in third:
        copy.wait_recv()
    for copy in first + second + third:
        copy.wait_send()


def gather_kernel(chips, block_ref, plane_ref, own_sem, x_send, x_recv, p_send, p_recv):
    slab, chan = lax.axis_index("slab"), lax.axis_index("chan")
    height = block_ref.shape[1]
    chip, core = chan // 2, lax.rem(chan, 2)
    partner = (slab, chan + 1 - 2 * core)
    peers = [(slab, 2 * lax.rem(chip + t, chips) + core) for t in range(1, chips)]
    entry_barrier(peers + [partner])

    def rows(index):
        return plane_ref.at[:, pl.ds(pl.multiple_of(index * height, height), height), :]

    own = pltpu.make_async_copy(block_ref, rows(chan), own_sem)
    own.start()
    across = []
    for t in range(1, chips):
        across.append(pltpu.make_async_remote_copy(
            src_ref=block_ref, dst_ref=rows(chan), send_sem=x_send.at[t - 1], recv_sem=x_recv.at[t - 1],
            device_id=peers[t - 1], device_id_type=MESH,
        ))
    order = [1, 3, 2]
    for t in order:
        across[t - 1].start()
    local = [pltpu.make_async_remote_copy(
        src_ref=block_ref, dst_ref=rows(chan), send_sem=p_send.at[0], recv_sem=p_recv.at[0], device_id=partner, device_id_type=MESH,
    )]
    local[0].start()
    for t in order:
        across[t - 1].wait_recv()
        source = 2 * lax.rem(chip + chips - t, chips) + core
        copy = pltpu.make_async_remote_copy(
            src_ref=rows(source), dst_ref=rows(source), send_sem=p_send.at[t], recv_sem=p_recv.at[t], device_id=partner, device_id_type=MESH,
        )
        copy.start()
        local.append(copy)
    own.wait()
    for copy in local:
        copy.wait_recv()
    for copy in across + local:
        copy.wait_send()


def whole(shape):
    zeros = (0,) * len(shape)
    return pl.BlockSpec(shape, lambda *_: zeros, pipeline_mode=pl.Buffered(1))


class Sizes:
    def __init__(self, slabs, groups, channels, planes, grid_len, capacity):
        self.slabs, self.groups = slabs, groups
        self.channels, self.planes, self.grid_len = channels, planes, grid_len
        self.capacity = capacity
        planes_all = channels * planes
        self.x_down, self.x_up, self.y_down, self.y_up = [jnp.asarray(t) for t in plane_tables(grid_len)]
        self.z_down, self.z_up = [jnp.asarray(t) for t in depth_tables(channels, planes, slabs, grid_len)]
        self.per_step = 4
        per_step = self.per_step
        self.steps = planes // per_step
        self.field_spec = pl.BlockSpec((channels, per_step, grid_len, grid_len), lambda i, s: (0, i, 0, 0))
        self.plane_spec = pl.BlockSpec((per_step, grid_len, grid_len), lambda i, s: (i, 0, 0))
        self.z_spec = pl.BlockSpec((1,) + self.z_down.shape[1:], lambda i, s: (s[0], 0, 0), pipeline_mode=pl.Buffered(1))
        self.packed_shape = (slabs, 2 * channels * KZ, capacity)
        self.volume = jax.ShapeDtypeStruct((channels, planes, grid_len, grid_len), BF)
        self.packed_out = jax.ShapeDtypeStruct(self.packed_shape, BF)
        self.wide_scratch = pltpu.VMEM((2 * GROUP * grid_len // LANES, planes_all * KXY // GROUP, LANES), F32)
        self.zt_scratch = pltpu.VMEM((2 * planes_all, KXY * KXY), BF)
        self.params = pltpu.CompilerParams(dimension_semantics=("arbitrary",), vmem_limit_bytes=30 << 20)


SMEM = pl.BlockSpec(memory_space=pltpu.SMEM)
VMEM = pl.BlockSpec(memory_space=pltpu.VMEM)
ANY = pl.BlockSpec(memory_space=pl.ANY)


def gather_call(z, forcing):
    chips = z.groups // 2
    return pl.pallas_call(
        functools.partial(gather_kernel, chips),
        out_shape=jax.ShapeDtypeStruct((z.planes, z.grid_len, z.grid_len), BF),
        in_specs=[ANY],
        out_specs=ANY,
        scratch_shapes=[pltpu.SemaphoreType.DMA] + [pltpu.SemaphoreType.DMA((chips - 1,))] * 2 + [pltpu.SemaphoreType.DMA((chips,))] * 2,
        compiler_params=pltpu.CompilerParams(collective_id=0, has_side_effects=True),
        name="gather_forcing",
    )(forcing)


def analyse_call(z, where, field, plane, slots):
    return pl.pallas_call(
        functools.partial(analyse_kernel, z.per_step),
        out_shape=(z.packed_out, z.volume),
        grid_spec=pltpu.PrefetchScalarGridSpec(
            num_scalar_prefetch=1, grid=(z.steps,),
            in_specs=[z.field_spec, z.plane_spec, whole(slots.shape), whole(z.x_down.shape), whole(z.y_down.shape), z.z_spec],
            out_specs=(VMEM, VMEM),
            scratch_shapes=[z.wide_scratch, z.zt_scratch],
        ),
        compiler_params=z.params,
        name="analyse",
    )(where, field, plane, slots, z.x_down, z.y_down, z.z_down)


def exchange_call(z, values, w_spec, forward):
    block = z.packed_shape[1:]
    pair = (z.groups, 2 * z.channels, z.capacity * KZ)
    return pl.pallas_call(
        functools.partial(mix_kernel, z.slabs, z.groups, forward),
        out_shape=z.packed_out,
        in_specs=[VMEM, VMEM],
        out_specs=VMEM,
        scratch_shapes=[
            pltpu.VMEM((z.slabs - 1,) + block, BF),
            pltpu.VMEM(block, F32),
            pltpu.VMEM(pair, BF),
            pltpu.VMEM(pair, BF),
            pltpu.VMEM(block, BF),
        ]
        + [pltpu.SemaphoreType.DMA((z.slabs - 1,))] * 2
        + [pltpu.SemaphoreType.DMA((z.groups - 1,))] * 2
        + [pltpu.SemaphoreType.DMA((z.slabs - 1,))] * 2,
        compiler_params=pltpu.CompilerParams(collective_id=1 if forward else 2, has_side_effects=True, vmem_limit_bytes=8 << 20),
        name="mix_forward" if forward else "mix_adjoint",
    )(values, w_spec)


def middle_call(z, where, skip_gain, bias, merged, spectra, slots):
    return pl.pallas_call(
        functools.partial(middle_kernel, z.per_step, 64),
        out_shape=(z.volume, z.volume, z.packed_out),
        grid_spec=pltpu.PrefetchScalarGridSpec(
            num_scalar_prefetch=1, grid=(z.steps,),
            in_specs=[SMEM, SMEM, VMEM, VMEM, whole(slots.shape), whole(z.x_down.shape), whole(z.x_up.shape), whole(z.y_down.shape), whole(z.y_up.shape), z.z_spec, z.z_spec],
            out_specs=(z.field_spec, VMEM, VMEM),
            scratch_shapes=[z.wide_scratch, z.wide_scratch, z.zt_scratch] + [pltpu.VMEM((z.grid_len, z.grid_len), F32)] * 2,
        ),
        compiler_params=z.params,
        name="synth_gelu_analyse",
    )(where, skip_gain, bias, merged, spectra, slots, z.x_down, z.x_up, z.y_down, z.y_up, z.z_down, z.z_up)


def final_call(z, where, skip_gain, grad_pre, adjoint, slots):
    return pl.pallas_call(
        functools.partial(final_kernel, z.per_step, 64),
        out_shape=z.volume,
        grid_spec=pltpu.PrefetchScalarGridSpec(
            num_scalar_prefetch=1, grid=(z.steps,),
            in_specs=[SMEM, VMEM, VMEM, whole(slots.shape), whole(z.x_up.shape), whole(z.y_up.shape), z.z_spec],
            out_specs=z.field_spec,
            scratch_shapes=[z.wide_scratch, z.zt_scratch],
        ),
        compiler_params=z.params,
        name="synth_gradient",
    )(where, skip_gain, grad_pre, adjoint, slots, z.x_up, z.y_up, z.z_up)


def per_device(slabs, groups, field, forcing, slot_column, w_spec, skip_gain, bias):
    channels, planes, grid_len, _ = field.shape
    capacity = slot_column.shape[1]
    z = Sizes(slabs, groups, channels, planes, grid_len, capacity)
    slots = slot_column.reshape(1, slabs * capacity)
    where = lax.axis_index("slab").astype(jnp.int32).reshape(1)
    plane = gather_call(z, forcing)
    packed, merged = analyse_call(z, where, field, plane, slots)
    spectra = exchange_call(z, packed, w_spec, True)
    output, grad_pre, packed_back = middle_call(z, where, skip_gain, bias, merged, spectra, slots)
    adjoint = exchange_call(z, packed_back, w_spec, False)
    gradient = final_call(z, where, skip_gain, grad_pre, adjoint, slots)
    return (output, gradient)


def solution(mesh):
    placed = (
        P("chan", "slab", None, None),
        P("slab", "chan", None),
        P(),
        P(None, "chan", None, "slab"),
        P("chan"),
        P("chan"),
    )
    slabs, groups = mesh.shape["slab"], mesh.shape["chan"]
    return jax.shard_map(
        functools.partial(per_device, slabs, groups),
        mesh=mesh,
        in_specs=placed,
        out_specs=(P("chan", "slab", None, None), P("chan", "slab", None, None)),
        check_vma=False,
    )
```

```python
import functools
import math

import jax
import jax.numpy as jnp
import ml_dtypes
import numpy as np
from jax import lax
from jax.experimental import pallas as pl
from jax.experimental.pallas import tpu as pltpu
from jax.sharding import PartitionSpec as P

KXY = 32
KZ = 16
MESH = pl.DeviceIdType.MESH
BF = jnp.bfloat16
F32 = jnp.float32
LANES = 128
GROUP = LANES // KXY


def bf16_table(values):
    return np.asarray(values, np.float32).astype(ml_dtypes.bfloat16)


def trig(freqs, coords, grid_len):
    angle = (np.outer(freqs, coords) % grid_len) * (2.0 * math.pi / grid_len)
    return np.cos(angle), np.sin(angle)


def plane_tables(grid_len):
    freqs = np.arange(KXY) - KXY // 2
    cos, sin = trig(freqs, np.arange(grid_len), grid_len)
    groups = KXY // GROUP
    scale = float(grid_len) ** -1.5
    x_down = np.zeros((GROUP, 2, groups, grid_len))
    x_up = np.zeros((grid_len, GROUP, 2, groups))
    y_down = np.zeros((GROUP, 2, grid_len, 2, GROUP, KXY))
    y_up = np.zeros((2, GROUP, KXY, GROUP, 2, grid_len))
    for k in range(GROUP):
        for g in range(groups):
            jx = g * GROUP + k
            x_down[k, 0, g], x_down[k, 1, g] = cos[jx], sin[jx]
            x_up[:, k, 0, g], x_up[:, k, 1, g] = scale * cos[jx], -scale * sin[jx]
        y_down[k, 0, :, 0, k], y_down[k, 1, :, 0, k] = cos.T, -sin.T
        y_down[k, 0, :, 1, k], y_down[k, 1, :, 1, k] = -sin.T, -cos.T
        y_up[0, k, :, k, 0], y_up[1, k, :, k, 0] = cos, -sin
        y_up[0, k, :, k, 1], y_up[1, k, :, k, 1] = sin, cos
    rows = 2 * KXY
    return (
        bf16_table(x_down.reshape(rows, grid_len)),
        bf16_table(x_up.reshape(grid_len, rows)),
        bf16_table(y_down.reshape(2 * GROUP * grid_len, 2 * LANES)),
        bf16_table(y_up.reshape(2 * LANES, 2 * GROUP * grid_len)),
    )


def depth_tables(channels, planes, slabs, grid_len):
    scale = float(grid_len) ** -1.5
    down, up = [], []
    eye = np.eye(channels)
    for s in range(slabs):
        cos, sin = trig(np.arange(KZ), s * planes + np.arange(planes), grid_len)
        parts = [[cos, sin], [-sin, cos]]
        full = np.zeros((2, channels, KZ, 2, channels, planes))
        for q in range(2):
            for r in range(2):
                full[q, :, :, r] = np.einsum("cd,mz->cmdz", eye, parts[q][r])
        full = full.reshape(2 * channels * KZ, 2 * channels * planes)
        for store, table in ((down, full * scale), (up, full.T)):
            high = bf16_table(table)
            low = bf16_table(table - high.astype(np.float64))
            store.append(np.concatenate([high, low], axis=1))
    return np.stack(down), np.stack(up)


def dot(a, b):
    return jnp.dot(a, b, preferred_element_type=F32)


def dot_nt(a, b):
    return lax.dot_general(a, b, (((1,), (1,)), ((), ())), preferred_element_type=F32)


def twice(block):
    return jnp.concatenate([block, block], axis=0)


def keep_x_rows(xs_ref, plane, planes_all, value):
    groups = KXY // GROUP
    width = value.shape[1]
    tiles = width // LANES
    for kp in range(2 * GROUP):
        for h in range(tiles):
            xs_ref[kp * tiles + h, pl.ds(plane, groups, stride=planes_all), :] = value[
                kp * groups : (kp + 1) * groups, h * LANES : (h + 1) * LANES
            ]


def plane_rows(ws_ref, plane, planes_all, width):
    groups = KXY // GROUP
    tiles = width // LANES
    columns = []
    for h in range(tiles):
        parts = [ws_ref[kp * tiles + h, pl.ds(plane, groups, stride=planes_all), :] for kp in range(2 * GROUP)]
        columns.append(jnp.concatenate(parts, axis=0))
    return jnp.concatenate(columns, axis=1)


def y_pass(xs_ref, y_down_ref):
    lhs = jnp.concatenate([xs_ref[j].astype(BF) for j in range(xs_ref.shape[0])], axis=1)
    return dot(lhs, y_down_ref[...])


def local_spectra(xs_ref, y_down_ref, z_down, zt_ref, shared_ref=None):
    planes_all = xs_ref.shape[1] * GROUP // KXY
    spectra = y_pass(xs_ref, y_down_ref)
    if shared_ref is not None:
        planes = shared_ref.shape[1] * GROUP // KXY
        shared = y_pass(shared_ref, y_down_ref)
    for g in range(KXY // GROUP):
        for q in range(2):
            lanes = slice(q * LANES, (q + 1) * LANES)
            part = spectra[g * planes_all : (g + 1) * planes_all, lanes]
            if shared_ref is not None:
                part = part + jnp.concatenate([shared[g * planes : (g + 1) * planes, lanes]] * (planes_all // planes), axis=0)
            zt_ref[q * planes_all : (q + 1) * planes_all, g * LANES : (g + 1) * LANES] = part.astype(BF)
    return dot(z_down, twice(zt_ref[...])).astype(BF)


def pack_columns(coeffs, slot_row):
    column = lax.broadcasted_iota(jnp.int32, (coeffs.shape[1], slot_row.shape[1]), 0)
    return dot(coeffs, (column == slot_row).astype(F32).astype(BF)).astype(BF)


def analysis_tail(xs_ref, y_down_ref, z_down_ref, slot_ref, zt_ref, packed_ref):
    coeffs = local_spectra(xs_ref, y_down_ref, z_down_ref[0], zt_ref)
    capacity = packed_ref.shape[2]
    chunk = 2 * capacity
    for n in range(slot_ref.shape[1] // chunk):
        part = pack_columns(coeffs, slot_ref[0:1, n * chunk : (n + 1) * chunk])
        packed_ref[2 * n] = part[:, :capacity]
        packed_ref[2 * n + 1] = part[:, capacity:]


def synthesis_head(recv_ref, slot_ref, z_up_ref, y_up_ref, zt_ref, ws_ref):
    planes_all = ws_ref.shape[1] * GROUP // KXY
    slabs = recv_ref.shape[0]
    by_slot = jnp.concatenate([recv_ref[s] for s in range(slabs)], axis=1)
    slots = by_slot.shape[1]
    chunk = 2 * LANES
    column = lax.broadcasted_iota(jnp.int32, (chunk, slots), 0)
    for n in range(KXY * KXY // chunk):
        pick = (column + n * chunk == slot_ref[0:1, :]).astype(F32).astype(BF)
        spectra = dot_nt(by_slot, pick).astype(BF)
        zt_ref[:, n * chunk : (n + 1) * chunk] = dot(z_up_ref[0], twice(spectra)).astype(BF)
    rows = []
    for g in range(KXY // GROUP):
        at = slice(g * LANES, (g + 1) * LANES)
        rows.append(jnp.concatenate([zt_ref[:planes_all, at], zt_ref[planes_all:, at]], axis=1))
    lhs = jnp.concatenate(rows, axis=0)
    chunk = 2 * LANES
    for j in range(ws_ref.shape[0] // 2):
        wide = dot(lhs, y_up_ref[:, j * chunk : (j + 1) * chunk])
        ws_ref[2 * j] = wide[:, :LANES]
        ws_ref[2 * j + 1] = wide[:, LANES:]


def gelu_pair(half):
    coeff = math.sqrt(2.0 / math.pi)
    square = half * half
    tangent = jnp.tanh(half * (2.0 * coeff + (8.0 * 0.044715 * coeff) * square))
    above = 1.0 + tangent
    value = half * above
    slope = above * (0.5 + (half * (1.0 - tangent)) * (coeff + (12.0 * 0.044715 * coeff) * square))
    return value, slope


class Planes:
    def __init__(self, step, per_step, channels, planes):
        self.step, self.per_step, self.count = step, per_step, per_step * channels
        self.planes, self.planes_all = planes, planes * channels

    def place(self, t):
        c = t // self.per_step
        zz = t - c * self.per_step
        return c, zz, c * self.planes + self.step * self.per_step + zz


def middle_kernel(per_step, rows, slab_ref, gain_ref, bias_ref, merged_ref, recv_ref, slot_ref, x_down_ref, x_up_ref, y_down_ref, y_up_ref, z_down_ref, z_up_ref, out_ref, grad_ref, packed_ref, xs_ref, ws_ref, zt_ref, sa_ref, sb_ref):
    step = pl.program_id(0)
    channels, _, grid_len, _ = merged_ref.shape
    at = Planes(step, per_step, channels, xs_ref.shape[1] * GROUP // KXY // channels)

    @pl.when(step == 0)
    def _():
        synthesis_head(recv_ref, slot_ref, z_up_ref, y_up_ref, zt_ref, ws_ref)

    def synth(t, s_ref):
        wp = plane_rows(ws_ref, at.place(t)[2], at.planes_all, grid_len).astype(BF)
        s_ref[...] = dot(x_up_ref[...], wp)

    def point(t, s_ref):
        c, zz, _ = at.place(t)
        zz_all = step * per_step + zz
        gain, bias = 0.5 * gain_ref[c], 0.5 * bias_ref[c]
        for start in range(0, grid_len, rows):
            span = slice(start, start + rows)
            merged = merged_ref[c, zz_all, span, :]
            value, slope = gelu_pair(0.5 * s_ref[span, :] + (gain * merged.astype(F32) + bias))
            out_ref[c, zz, span, :] = value.astype(BF)
            grad_ref[c, zz_all, span, :] = (value * slope).astype(BF)

    def down(t):
        c, zz, plane = at.place(t)
        keep_x_rows(xs_ref, plane, at.planes_all, dot(x_down_ref[...], grad_ref[c, step * per_step + zz]))

    synth(0, sa_ref)

    def body(j, carry):
        t = 2 * j
        synth(t + 1, sb_ref)
        down(jnp.maximum(t - 1, 0))
        point(t, sa_ref)
        synth(jnp.minimum(t + 2, at.count - 1), sa_ref)
        down(t)
        point(t + 1, sb_ref)
        return carry

    lax.fori_loop(0, at.count // 2, body, 0)
    down(at.count - 1)

    @pl.when(step == pl.num_programs(0) - 1)
    def _():
        analysis_tail(xs_ref, y_down_ref, z_down_ref, slot_ref, zt_ref, packed_ref)


def final_kernel(per_step, rows, slab_ref, gain_ref, grad_ref, recv_ref, slot_ref, x_up_ref, y_up_ref, z_up_ref, out_ref, ws_ref, zt_ref):
    step = pl.program_id(0)
    channels, _, grid_len, _ = grad_ref.shape
    at = Planes(step, per_step, channels, ws_ref.shape[1] * GROUP // KXY // channels)

    @pl.when(step == 0)
    def _():
        synthesis_head(recv_ref, slot_ref, z_up_ref, y_up_ref, zt_ref, ws_ref)

    def body(zz, carry):
        for c in range(channels):
            wp = plane_rows(ws_ref, c * at.planes + step * per_step + zz, at.planes_all, grid_len).astype(BF)
            out_ref[c, zz] = (dot(x_up_ref[...], wp) + gain_ref[c] * grad_ref[c, step * per_step + zz].astype(F32)).astype(BF)
        return carry

    lax.fori_loop(0, per_step, body, 0)


def entry_barrier(targets):
    barrier = pltpu.get_barrier_semaphore()
    for target in targets:
        pl.semaphore_signal(barrier, inc=1, device_id=target, device_id_type=MESH)
    pl.semaphore_wait(barrier, len(targets))


def spread(block, start, width):
    slots = block.shape[1]
    lane = lax.broadcasted_iota(jnp.int32, (slots, width), 1) + start
    row = lax.broadcasted_iota(jnp.int32, (slots, width), 0)
    expand = (lane // KZ == row).astype(F32).astype(BF)
    high = block.astype(BF)
    low = (block - high.astype(F32)).astype(BF)
    wide = dot(high, expand) + dot(low, expand)
    pairs = wide.shape[0] // KZ
    wide = wide.reshape(pairs, KZ, width)
    m_row = lax.broadcasted_iota(jnp.int32, wide.shape, 1)
    m_lane = lax.broadcasted_iota(jnp.int32, wide.shape, 2) % KZ
    return jnp.sum(jnp.where(m_row == m_lane, wide, 0.0), axis=1)


def unspread(pairs, start, slots):
    count, width = pairs.shape
    shape = (count, KZ, width)
    m_row = lax.broadcasted_iota(jnp.int32, shape, 1)
    m_lane = lax.broadcasted_iota(jnp.int32, shape, 2) % KZ
    wide = jnp.where(m_row == m_lane, jnp.broadcast_to(pairs[:, None, :], shape), 0.0)
    wide = wide.reshape(count * KZ, width).astype(BF)
    lane = lax.broadcasted_iota(jnp.int32, (slots, width), 1) + start
    row = lax.broadcasted_iota(jnp.int32, (slots, width), 0)
    collect = (lane // KZ == row).astype(F32).astype(BF)
    return dot_nt(wide, collect)


def peers_of(slabs, groups):
    slab, chan = lax.axis_index("slab"), lax.axis_index("chan")
    slab_peer = [(lax.rem(slab + d, slabs), chan) for d in range(1, slabs)]
    chan_peer = [(slab, lax.rem(chan + d, groups)) for d in range(1, groups)]
    return slab, chan, slab_peer, chan_peer


def spectra_copy(packed_ref, rx, peer, d, s_send, s_recv):
    return pltpu.make_async_remote_copy(
        src_ref=packed_ref.at[peer[0]], dst_ref=rx.at[d - 1], send_sem=s_send.at[d - 1], recv_sem=s_recv.at[d - 1],
        device_id=peer, device_id_type=MESH,
    )


def mix_kernel(slabs, groups, forward, packed_ref, w_ref, recv_ref, rx, tx2, rx2, mine, *sems):
    _, _, slab_peer, chan_peer = peers_of(slabs, groups)
    entry_barrier(slab_peer + chan_peer)
    first = [spectra_copy(packed_ref, rx, slab_peer[d - 1], d, *sems[:2]) for d in range(1, slabs)]
    for copy in first:
        copy.start()
    exchange_body(slabs, groups, forward, first, packed_ref, w_ref, recv_ref, rx, tx2, rx2, mine, *sems)


def exchange_body(slabs, groups, forward, first, packed_ref, w_ref, recv_ref, rx, tx2, rx2, mine, s_send, s_recv, c_send, c_recv, g_send, g_recv):
    slab, chan, slab_peer, chan_peer = peers_of(slabs, groups)
    total = packed_ref[slab].astype(F32)
    for d in range(1, slabs):
        first[d - 1].wait_recv()
        total = total + rx[d - 1].astype(F32)
    slots = total.shape[1]
    wide = slots * KZ
    chunk = 512
    own = rx2.shape[1] // 2
    outputs = own * groups
    if forward:
        for start in range(0, wide, chunk):
            at = slice(start, start + chunk)
            u = spread(total, start, chunk)
            real = jnp.zeros((outputs, chunk), F32)
            imag = jnp.zeros((outputs, chunk), F32)
            for c in range(own):
                w0, w1 = w_ref[0, c, :, at].astype(F32), w_ref[1, c, :, at].astype(F32)
                ur, ui = u[c : c + 1], u[own + c : own + c + 1]
                real = real + (w0 * ur - w1 * ui)
                imag = imag + (w1 * ur + w0 * ui)
            for e in range(groups):
                rows = slice(e * own, (e + 1) * own)
                tx2[e, :, at] = jnp.concatenate([real[rows], imag[rows]], axis=0).astype(BF)
    else:
        for start in range(0, wide, chunk):
            at = slice(start, start + chunk)
            lane = lax.broadcasted_iota(jnp.int32, (2 * own, chunk), 1)
            double = jnp.where(lane % KZ == 0, 1.0, 2.0)
            tx2[0, :, at] = (spread(total, start, chunk) * double).astype(BF)
    second = []
    for d in range(1, groups):
        peer = chan_peer[d - 1]
        copy = pltpu.make_async_remote_copy(
            src_ref=tx2.at[peer[1]] if forward else tx2.at[0], dst_ref=rx2.at[chan], send_sem=c_send.at[d - 1], recv_sem=c_recv.at[d - 1],
            device_id=peer, device_id_type=MESH,
        )
        copy.start()
        second.append(copy)
    rx2[chan] = tx2[chan] if forward else tx2[0]
    for copy in second:
        copy.wait_recv()
    result = jnp.zeros((2 * own * KZ, slots), F32)
    for start in range(0, wide, chunk):
        at = slice(start, start + chunk)
        if forward:
            pairs = rx2[0, :, at].astype(F32)
            for e in range(1, groups):
                pairs = pairs + rx2[e, :, at].astype(F32)
            lane = lax.broadcasted_iota(jnp.int32, (2 * own, chunk), 1)
            pairs = pairs * jnp.where(lane % KZ == 0, 1.0, 2.0)
        else:
            blocks = [rx2[e, :, at].astype(F32) for e in range(groups)]
            real = jnp.concatenate([b[:own] for b in blocks], axis=0)
            imag = jnp.concatenate([b[own:] for b in blocks], axis=0)
            reals, imags = [], []
            for c in range(own):
                w0, w1 = w_ref[0, c, :, at].astype(F32), w_ref[1, c, :, at].astype(F32)
                reals.append(jnp.sum(w0 * real + w1 * imag, axis=0, keepdims=True))
                imags.append(jnp.sum(w0 * imag - w1 * real, axis=0, keepdims=True))
            pairs = jnp.concatenate(reals + imags, axis=0)
        result = result + unspread(pairs, start, slots)
    mine[...] = result.astype(BF)
    third = []
    for d in range(1, slabs):
        copy = pltpu.make_async_remote_copy(
            src_ref=mine, dst_ref=recv_ref.at[slab], send_sem=g_send.at[d - 1], recv_sem=g_recv.at[d - 1],
            device_id=slab_peer[d - 1], device_id_type=MESH,
        )
        copy.start()
        third.append(copy)
    recv_ref[slab] = mine[...]
    for copy in third:
        copy.wait_recv()
    for copy in first + second + third:
        copy.wait_send()


def front_kernel(slabs, groups, field_hbm, forcing_hbm, slots_hbm, w_hbm, x_down_hbm, y_down_hbm, z_down_hbm, recv_ref, merged_ref,
                 plane_ref, xs_ref, xf_ref, zt_ref, packed_ref, rx, tx2, rx2, mine, slot_ref, w_ref, x_down_ref, y_down_ref, z_down_ref,
                 in_sem, field_sem, x_send, x_recv, p_send, p_recv, *sems):
    slab, chan, slab_peer, chan_peer = peers_of(slabs, groups)
    channels, planes = merged_ref.shape[:2]
    planes_all = channels * planes
    height = forcing_hbm.shape[1]
    chips = groups // 2
    chip, core = chan // 2, lax.rem(chan, 2)
    partner = (slab, chan + 1 - 2 * core)

    def near(t):
        return 2 * lax.rem(chip + chips + t, chips) + core

    def rows(index, start, count):
        return plane_ref.at[pl.ds(start, count), pl.ds(pl.multiple_of(index * height, height), height), :]

    fields = [pltpu.make_async_copy(field_hbm.at[c], merged_ref.at[c], field_sem.at[c]) for c in range(channels)]
    loads = [
        pltpu.make_async_copy(x_down_hbm, x_down_ref, in_sem.at[0]),
        pltpu.make_async_copy(y_down_hbm, y_down_ref, in_sem.at[1]),
        pltpu.make_async_copy(z_down_hbm.at[slab], z_down_ref, in_sem.at[2]),
        pltpu.make_async_copy(slots_hbm, slot_ref, in_sem.at[3]),
        pltpu.make_async_copy(w_hbm, w_ref, in_sem.at[4]),
        pltpu.make_async_copy(forcing_hbm, rows(chan, 0, planes), in_sem.at[5]),
    ]
    loads[0].start()
    for copy in fields + loads[1:]:
        copy.start()
    entry_barrier(slab_peer + chan_peer)

    half = planes // 2

    def across(index, start, to, n, source=None):
        return pltpu.make_async_remote_copy(
            src_ref=rows(index, start, half) if source is None else source, dst_ref=rows(index, start, half),
            send_sem=x_send.at[n], recv_sem=x_recv.at[n], device_id=(slab, to), device_id_type=MESH,
        )

    def beside(index, start, count, n, source=None):
        return pltpu.make_async_remote_copy(
            src_ref=rows(index, start, count) if source is None else source, dst_ref=rows(index, start, count),
            send_sem=p_send.at[n], recv_sem=p_recv.at[n], device_id=partner, device_id_type=MESH,
        )

    low, high = forcing_hbm.at[pl.ds(0, half)], forcing_hbm.at[pl.ds(half, half)]
    right_low = across(chan, 0, near(1), 0, low)
    left_high = across(chan, half, near(-1), 1, high)
    right_high = across(chan, half, near(1), 2, high)
    left_low = across(chan, 0, near(-1), 3, low)
    for copy in (right_low, left_high, right_high, left_low):
        copy.start()
    own = beside(chan, 0, planes, 0, forcing_hbm)
    own.start()
    sent = [right_low, left_high, right_high, left_low, own]
    beside_all = [own]

    def pass_on(copies):
        for copy in copies:
            copy.start()
            sent.append(copy)

    def x_pass(c):
        fields[c].wait()

        def body(zz, carry):
            keep_x_rows(xs_ref, c * planes + zz, planes_all, dot(x_down_ref[...], merged_ref[c, zz]))
            return carry

        lax.fori_loop(0, planes, body, 0, unroll=4)

    loads[0].wait()
    x_pass(0)
    right_low.wait_recv()
    left_high.wait_recv()
    far_low = across(near(-1), 0, near(1), 4)
    far_high = across(near(1), half, near(-1), 5)
    more = [beside(near(-1), 0, half, 1), beside(near(1), half, half, 2)]
    beside_all += more
    pass_on([far_low, far_high] + more)
    x_pass(1)
    right_high.wait_recv()
    left_low.wait_recv()
    more = [beside(near(-1), half, half, 3), beside(near(1), 0, half, 4)]
    beside_all += more
    pass_on(more)
    for c in range(2, channels):
        x_pass(c)
    far_low.wait_recv()
    far_high.wait_recv()
    more = [beside(near(2), 0, half, 5), beside(near(2), half, half, 6)]
    beside_all += more
    pass_on(more)
    loads[5].wait()
    for copy in beside_all:
        copy.wait_recv()

    def forcing_body(zz, carry):
        keep_x_rows(xf_ref, zz, planes, dot(x_down_ref[...], plane_ref[zz]))
        return carry

    lax.fori_loop(0, planes, forcing_body, 0, unroll=4)
    for copy in loads[1:4]:
        copy.wait()
    coeffs = local_spectra(xs_ref, y_down_ref, z_down_ref[...], zt_ref, xf_ref)
    capacity = packed_ref.shape[2]
    first = []
    for d in range(1, slabs, 2):
        targets = [lax.rem(slab + d, slabs), lax.rem(slab + d + 1, slabs)]
        part = pack_columns(coeffs, jnp.concatenate([slot_ref[pl.ds(t, 1), :] for t in targets], axis=1))
        for n, t in enumerate(targets):
            packed_ref[t] = part[:, n * capacity : (n + 1) * capacity]
            if d + n < slabs:
                copy = spectra_copy(packed_ref, rx, slab_peer[d + n - 1], d + n, *sems[:2])
                copy.start()
                first.append(copy)

    def merge_body(zz, carry):
        for c in range(channels):
            merged_ref[c, zz] = merged_ref[c, zz] + plane_ref[zz]
        return carry

    lax.fori_loop(0, planes, merge_body, 0)
    loads[4].wait()
    exchange_body(slabs, groups, True, first, packed_ref, w_ref, recv_ref, rx, tx2, rx2, mine, *sems)
    for copy in sent:
        copy.wait_send()


def whole(shape):
    zeros = (0,) * len(shape)
    return pl.BlockSpec(shape, lambda *_: zeros, pipeline_mode=pl.Buffered(1))


class Sizes:
    def __init__(self, slabs, groups, channels, planes, grid_len, capacity):
        self.slabs, self.groups = slabs, groups
        self.channels, self.planes, self.grid_len = channels, planes, grid_len
        self.capacity = capacity
        planes_all = channels * planes
        self.x_down, self.x_up, self.y_down, self.y_up = [jnp.asarray(t) for t in plane_tables(grid_len)]
        self.z_down, self.z_up = [jnp.asarray(t) for t in depth_tables(channels, planes, slabs, grid_len)]
        self.per_step = 4
        per_step = self.per_step
        self.steps = planes // per_step
        self.field_spec = pl.BlockSpec((channels, per_step, grid_len, grid_len), lambda i, s: (0, i, 0, 0))
        self.plane_spec = pl.BlockSpec((per_step, grid_len, grid_len), lambda i, s: (i, 0, 0))
        self.z_spec = pl.BlockSpec((1,) + self.z_down.shape[1:], lambda i, s: (s[0], 0, 0), pipeline_mode=pl.Buffered(1))
        self.packed_shape = (slabs, 2 * channels * KZ, capacity)
        self.volume = jax.ShapeDtypeStruct((channels, planes, grid_len, grid_len), BF)
        self.packed_out = jax.ShapeDtypeStruct(self.packed_shape, BF)
        self.wide_scratch = pltpu.VMEM((2 * GROUP * grid_len // LANES, planes_all * KXY // GROUP, LANES), F32)
        self.zt_scratch = pltpu.VMEM((2 * planes_all, KXY * KXY), BF)
        self.params = pltpu.CompilerParams(dimension_semantics=("arbitrary",), vmem_limit_bytes=30 << 20)


SMEM = pl.BlockSpec(memory_space=pltpu.SMEM)
VMEM = pl.BlockSpec(memory_space=pltpu.VMEM)
HBM = pl.BlockSpec(memory_space=pltpu.HBM)


def front_call(z, field, forcing, slot_column, w_spec):
    block = z.packed_shape[1:]
    pair = (z.groups, 2 * z.channels, z.capacity * KZ)
    tiles = 2 * GROUP * z.grid_len // LANES
    dma = pltpu.SemaphoreType.DMA
    return pl.pallas_call(
        functools.partial(front_kernel, z.slabs, z.groups),
        out_shape=(z.packed_out, z.volume),
        in_specs=[HBM] * 7,
        out_specs=(VMEM, VMEM),
        scratch_shapes=[
            pltpu.VMEM((z.planes, z.grid_len, z.grid_len), BF),
            z.wide_scratch,
            pltpu.VMEM((tiles, z.planes * KXY // GROUP, LANES), F32),
            z.zt_scratch,
            pltpu.VMEM(z.packed_shape, BF),
            pltpu.VMEM((z.slabs - 1,) + block, BF),
            pltpu.VMEM(pair, BF),
            pltpu.VMEM(pair, BF),
            pltpu.VMEM(block, BF),
            pltpu.VMEM(slot_column.shape, jnp.int32),
            pltpu.VMEM(w_spec.shape, BF),
            pltpu.VMEM(z.x_down.shape, BF),
            pltpu.VMEM(z.y_down.shape, BF),
            pltpu.VMEM(z.z_down.shape[1:], BF),
            dma((6,)), dma((z.channels,)), dma((6,)), dma((6,)), dma((7,)), dma((7,)),
        ]
        + [dma((z.slabs - 1,))] * 2 + [dma((z.groups - 1,))] * 2 + [dma((z.slabs - 1,))] * 2,
        compiler_params=pltpu.CompilerParams(collective_id=1, has_side_effects=True, vmem_limit_bytes=26 << 20),
        name="gather_analyse_mix",
    )(*[pltpu.with_memory_space_constraint(v, pltpu.HBM) for v in (field, forcing, slot_column, w_spec, z.x_down, z.y_down, z.z_down)])


def exchange_call(z, values, w_spec):
    block = z.packed_shape[1:]
    pair = (z.groups, 2 * z.channels, z.capacity * KZ)
    return pl.pallas_call(
        functools.partial(mix_kernel, z.slabs, z.groups, False),
        out_shape=z.packed_out,
        in_specs=[VMEM, VMEM],
        out_specs=VMEM,
        scratch_shapes=[
            pltpu.VMEM((z.slabs - 1,) + block, BF),
            pltpu.VMEM(pair, BF),
            pltpu.VMEM(pair, BF),
            pltpu.VMEM(block, BF),
        ]
        + [pltpu.SemaphoreType.DMA((z.slabs - 1,))] * 2
        + [pltpu.SemaphoreType.DMA((z.groups - 1,))] * 2
        + [pltpu.SemaphoreType.DMA((z.slabs - 1,))] * 2,
        compiler_params=pltpu.CompilerParams(collective_id=2, has_side_effects=True, vmem_limit_bytes=8 << 20),
        name="mix_adjoint",
    )(values, w_spec)


def middle_call(z, where, skip_gain, bias, merged, spectra, slots):
    return pl.pallas_call(
        functools.partial(middle_kernel, z.per_step, 64),
        out_shape=(z.volume, z.volume, z.packed_out),
        grid_spec=pltpu.PrefetchScalarGridSpec(
            num_scalar_prefetch=1, grid=(z.steps,),
            in_specs=[SMEM, SMEM, VMEM, VMEM, whole(slots.shape), whole(z.x_down.shape), whole(z.x_up.shape), whole(z.y_down.shape), whole(z.y_up.shape), z.z_spec, z.z_spec],
            out_specs=(z.field_spec, VMEM, VMEM),
            scratch_shapes=[z.wide_scratch, z.wide_scratch, z.zt_scratch] + [pltpu.VMEM((z.grid_len, z.grid_len), F32)] * 2,
        ),
        compiler_params=z.params,
        name="synth_gelu_analyse",
    )(where, skip_gain, bias, merged, spectra, slots, z.x_down, z.x_up, z.y_down, z.y_up, z.z_down, z.z_up)


def final_call(z, where, skip_gain, grad_pre, adjoint, slots):
    return pl.pallas_call(
        functools.partial(final_kernel, z.per_step, 64),
        out_shape=z.volume,
        grid_spec=pltpu.PrefetchScalarGridSpec(
            num_scalar_prefetch=1, grid=(z.steps,),
            in_specs=[SMEM, VMEM, VMEM, whole(slots.shape), whole(z.x_up.shape), whole(z.y_up.shape), z.z_spec],
            out_specs=z.field_spec,
            scratch_shapes=[z.wide_scratch, z.zt_scratch],
        ),
        compiler_params=z.params,
        name="synth_gradient",
    )(where, skip_gain, grad_pre, adjoint, slots, z.x_up, z.y_up, z.z_up)


def per_device(slabs, groups, field, forcing, slot_column, w_spec, skip_gain, bias):
    channels, planes, grid_len, _ = field.shape
    capacity = slot_column.shape[1]
    z = Sizes(slabs, groups, channels, planes, grid_len, capacity)
    slots = slot_column.reshape(1, slabs * capacity)
    where = lax.axis_index("slab").astype(jnp.int32).reshape(1)
    spectra, merged = front_call(z, field, forcing, slot_column, w_spec)
    output, grad_pre, packed_back = middle_call(z, where, skip_gain, bias, merged, spectra, slots)
    adjoint = exchange_call(z, packed_back, w_spec)
    gradient = final_call(z, where, skip_gain, grad_pre, adjoint, slots)
    return (output, gradient)


def solution(mesh):
    placed = (
        P("chan", "slab", None, None),
        P("slab", "chan", None),
        P(),
        P(None, "chan", None, "slab"),
        P("chan"),
        P("chan"),
    )
    slabs, groups = mesh.shape["slab"], mesh.shape["chan"]
    return jax.shard_map(
        functools.partial(per_device, slabs, groups),
        mesh=mesh,
        in_specs=placed,
        out_specs=(P("chan", "slab", None, None), P("chan", "slab", None, None)),
        check_vma=False,
    )
```

```python
import functools
import math

import jax
import jax.numpy as jnp
import ml_dtypes
import numpy as np
from jax import lax
from jax.experimental import pallas as pl
from jax.experimental.pallas import tpu as pltpu
from jax.sharding import PartitionSpec as P

KXY = 32
KZ = 16
MESH = pl.DeviceIdType.MESH
BF = jnp.bfloat16
F32 = jnp.float32
LANES = 128
BIAS_ROWS = 16
GROUP = LANES // KXY


def bf16_table(values):
    return np.asarray(values, np.float32).astype(ml_dtypes.bfloat16)


def trig(freqs, coords, grid_len):
    angle = (np.outer(freqs, coords) % grid_len) * (2.0 * math.pi / grid_len)
    return np.cos(angle), np.sin(angle)


def plane_tables(grid_len):
    freqs = np.arange(KXY) - KXY // 2
    cos, sin = trig(freqs, np.arange(grid_len), grid_len)
    groups = KXY // GROUP
    scale = float(grid_len) ** -1.5
    x_down = np.zeros((GROUP, 2, groups, grid_len))
    x_up = np.zeros((grid_len, GROUP, 2, groups))
    y_down = np.zeros((GROUP, 2, grid_len, 2, GROUP, KXY))
    y_up = np.zeros((2, GROUP, KXY, GROUP, 2, grid_len))
    for k in range(GROUP):
        for g in range(groups):
            jx = g * GROUP + k
            x_down[k, 0, g], x_down[k, 1, g] = cos[jx], sin[jx]
            x_up[:, k, 0, g], x_up[:, k, 1, g] = scale * cos[jx], -scale * sin[jx]
        y_down[k, 0, :, 0, k], y_down[k, 1, :, 0, k] = cos.T, -sin.T
        y_down[k, 0, :, 1, k], y_down[k, 1, :, 1, k] = -sin.T, -cos.T
        y_up[0, k, :, k, 0], y_up[1, k, :, k, 0] = cos, -sin
        y_up[0, k, :, k, 1], y_up[1, k, :, k, 1] = sin, cos
    rows = 2 * KXY
    return (
        bf16_table(x_down.reshape(rows, grid_len)),
        bf16_table(x_up.reshape(grid_len, rows)),
        bf16_table(y_down.reshape(2 * GROUP * grid_len, 2 * LANES)),
        bf16_table(y_up.reshape(2 * LANES, 2 * GROUP * grid_len)),
    )


def depth_tables(channels, planes, slabs, grid_len):
    scale = float(grid_len) ** -1.5
    down, up = [], []
    eye = np.eye(channels)
    for s in range(slabs):
        cos, sin = trig(np.arange(KZ), s * planes + np.arange(planes), grid_len)
        parts = [[cos, sin], [-sin, cos]]
        full = np.zeros((2, channels, KZ, 2, channels, planes))
        for q in range(2):
            for r in range(2):
                full[q, :, :, r] = np.einsum("cd,mz->cmdz", eye, parts[q][r])
        full = full.reshape(2 * channels * KZ, 2 * channels * planes)
        for store, table in ((down, full * scale), (up, full.T)):
            high = bf16_table(table)
            low = bf16_table(table - high.astype(np.float64))
            store.append(np.concatenate([high, low], axis=1))
    return np.stack(down), np.stack(up)


def dot(a, b):
    return jnp.dot(a, b, preferred_element_type=F32)


def dot_nt(a, b):
    return lax.dot_general(a, b, (((1,), (1,)), ((), ())), preferred_element_type=F32)


def twice(block):
    return jnp.concatenate([block, block], axis=0)


def tile_rows(plane):
    groups = KXY // GROUP
    return pl.ds(pl.multiple_of(plane * groups, groups), groups)


def keep_x_rows(xs_ref, plane, value):
    groups = KXY // GROUP
    tiles = value.shape[1] // LANES
    for kp in range(2 * GROUP):
        for h in range(tiles):
            xs_ref[kp * tiles + h, tile_rows(plane), :] = value[kp * groups : (kp + 1) * groups, h * LANES : (h + 1) * LANES]


def plane_rows(ws_ref, plane, width):
    tiles = width // LANES
    columns = []
    for h in range(tiles):
        parts = [ws_ref[kp * tiles + h, tile_rows(plane), :] for kp in range(2 * GROUP)]
        columns.append(jnp.concatenate(parts, axis=0))
    return jnp.concatenate(columns, axis=1)


def y_pass(xs_ref, y_down_ref):
    lhs = jnp.concatenate([xs_ref[j].astype(BF) for j in range(xs_ref.shape[0])], axis=1)
    return dot(lhs, y_down_ref[...])


def local_spectra(xs_ref, y_down_ref, z_down, zt_ref, sp_ref, shared_ref=None):
    groups = KXY // GROUP
    rows = xs_ref.shape[1]
    planes_all = rows // groups
    spectra = y_pass(xs_ref, y_down_ref)
    for q in range(2):
        sp_ref[q, :rows, :] = spectra[:, q * LANES : (q + 1) * LANES]
    if shared_ref is not None:
        more = shared_ref.shape[1]
        planes = more // groups
        shared = y_pass(shared_ref, y_down_ref)
        for q in range(2):
            sp_ref[q, rows : rows + more, :] = shared[:, q * LANES : (q + 1) * LANES]
    for g in range(groups):
        for q in range(2):
            part = sp_ref[q, pl.ds(g, planes_all, stride=groups), :]
            if shared_ref is not None:
                common = sp_ref[q, pl.ds(rows + g, planes, stride=groups), :]
                part = part + jnp.concatenate([common] * (planes_all // planes), axis=0)
            zt_ref[q * planes_all : (q + 1) * planes_all, g * LANES : (g + 1) * LANES] = part.astype(BF)
    return dot(z_down, twice(zt_ref[...])).astype(BF)


def pack_columns(coeffs, slot_row):
    column = lax.broadcasted_iota(jnp.int32, (coeffs.shape[1], slot_row.shape[1]), 0)
    return dot(coeffs, (column == slot_row).astype(F32).astype(BF)).astype(BF)


def analysis_tail(xs_ref, y_down_ref, z_down_ref, slot_ref, zt_ref, sp_ref, packed_ref):
    coeffs = local_spectra(xs_ref, y_down_ref, z_down_ref[0], zt_ref, sp_ref)
    capacity = packed_ref.shape[2]
    chunk = 2 * capacity
    for n in range(slot_ref.shape[1] // chunk):
        part = pack_columns(coeffs, slot_ref[0:1, n * chunk : (n + 1) * chunk])
        packed_ref[2 * n] = part[:, :capacity]
        packed_ref[2 * n + 1] = part[:, capacity:]


def synthesis_head(recv_ref, slot_ref, z_up_ref, y_up_ref, sp_ref, ws_ref):
    groups = KXY // GROUP
    rows = ws_ref.shape[1]
    planes_all = rows // groups
    slabs = recv_ref.shape[0]
    by_slot = jnp.concatenate([recv_ref[s] for s in range(slabs)], axis=1)
    slots = by_slot.shape[1]
    chunk = 2 * LANES
    column = lax.broadcasted_iota(jnp.int32, (chunk, slots), 0)
    for n in range(KXY * KXY // chunk):
        pick = (column + n * chunk == slot_ref[0:1, :]).astype(F32).astype(BF)
        spectra = dot_nt(by_slot, pick).astype(BF)
        planes = dot(z_up_ref[0], twice(spectra))
        for gg in range(2):
            for q in range(2):
                sp_ref[q, pl.ds(2 * n + gg, planes_all, stride=groups), :] = planes[
                    q * planes_all : (q + 1) * planes_all, gg * LANES : (gg + 1) * LANES
                ]
    lhs = jnp.concatenate([sp_ref[q, :rows, :].astype(BF) for q in range(2)], axis=1)
    for j in range(ws_ref.shape[0] // 2):
        wide = dot(lhs, y_up_ref[:, j * chunk : (j + 1) * chunk])
        ws_ref[2 * j] = wide[:, :LANES]
        ws_ref[2 * j + 1] = wide[:, LANES:]


def gelu_pair(half):
    coeff = math.sqrt(2.0 / math.pi)
    square = half * half
    tangent = jnp.tanh(half * (2.0 * coeff + (8.0 * 0.044715 * coeff) * square))
    turned = half * tangent
    value = half + turned
    inner = 0.5 + (half - turned) * (coeff + (12.0 * 0.044715 * coeff) * square)
    return value, (value * (1.0 + tangent)) * inner


class Planes:
    def __init__(self, step, per_step, channels, planes):
        self.step, self.per_step, self.count = step, per_step, per_step * channels
        self.planes, self.planes_all = planes, planes * channels

    def place(self, t):
        c = t // self.per_step
        zz = t - c * self.per_step
        return c, zz, c * self.planes + self.step * self.per_step + zz


def middle_kernel(per_step, rows, slab_ref, gain_ref, bias_ref, merged_ref, recv_ref, slot_ref, x_down_ref, x_up_ref, y_down_ref, y_up_ref, z_down_ref, z_up_ref, out_ref, grad_ref, packed_ref, xs_ref, ws_ref, zt_ref, sp_ref, sa_ref, sb_ref, ga_ref, gb_ref):
    step = pl.program_id(0)
    channels, _, grid_len, _ = merged_ref.shape
    at = Planes(step, per_step, channels, xs_ref.shape[1] * GROUP // KXY // channels)

    @pl.when(step == 0)
    def _():
        synthesis_head(recv_ref, slot_ref, z_up_ref, y_up_ref, sp_ref, ws_ref)

    def synth(t, s_ref):
        c, _, plane = at.place(t)
        shift = jnp.full((BIAS_ROWS, grid_len), 0.5 * bias_ref[c], F32)
        high = shift.astype(BF).astype(F32)
        row = lax.broadcasted_iota(jnp.int32, shift.shape, 0)
        shift = jnp.where(row == 0, high, jnp.where(row == 1, shift - high, 0.0))
        s_ref[...] = dot(x_up_ref[...], jnp.concatenate([plane_rows(ws_ref, plane, grid_len), shift], axis=0).astype(BF))

    def point(t, s_ref, g_ref):
        c, zz, _ = at.place(t)
        zz_all = step * per_step + zz
        gain = 0.5 * gain_ref[c]
        for start in range(0, grid_len, rows):
            span = slice(start, start + rows)
            merged = merged_ref[c, zz_all, span, :]
            value, grad = gelu_pair(s_ref[span, :] + gain * merged.astype(F32))
            grad = grad.astype(BF)
            out_ref[c, zz, span, :] = value.astype(BF)
            grad_ref[c, zz_all, span, :] = grad
            g_ref[span, :] = grad

    def down(t, g_ref):
        keep_x_rows(xs_ref, at.place(t)[2], dot(x_down_ref[...], g_ref[...]))

    synth(0, sa_ref)

    def body(j, carry):
        t = 2 * j
        synth(t + 1, sb_ref)
        down(jnp.maximum(t - 1, 0), gb_ref)
        point(t, sa_ref, ga_ref)
        synth(jnp.minimum(t + 2, at.count - 1), sa_ref)
        down(t, ga_ref)
        point(t + 1, sb_ref, gb_ref)
        return carry

    lax.fori_loop(0, at.count // 2, body, 0)
    down(at.count - 1, gb_ref)

    @pl.when(step == pl.num_programs(0) - 1)
    def _():
        analysis_tail(xs_ref, y_down_ref, z_down_ref, slot_ref, zt_ref, sp_ref, packed_ref)


def final_kernel(per_step, rows, slab_ref, gain_ref, grad_ref, recv_ref, slot_ref, x_up_ref, y_up_ref, z_up_ref, out_ref, ws_ref, sp_ref):
    step = pl.program_id(0)
    channels, _, grid_len, _ = grad_ref.shape
    at = Planes(step, per_step, channels, ws_ref.shape[1] * GROUP // KXY // channels)

    @pl.when(step == 0)
    def _():
        synthesis_head(recv_ref, slot_ref, z_up_ref, y_up_ref, sp_ref, ws_ref)

    def body(zz, carry):
        for c in range(channels):
            wp = plane_rows(ws_ref, c * at.planes + step * per_step + zz, grid_len).astype(BF)
            out_ref[c, zz] = (dot(x_up_ref[...], wp) + gain_ref[c] * grad_ref[c, step * per_step + zz].astype(F32)).astype(BF)
        return carry

    lax.fori_loop(0, per_step, body, 0)


def entry_barrier(targets):
    barrier = pltpu.get_barrier_semaphore()
    for target in targets:
        pl.semaphore_signal(barrier, inc=1, device_id=target, device_id_type=MESH)
    pl.semaphore_wait(barrier, len(targets))


def spread(block, start, width):
    slots = block.shape[1]
    lane = lax.broadcasted_iota(jnp.int32, (slots, width), 1) + start
    row = lax.broadcasted_iota(jnp.int32, (slots, width), 0)
    expand = (lane // KZ == row).astype(F32).astype(BF)
    high = block.astype(BF)
    low = (block - high.astype(F32)).astype(BF)
    wide = dot(high, expand) + dot(low, expand)
    pairs = wide.shape[0] // KZ
    wide = wide.reshape(pairs, KZ, width)
    m_row = lax.broadcasted_iota(jnp.int32, wide.shape, 1)
    m_lane = lax.broadcasted_iota(jnp.int32, wide.shape, 2) % KZ
    return jnp.sum(jnp.where(m_row == m_lane, wide, 0.0), axis=1)


def unspread(pairs, start, slots):
    count, width = pairs.shape
    shape = (count, KZ, width)
    m_row = lax.broadcasted_iota(jnp.int32, shape, 1)
    m_lane = lax.broadcasted_iota(jnp.int32, shape, 2) % KZ
    wide = jnp.where(m_row == m_lane, jnp.broadcast_to(pairs[:, None, :], shape), 0.0)
    wide = wide.reshape(count * KZ, width).astype(BF)
    lane = lax.broadcasted_iota(jnp.int32, (slots, width), 1) + start
    row = lax.broadcasted_iota(jnp.int32, (slots, width), 0)
    collect = (lane // KZ == row).astype(F32).astype(BF)
    return dot_nt(wide, collect)


def peers_of(slabs, groups):
    slab, chan = lax.axis_index("slab"), lax.axis_index("chan")
    slab_peer = [(lax.rem(slab + d, slabs), chan) for d in range(1, slabs)]
    chan_peer = [(slab, lax.rem(chan + d, groups)) for d in range(1, groups)]
    return slab, chan, slab_peer, chan_peer


def spectra_copy(packed_ref, rx, peer, d, s_send, s_recv):
    return pltpu.make_async_remote_copy(
        src_ref=packed_ref.at[peer[0]], dst_ref=rx.at[d - 1], send_sem=s_send.at[d - 1], recv_sem=s_recv.at[d - 1],
        device_id=peer, device_id_type=MESH,
    )


def mix_kernel(slabs, groups, forward, packed_ref, w_ref, recv_ref, rx, tx2, rx2, mine, *sems):
    _, _, slab_peer, chan_peer = peers_of(slabs, groups)
    entry_barrier(slab_peer + chan_peer)
    first = [spectra_copy(packed_ref, rx, slab_peer[d - 1], d, *sems[:2]) for d in range(1, slabs)]
    for copy in first:
        copy.start()
    exchange_body(slabs, groups, forward, first, packed_ref, w_ref, recv_ref, rx, tx2, rx2, mine, *sems)


def exchange_body(slabs, groups, forward, first, packed_ref, w_ref, recv_ref, rx, tx2, rx2, mine, s_send, s_recv, c_send, c_recv, g_send, g_recv):
    slab, chan, slab_peer, chan_peer = peers_of(slabs, groups)
    total = packed_ref[slab].astype(F32)
    for d in range(1, slabs):
        first[d - 1].wait_recv()
        total = total + rx[d - 1].astype(F32)
    slots = total.shape[1]
    wide = slots * KZ
    chunk = 512
    own = rx2.shape[1] // 2
    outputs = own * groups
    if forward:
        for start in range(0, wide, chunk):
            at = slice(start, start + chunk)
            u = spread(total, start, chunk)
            real = jnp.zeros((outputs, chunk), F32)
            imag = jnp.zeros((outputs, chunk), F32)
            for c in range(own):
                w0, w1 = w_ref[0, c, :, at].astype(F32), w_ref[1, c, :, at].astype(F32)
                ur, ui = u[c : c + 1], u[own + c : own + c + 1]
                real = real + (w0 * ur - w1 * ui)
                imag = imag + (w1 * ur + w0 * ui)
            for e in range(groups):
                rows = slice(e * own, (e + 1) * own)
                tx2[e, :, at] = jnp.concatenate([real[rows], imag[rows]], axis=0).astype(BF)
    else:
        for start in range(0, wide, chunk):
            at = slice(start, start + chunk)
            lane = lax.broadcasted_iota(jnp.int32, (2 * own, chunk), 1)
            double = jnp.where(lane % KZ == 0, 1.0, 2.0)
            tx2[0, :, at] = (spread(total, start, chunk) * double).astype(BF)
    second = []
    for d in range(1, groups):
        peer = chan_peer[d - 1]
        copy = pltpu.make_async_remote_copy(
            src_ref=tx2.at[peer[1]] if forward else tx2.at[0], dst_ref=rx2.at[chan], send_sem=c_send.at[d - 1], recv_sem=c_recv.at[d - 1],
            device_id=peer, device_id_type=MESH,
        )
        copy.start()
        second.append(copy)
    rx2[chan] = tx2[chan] if forward else tx2[0]
    for copy in second:
        copy.wait_recv()
    result = jnp.zeros((2 * own * KZ, slots), F32)
    for start in range(0, wide, chunk):
        at = slice(start, start + chunk)
        if forward:
            pairs = rx2[0, :, at].astype(F32)
            for e in range(1, groups):
                pairs = pairs + rx2[e, :, at].astype(F32)
            lane = lax.broadcasted_iota(jnp.int32, (2 * own, chunk), 1)
            pairs = pairs * jnp.where(lane % KZ == 0, 1.0, 2.0)
        else:
            blocks = [rx2[e, :, at].astype(F32) for e in range(groups)]
            real = jnp.concatenate([b[:own] for b in blocks], axis=0)
            imag = jnp.concatenate([b[own:] for b in blocks], axis=0)
            reals, imags = [], []
            for c in range(own):
                w0, w1 = w_ref[0, c, :, at].astype(F32), w_ref[1, c, :, at].astype(F32)
                reals.append(jnp.sum(w0 * real + w1 * imag, axis=0, keepdims=True))
                imags.append(jnp.sum(w0 * imag - w1 * real, axis=0, keepdims=True))
            pairs = jnp.concatenate(reals + imags, axis=0)
        result = result + unspread(pairs, start, slots)
    mine[...] = result.astype(BF)
    third = []
    for d in range(1, slabs):
        copy = pltpu.make_async_remote_copy(
            src_ref=mine, dst_ref=recv_ref.at[slab], send_sem=g_send.at[d - 1], recv_sem=g_recv.at[d - 1],
            device_id=slab_peer[d - 1], device_id_type=MESH,
        )
        copy.start()
        third.append(copy)
    recv_ref[slab] = mine[...]
    for copy in third:
        copy.wait_recv()
    for copy in first + second + third:
        copy.wait_send()


def front_kernel(slabs, groups, field_hbm, forcing_hbm, slots_hbm, w_hbm, x_down_hbm, y_down_hbm, z_down_hbm, recv_ref, merged_ref,
                 plane_ref, xs_ref, xf_ref, zt_ref, sp_ref, packed_ref, rx, tx2, rx2, mine, slot_ref, w_ref, x_down_ref, y_down_ref, z_down_ref,
                 in_sem, field_sem, x_send, x_recv, p_send, p_recv, *sems):
    slab, chan, slab_peer, chan_peer = peers_of(slabs, groups)
    channels, planes = merged_ref.shape[:2]
    height = forcing_hbm.shape[1]
    chips = groups // 2
    chip, core = chan // 2, lax.rem(chan, 2)
    partner = (slab, chan + 1 - 2 * core)

    def near(t):
        return 2 * lax.rem(chip + chips + t, chips) + core

    def rows(index, start, count):
        return plane_ref.at[pl.ds(start, count), pl.ds(pl.multiple_of(index * height, height), height), :]

    fields = [pltpu.make_async_copy(field_hbm.at[c], merged_ref.at[c], field_sem.at[c]) for c in range(channels)]
    loads = [
        pltpu.make_async_copy(x_down_hbm, x_down_ref, in_sem.at[0]),
        pltpu.make_async_copy(y_down_hbm, y_down_ref, in_sem.at[1]),
        pltpu.make_async_copy(z_down_hbm.at[slab], z_down_ref, in_sem.at[2]),
        pltpu.make_async_copy(slots_hbm, slot_ref, in_sem.at[3]),
        pltpu.make_async_copy(w_hbm, w_ref, in_sem.at[4]),
        pltpu.make_async_copy(forcing_hbm, rows(chan, 0, planes), in_sem.at[5]),
    ]
    loads[0].start()
    for copy in fields + loads[1:]:
        copy.start()
    entry_barrier(slab_peer + chan_peer)

    half = planes // 2

    def across(index, start, to, n, source=None):
        return pltpu.make_async_remote_copy(
            src_ref=rows(index, start, half) if source is None else source, dst_ref=rows(index, start, half),
            send_sem=x_send.at[n], recv_sem=x_recv.at[n], device_id=(slab, to), device_id_type=MESH,
        )

    def beside(index, start, count, n, source=None):
        return pltpu.make_async_remote_copy(
            src_ref=rows(index, start, count) if source is None else source, dst_ref=rows(index, start, count),
            send_sem=p_send.at[n], recv_sem=p_recv.at[n], device_id=partner, device_id_type=MESH,
        )

    low, high = forcing_hbm.at[pl.ds(0, half)], forcing_hbm.at[pl.ds(half, half)]
    right_low = across(chan, 0, near(1), 0, low)
    left_high = across(chan, half, near(-1), 1, high)
    right_high = across(chan, half, near(1), 2, high)
    left_low = across(chan, 0, near(-1), 3, low)
    for copy in (right_low, left_high, right_high, left_low):
        copy.start()
    own = beside(chan, 0, planes, 0, forcing_hbm)
    own.start()
    sent = [right_low, left_high, right_high, left_low, own]
    beside_all = [own]

    def pass_on(copies):
        for copy in copies:
            copy.start()
            sent.append(copy)

    def x_pass(c):
        fields[c].wait()

        def body(zz, carry):
            keep_x_rows(xs_ref, c * planes + zz, dot(x_down_ref[...], merged_ref[c, zz]))
            return carry

        lax.fori_loop(0, planes, body, 0, unroll=4)

    loads[0].wait()
    x_pass(0)
    right_low.wait_recv()
    left_high.wait_recv()
    far_low = across(near(-1), 0, near(1), 4)
    far_high = across(near(1), half, near(-1), 5)
    more = [beside(near(-1), 0, half, 1), beside(near(1), half, half, 2)]
    beside_all += more
    pass_on([far_low, far_high] + more)
    x_pass(1)
    right_high.wait_recv()
    left_low.wait_recv()
    more = [beside(near(-1), half, half, 3), beside(near(1), 0, half, 4)]
    beside_all += more
    pass_on(more)
    for c in range(2, channels):
        x_pass(c)
    far_low.wait_recv()
    far_high.wait_recv()
    more = [beside(near(2), 0, half, 5), beside(near(2), half, half, 6)]
    beside_all += more
    pass_on(more)
    loads[5].wait()
    for copy in beside_all:
        copy.wait_recv()

    def forcing_body(zz, carry):
        keep_x_rows(xf_ref, zz, dot(x_down_ref[...], plane_ref[zz]))
        return carry

    lax.fori_loop(0, planes, forcing_body, 0, unroll=4)
    for copy in loads[1:4]:
        copy.wait()
    coeffs = local_spectra(xs_ref, y_down_ref, z_down_ref[...], zt_ref, sp_ref, xf_ref)
    capacity = packed_ref.shape[2]
    first = []
    for d in range(1, slabs, 2):
        targets = [lax.rem(slab + d, slabs), lax.rem(slab + d + 1, slabs)]
        part = pack_columns(coeffs, jnp.concatenate([slot_ref[pl.ds(t, 1), :] for t in targets], axis=1))
        for n, t in enumerate(targets):
            packed_ref[t] = part[:, n * capacity : (n + 1) * capacity]
            if d + n < slabs:
                copy = spectra_copy(packed_ref, rx, slab_peer[d + n - 1], d + n, *sems[:2])
                copy.start()
                first.append(copy)

    def merge_body(zz, carry):
        for c in range(channels):
            merged_ref[c, zz] = merged_ref[c, zz] + plane_ref[zz]
        return carry

    lax.fori_loop(0, planes, merge_body, 0)
    loads[4].wait()
    exchange_body(slabs, groups, True, first, packed_ref, w_ref, recv_ref, rx, tx2, rx2, mine, *sems)
    for copy in sent:
        copy.wait_send()


def whole(shape):
    zeros = (0,) * len(shape)
    return pl.BlockSpec(shape, lambda *_: zeros, pipeline_mode=pl.Buffered(1))


class Sizes:
    def __init__(self, slabs, groups, channels, planes, grid_len, capacity):
        self.slabs, self.groups = slabs, groups
        self.channels, self.planes, self.grid_len = channels, planes, grid_len
        self.capacity = capacity
        planes_all = channels * planes
        x_down, x_up, y_down, y_up = plane_tables(grid_len)
        ones = np.zeros((grid_len, BIAS_ROWS), x_up.dtype)
        ones[:, :2] = 1
        half = bf16_table(0.5 * x_up.astype(np.float32))
        self.x_down, self.x_up, self.y_down, self.y_up = [jnp.asarray(t) for t in (x_down, x_up, y_down, y_up)]
        self.x_up_half = jnp.asarray(np.concatenate([half, ones], axis=1))
        self.z_down, self.z_up = [jnp.asarray(t) for t in depth_tables(channels, planes, slabs, grid_len)]
        self.per_step = 4
        per_step = self.per_step
        self.steps = planes // per_step
        self.field_spec = pl.BlockSpec((channels, per_step, grid_len, grid_len), lambda i, s: (0, i, 0, 0))
        self.plane_spec = pl.BlockSpec((per_step, grid_len, grid_len), lambda i, s: (i, 0, 0))
        self.z_spec = pl.BlockSpec((1,) + self.z_down.shape[1:], lambda i, s: (s[0], 0, 0), pipeline_mode=pl.Buffered(1))
        self.packed_shape = (slabs, 2 * channels * KZ, capacity)
        self.volume = jax.ShapeDtypeStruct((channels, planes, grid_len, grid_len), BF)
        self.packed_out = jax.ShapeDtypeStruct(self.packed_shape, BF)
        self.wide_scratch = pltpu.VMEM((2 * GROUP * grid_len // LANES, planes_all * KXY // GROUP, LANES), F32)
        self.sp_scratch = pltpu.VMEM((2, (planes_all + planes) * KXY // GROUP, LANES), F32)
        self.zt_scratch = pltpu.VMEM((2 * planes_all, KXY * KXY), BF)
        self.params = pltpu.CompilerParams(dimension_semantics=("arbitrary",), vmem_limit_bytes=30 << 20)


SMEM = pl.BlockSpec(memory_space=pltpu.SMEM)
VMEM = pl.BlockSpec(memory_space=pltpu.VMEM)
HBM = pl.BlockSpec(memory_space=pltpu.HBM)


def front_call(z, field, forcing, slot_column, w_spec):
    block = z.packed_shape[1:]
    pair = (z.groups, 2 * z.channels, z.capacity * KZ)
    tiles = 2 * GROUP * z.grid_len // LANES
    dma = pltpu.SemaphoreType.DMA
    return pl.pallas_call(
        functools.partial(front_kernel, z.slabs, z.groups),
        out_shape=(z.packed_out, z.volume),
        in_specs=[HBM] * 7,
        out_specs=(VMEM, VMEM),
        scratch_shapes=[
            pltpu.VMEM((z.planes, z.grid_len, z.grid_len), BF),
            z.wide_scratch,
            pltpu.VMEM((tiles, z.planes * KXY // GROUP, LANES), F32),
            z.zt_scratch,
            z.sp_scratch,
            pltpu.VMEM(z.packed_shape, BF),
            pltpu.VMEM((z.slabs - 1,) + block, BF),
            pltpu.VMEM(pair, BF),
            pltpu.VMEM(pair, BF),
            pltpu.VMEM(block, BF),
            pltpu.VMEM(slot_column.shape, jnp.int32),
            pltpu.VMEM(w_spec.shape, BF),
            pltpu.VMEM(z.x_down.shape, BF),
            pltpu.VMEM(z.y_down.shape, BF),
            pltpu.VMEM(z.z_down.shape[1:], BF),
            dma((6,)), dma((z.channels,)), dma((6,)), dma((6,)), dma((7,)), dma((7,)),
        ]
        + [dma((z.slabs - 1,))] * 2 + [dma((z.groups - 1,))] * 2 + [dma((z.slabs - 1,))] * 2,
        compiler_params=pltpu.CompilerParams(collective_id=1, has_side_effects=True, vmem_limit_bytes=26 << 20),
        name="gather_analyse_mix",
    )(*[pltpu.with_memory_space_constraint(v, pltpu.HBM) for v in (field, forcing, slot_column, w_spec, z.x_down, z.y_down, z.z_down)])


def exchange_call(z, values, w_spec):
    block = z.packed_shape[1:]
    pair = (z.groups, 2 * z.channels, z.capacity * KZ)
    return pl.pallas_call(
        functools.partial(mix_kernel, z.slabs, z.groups, False),
        out_shape=z.packed_out,
        in_specs=[VMEM, VMEM],
        out_specs=VMEM,
        scratch_shapes=[
            pltpu.VMEM((z.slabs - 1,) + block, BF),
            pltpu.VMEM(pair, BF),
            pltpu.VMEM(pair, BF),
            pltpu.VMEM(block, BF),
        ]
        + [pltpu.SemaphoreType.DMA((z.slabs - 1,))] * 2
        + [pltpu.SemaphoreType.DMA((z.groups - 1,))] * 2
        + [pltpu.SemaphoreType.DMA((z.slabs - 1,))] * 2,
        compiler_params=pltpu.CompilerParams(collective_id=2, has_side_effects=True, vmem_limit_bytes=8 << 20),
        name="mix_adjoint",
    )(values, w_spec)


def middle_call(z, where, skip_gain, bias, merged, spectra, slots):
    return pl.pallas_call(
        functools.partial(middle_kernel, z.per_step, 64),
        out_shape=(z.volume, z.volume, z.packed_out),
        grid_spec=pltpu.PrefetchScalarGridSpec(
            num_scalar_prefetch=1, grid=(z.steps,),
            in_specs=[SMEM, SMEM, VMEM, VMEM, whole(slots.shape), whole(z.x_down.shape), whole(z.x_up_half.shape), whole(z.y_down.shape), whole(z.y_up.shape), z.z_spec, z.z_spec],
            out_specs=(z.field_spec, VMEM, VMEM),
            scratch_shapes=[z.wide_scratch, z.wide_scratch, z.zt_scratch, z.sp_scratch] + [pltpu.VMEM((z.grid_len, z.grid_len), F32)] * 2 + [pltpu.VMEM((z.grid_len, z.grid_len), BF)] * 2,
        ),
        compiler_params=z.params,
        name="synth_gelu_analyse",
    )(where, skip_gain, bias, merged, spectra, slots, z.x_down, z.x_up_half, z.y_down, z.y_up, z.z_down, z.z_up)


def final_call(z, where, skip_gain, grad_pre, adjoint, slots):
    return pl.pallas_call(
        functools.partial(final_kernel, z.per_step, 64),
        out_shape=z.volume,
        grid_spec=pltpu.PrefetchScalarGridSpec(
            num_scalar_prefetch=1, grid=(z.steps,),
            in_specs=[SMEM, VMEM, VMEM, whole(slots.shape), whole(z.x_up.shape), whole(z.y_up.shape), z.z_spec],
            out_specs=z.field_spec,
            scratch_shapes=[z.wide_scratch, z.sp_scratch],
        ),
        compiler_params=z.params,
        name="synth_gradient",
    )(where, skip_gain, grad_pre, adjoint, slots, z.x_up, z.y_up, z.z_up)


def per_device(slabs, groups, field, forcing, slot_column, w_spec, skip_gain, bias):
    channels, planes, grid_len, _ = field.shape
    capacity = slot_column.shape[1]
    z = Sizes(slabs, groups, channels, planes, grid_len, capacity)
    slots = slot_column.reshape(1, slabs * capacity)
    where = lax.axis_index("slab").astype(jnp.int32).reshape(1)
    spectra, merged = front_call(z, field, forcing, slot_column, w_spec)
    output, grad_pre, packed_back = middle_call(z, where, skip_gain, bias, merged, spectra, slots)
    adjoint = exchange_call(z, packed_back, w_spec)
    gradient = final_call(z, where, skip_gain, grad_pre, adjoint, slots)
    return (output, gradient)


def solution(mesh):
    placed = (
        P("chan", "slab", None, None),
        P("slab", "chan", None),
        P(),
        P(None, "chan", None, "slab"),
        P("chan"),
        P("chan"),
    )
    slabs, groups = mesh.shape["slab"], mesh.shape["chan"]
    return jax.shard_map(
        functools.partial(per_device, slabs, groups),
        mesh=mesh,
        in_specs=placed,
        out_specs=(P("chan", "slab", None, None), P("chan", "slab", None, None)),
        check_vma=False,
    )
```

```python
import functools
import math

import jax
import jax.numpy as jnp
import ml_dtypes
import numpy as np
from jax import lax
from jax.experimental import pallas as pl
from jax.experimental.pallas import tpu as pltpu
from jax.sharding import PartitionSpec as P

KXY = 32
KZ = 16
MESH = pl.DeviceIdType.MESH
BF = jnp.bfloat16
F32 = jnp.float32
LANES = 128
PIECES = 2
BIAS_ROWS = 16
GROUP = LANES // KXY


def bf16_table(values):
    return np.asarray(values, np.float32).astype(ml_dtypes.bfloat16)


def trig(freqs, coords, grid_len):
    angle = (np.outer(freqs, coords) % grid_len) * (2.0 * math.pi / grid_len)
    return np.cos(angle), np.sin(angle)


def plane_tables(grid_len):
    freqs = np.arange(KXY) - KXY // 2
    cos, sin = trig(freqs, np.arange(grid_len), grid_len)
    groups = KXY // GROUP
    scale = float(grid_len) ** -1.5
    x_down = np.zeros((GROUP, 2, groups, grid_len))
    x_up = np.zeros((grid_len, GROUP, 2, groups))
    y_down = np.zeros((GROUP, 2, grid_len, 2, GROUP, KXY))
    y_up = np.zeros((2, GROUP, KXY, GROUP, 2, grid_len))
    for k in range(GROUP):
        for g in range(groups):
            jx = g * GROUP + k
            x_down[k, 0, g], x_down[k, 1, g] = cos[jx], sin[jx]
            x_up[:, k, 0, g], x_up[:, k, 1, g] = scale * cos[jx], -scale * sin[jx]
        y_down[k, 0, :, 0, k], y_down[k, 1, :, 0, k] = cos.T, -sin.T
        y_down[k, 0, :, 1, k], y_down[k, 1, :, 1, k] = -sin.T, -cos.T
        y_up[0, k, :, k, 0], y_up[1, k, :, k, 0] = cos, -sin
        y_up[0, k, :, k, 1], y_up[1, k, :, k, 1] = sin, cos
    rows = 2 * KXY
    return (
        bf16_table(x_down.reshape(rows, grid_len)),
        bf16_table(x_up.reshape(grid_len, rows)),
        bf16_table(y_down.reshape(2 * GROUP * grid_len, 2 * LANES)),
        bf16_table(y_up.reshape(2 * LANES, 2 * GROUP * grid_len)),
    )


def depth_tables(channels, planes, slabs, grid_len):
    scale = float(grid_len) ** -1.5
    down, up = [], []
    eye = np.eye(channels)
    for s in range(slabs):
        cos, sin = trig(np.arange(KZ), s * planes + np.arange(planes), grid_len)
        parts = [[cos, sin], [-sin, cos]]
        full = np.zeros((2, channels, KZ, 2, channels, planes))
        for q in range(2):
            for r in range(2):
                full[q, :, :, r] = np.einsum("cd,mz->cmdz", eye, parts[q][r])
        full = full.reshape(2, channels, PIECES, KZ // PIECES, -1).transpose(2, 0, 1, 3, 4)
        full = full.reshape(2 * channels * KZ, 2 * channels * planes)
        for store, table in ((down, full * scale), (up, full.T)):
            high = bf16_table(table)
            low = bf16_table(table - high.astype(np.float64))
            store.append(np.concatenate([high, low], axis=1))
    return np.stack(down), np.stack(up)


def dot(a, b):
    return jnp.dot(a, b, preferred_element_type=F32)


def dot_nt(a, b):
    return lax.dot_general(a, b, (((1,), (1,)), ((), ())), preferred_element_type=F32)


def twice(block):
    return jnp.concatenate([block, block], axis=0)


def tile_rows(plane):
    groups = KXY // GROUP
    return pl.ds(pl.multiple_of(plane * groups, groups), groups)


def keep_x_rows(xs_ref, plane, value):
    groups = KXY // GROUP
    tiles = value.shape[1] // LANES
    for kp in range(2 * GROUP):
        for h in range(tiles):
            xs_ref[kp * tiles + h, tile_rows(plane), :] = value[kp * groups : (kp + 1) * groups, h * LANES : (h + 1) * LANES]


def plane_rows(ws_ref, plane, width):
    tiles = width // LANES
    columns = []
    for h in range(tiles):
        parts = [ws_ref[kp * tiles + h, tile_rows(plane), :] for kp in range(2 * GROUP)]
        columns.append(jnp.concatenate(parts, axis=0))
    return jnp.concatenate(columns, axis=1)


def y_pass(xs_ref, y_down_ref):
    lhs = jnp.concatenate([xs_ref[j].astype(BF) for j in range(xs_ref.shape[0])], axis=1)
    return dot(lhs, y_down_ref[...])


def local_spectra(xs_ref, y_down_ref, z_down, zt_ref, sp_ref):
    groups = KXY // GROUP
    rows = xs_ref.shape[1]
    count = rows // groups
    half = zt_ref.shape[0] // 2
    spectra = y_pass(xs_ref, y_down_ref)
    for q in range(2):
        sp_ref[q, :rows, :] = spectra[:, q * LANES : (q + 1) * LANES]
    if count < half:
        zt_ref[...] = jnp.zeros_like(zt_ref)
    for g in range(groups):
        for q in range(2):
            part = sp_ref[q, pl.ds(g, count, stride=groups), :]
            zt_ref[q * half : q * half + count, g * LANES : (g + 1) * LANES] = part.astype(BF)
    return dot(z_down, twice(zt_ref[...]))


def pick_columns(columns, slot_row):
    column = lax.broadcasted_iota(jnp.int32, (columns, slot_row.shape[1]), 0)
    return (column == slot_row).astype(F32).astype(BF)


def analysis_tail(xs_ref, y_down_ref, z_down_ref, slot_ref, zt_ref, sp_ref, packed_ref):
    coeffs = local_spectra(xs_ref, y_down_ref, z_down_ref[0], zt_ref, sp_ref).astype(BF)
    capacity = packed_ref.shape[2]
    chunk = 2 * capacity
    for n in range(slot_ref.shape[1] // chunk):
        part = dot(coeffs, pick_columns(coeffs.shape[1], slot_ref[0:1, n * chunk : (n + 1) * chunk])).astype(BF)
        packed_ref[2 * n] = part[:, :capacity]
        packed_ref[2 * n + 1] = part[:, capacity:]


def synthesis_head(recv_ref, slot_ref, z_up_ref, y_up_ref, sp_ref, ws_ref):
    groups = KXY // GROUP
    rows = ws_ref.shape[1]
    planes_all = rows // groups
    slabs = recv_ref.shape[0]
    by_slot = jnp.concatenate([recv_ref[s] for s in range(slabs)], axis=1)
    slots = by_slot.shape[1]
    chunk = 2 * LANES
    column = lax.broadcasted_iota(jnp.int32, (chunk, slots), 0)
    for n in range(KXY * KXY // chunk):
        pick = (column + n * chunk == slot_ref[0:1, :]).astype(F32).astype(BF)
        spectra = dot_nt(by_slot, pick).astype(BF)
        planes = dot(z_up_ref[0], twice(spectra))
        for gg in range(2):
            for q in range(2):
                sp_ref[q, pl.ds(2 * n + gg, planes_all, stride=groups), :] = planes[
                    q * planes_all : (q + 1) * planes_all, gg * LANES : (gg + 1) * LANES
                ]
    lhs = jnp.concatenate([sp_ref[q, :rows, :].astype(BF) for q in range(2)], axis=1)
    for j in range(ws_ref.shape[0] // 2):
        wide = dot(lhs, y_up_ref[:, j * chunk : (j + 1) * chunk])
        ws_ref[2 * j] = wide[:, :LANES]
        ws_ref[2 * j + 1] = wide[:, LANES:]


def gelu_pair(half):
    coeff = math.sqrt(2.0 / math.pi)
    square = half * half
    tangent = jnp.tanh(half * (2.0 * coeff + (8.0 * 0.044715 * coeff) * square))
    turned = half * tangent
    value = half + turned
    inner = 0.5 + (half - turned) * (coeff + (12.0 * 0.044715 * coeff) * square)
    return value, (value * (1.0 + tangent)) * inner


class Planes:
    def __init__(self, step, per_step, channels, planes):
        self.step, self.per_step, self.count = step, per_step, per_step * channels
        self.planes, self.planes_all = planes, planes * channels

    def place(self, t):
        c = t // self.per_step
        zz = t - c * self.per_step
        return c, zz, c * self.planes + self.step * self.per_step + zz


def middle_kernel(per_step, rows, slab_ref, gain_ref, bias_ref, merged_ref, recv_ref, slot_ref, x_down_ref, x_up_ref, y_down_ref, y_up_ref, z_down_ref, z_up_ref, out_ref, grad_ref, packed_ref, xs_ref, ws_ref, zt_ref, sp_ref, sa_ref, sb_ref, ga_ref, gb_ref):
    step = pl.program_id(0)
    channels, _, grid_len, _ = merged_ref.shape
    at = Planes(step, per_step, channels, xs_ref.shape[1] * GROUP // KXY // channels)

    @pl.when(step == 0)
    def _():
        synthesis_head(recv_ref, slot_ref, z_up_ref, y_up_ref, sp_ref, ws_ref)

    def synth(t, s_ref):
        c, _, plane = at.place(t)
        shift = jnp.full((BIAS_ROWS, grid_len), 0.5 * bias_ref[c], F32)
        high = shift.astype(BF).astype(F32)
        row = lax.broadcasted_iota(jnp.int32, shift.shape, 0)
        shift = jnp.where(row == 0, high, jnp.where(row == 1, shift - high, 0.0))
        s_ref[...] = dot(x_up_ref[...], jnp.concatenate([plane_rows(ws_ref, plane, grid_len), shift], axis=0).astype(BF))

    def point(t, s_ref, g_ref):
        c, zz, _ = at.place(t)
        zz_all = step * per_step + zz
        gain = 0.5 * gain_ref[c]
        for start in range(0, grid_len, rows):
            span = slice(start, start + rows)
            merged = merged_ref[c, zz_all, span, :]
            value, grad = gelu_pair(s_ref[span, :] + gain * merged.astype(F32))
            grad = grad.astype(BF)
            out_ref[c, zz, span, :] = value.astype(BF)
            grad_ref[c, zz_all, span, :] = grad
            g_ref[span, :] = grad

    def down(t, g_ref):
        keep_x_rows(xs_ref, at.place(t)[2], dot(x_down_ref[...], g_ref[...]))

    synth(0, sa_ref)

    def body(j, carry):
        t = 2 * j
        synth(t + 1, sb_ref)
        down(jnp.maximum(t - 1, 0), gb_ref)
        point(t, sa_ref, ga_ref)
        synth(jnp.minimum(t + 2, at.count - 1), sa_ref)
        down(t, ga_ref)
        point(t + 1, sb_ref, gb_ref)
        return carry

    lax.fori_loop(0, at.count // 2, body, 0)
    down(at.count - 1, gb_ref)

    @pl.when(step == pl.num_programs(0) - 1)
    def _():
        analysis_tail(xs_ref, y_down_ref, z_down_ref, slot_ref, zt_ref, sp_ref, packed_ref)


def final_kernel(per_step, rows, slab_ref, gain_ref, grad_ref, recv_ref, slot_ref, x_up_ref, y_up_ref, z_up_ref, out_ref, ws_ref, sp_ref):
    step = pl.program_id(0)
    channels, _, grid_len, _ = grad_ref.shape
    at = Planes(step, per_step, channels, ws_ref.shape[1] * GROUP // KXY // channels)

    @pl.when(step == 0)
    def _():
        synthesis_head(recv_ref, slot_ref, z_up_ref, y_up_ref, sp_ref, ws_ref)

    def body(zz, carry):
        for c in range(channels):
            wp = plane_rows(ws_ref, c * at.planes + step * per_step + zz, grid_len).astype(BF)
            out_ref[c, zz] = (dot(x_up_ref[...], wp) + gain_ref[c] * grad_ref[c, step * per_step + zz].astype(F32)).astype(BF)
        return carry

    lax.fori_loop(0, per_step, body, 0)


def announce(targets):
    barrier = pltpu.get_barrier_semaphore()
    for target in targets:
        pl.semaphore_signal(barrier, inc=1, device_id=target, device_id_type=MESH)


def await_peers(targets):
    pl.semaphore_wait(pltpu.get_barrier_semaphore(), len(targets))


def reorder_weights(w_ref, wide_ref):
    width = w_ref.shape[3]
    slots = width // KZ
    flat = w_ref[...].reshape(-1, width)
    chunk = 2 * slots

    def body(n, carry):
        source = lax.broadcasted_iota(jnp.int32, (width, chunk), 0)
        lane = lax.broadcasted_iota(jnp.int32, (1, chunk), 1)
        wanted = jnp.where(lane < slots, lane * KZ, (lane - slots) * KZ + 1) + 2 * n
        moved = dot(flat, (source == wanted).astype(F32).astype(BF)).astype(BF)
        wide_ref[:, :, :, pl.ds(pl.multiple_of(n * chunk, chunk), chunk)] = moved.reshape(w_ref.shape[:3] + (chunk,))
        return carry

    lax.fori_loop(0, width // chunk, body, 0)


def peers_of(slabs, groups):
    slab, chan = lax.axis_index("slab"), lax.axis_index("chan")
    slab_peer = [(lax.rem(slab + d, slabs), chan) for d in range(1, slabs)]
    chan_peer = [(slab, lax.rem(chan + d, groups)) for d in range(1, groups)]
    return slab, chan, slab_peer, chan_peer


def spectra_copy(packed_ref, rx, peer, d, piece, s_send, s_recv):
    rows = packed_ref.shape[1] // PIECES
    part = pl.ds(piece * rows, rows)
    n = piece * rx.shape[0] + d - 1
    return pltpu.make_async_remote_copy(
        src_ref=packed_ref.at[peer[0], part], dst_ref=rx.at[d - 1, part], send_sem=s_send.at[n], recv_sem=s_recv.at[n],
        device_id=peer, device_id_type=MESH,
    )


def mix_kernel(slabs, groups, packed_ref, wide_ref, recv_ref, rx, tx2, rx2, mine, stage, *sems):
    _, _, slab_peer, chan_peer = peers_of(slabs, groups)
    announce(slab_peer + chan_peer)
    await_peers(slab_peer + chan_peer)
    first = [[spectra_copy(packed_ref, rx, slab_peer[d - 1], d, p, *sems[:2]) for d in range(1, slabs)] for p in range(PIECES)]
    for copy in sum(first, []):
        copy.start()
    exchange_body(slabs, groups, False, first, packed_ref, wide_ref, recv_ref, rx, tx2, rx2, mine, stage, *sems)


def exchange_body(slabs, groups, forward, first, packed_ref, wide_ref, recv_ref, rx, tx2, rx2, mine, stage, s_send, s_recv, c_send, c_recv, g_send, g_recv, shared=None, filler=None):
    slab, chan, slab_peer, chan_peer = peers_of(slabs, groups)
    rows, slots = packed_ref.shape[1] // PIECES, packed_ref.shape[2]
    kept = KZ // PIECES
    own = rx2.shape[1] // 2
    pairs = 2 * own
    outputs = own * groups
    wide = kept * slots
    step = min(kept, 4)

    def factor(piece, m):
        return 1.0 if piece == 0 and m == 0 else 2.0

    def at_m(piece, m, count=1):
        return slice((piece * kept + m) * slots, (piece * kept + m + count) * slots)

    second = []
    for p in range(PIECES):
        span = slice(p * rows, (p + 1) * rows)
        total = packed_ref[slab, span, :].astype(F32)
        for d in range(1, slabs):
            first[p][d - 1].wait_recv()
            total = total + rx[d - 1, span, :].astype(F32)
        stage[...] = total
        tiles = [stage[pl.ds(m, pairs, stride=kept), :] for m in range(kept)]
        if shared is not None:
            common = shared() if p == 0 else common
            for m in range(kept):
                both = [common[(2 * p + q) * kept + m : (2 * p + q) * kept + m + 1, :] for q in range(2)]
                tiles[m] = tiles[m] + jnp.concatenate([jnp.broadcast_to(b, (own, slots)) for b in both], axis=0)
        if forward:
            for m in range(0, kept, step):
                at = at_m(p, m, step)
                u = jnp.concatenate(tiles[m : m + step], axis=1)
                real = jnp.zeros((outputs, step * slots), F32)
                imag = jnp.zeros((outputs, step * slots), F32)
                for c in range(own):
                    w0, w1 = wide_ref[0, c, :, at].astype(F32), wide_ref[1, c, :, at].astype(F32)
                    ur, ui = u[c : c + 1], u[own + c : own + c + 1]
                    real = real + (w0 * ur - w1 * ui)
                    imag = imag + (w1 * ur + w0 * ui)
                for e in range(groups):
                    some = slice(e * own, (e + 1) * own)
                    tx2[e, :, at] = jnp.concatenate([real[some], imag[some]], axis=0).astype(BF)
        else:
            for m in range(kept):
                tx2[0, :, at_m(p, m)] = (tiles[m] * factor(p, m)).astype(BF)
        lanes = pl.ds(p * wide, wide)
        copies = []
        for d in range(1, groups):
            peer = chan_peer[d - 1]
            n = p * (groups - 1) + d - 1
            copy = pltpu.make_async_remote_copy(
                src_ref=tx2.at[peer[1] if forward else 0, :, lanes], dst_ref=rx2.at[chan, :, lanes], send_sem=c_send.at[n], recv_sem=c_recv.at[n],
                device_id=peer, device_id_type=MESH,
            )
            copy.start()
            copies.append(copy)
        rx2[chan, :, lanes] = tx2[chan if forward else 0, :, lanes]
        second.append(copies)
    third = []
    for p in range(PIECES):
        for copy in second[p]:
            copy.wait_recv()
        for m in range(0, kept, step):
            at = at_m(p, m, step)
            if forward:
                result = rx2[0, :, at].astype(F32)
                for e in range(1, groups):
                    result = result + rx2[e, :, at].astype(F32)
            else:
                blocks = [rx2[e, :, at].astype(F32) for e in range(groups)]
                real = jnp.concatenate([b[:own] for b in blocks], axis=0)
                imag = jnp.concatenate([b[own:] for b in blocks], axis=0)
                reals, imags = [], []
                for c in range(own):
                    w0, w1 = wide_ref[0, c, :, at].astype(F32), wide_ref[1, c, :, at].astype(F32)
                    reals.append(jnp.sum(w0 * real + w1 * imag, axis=0, keepdims=True))
                    imags.append(jnp.sum(w0 * imag - w1 * real, axis=0, keepdims=True))
                result = jnp.concatenate(reals + imags, axis=0)
            for k in range(step):
                part = result[:, k * slots : (k + 1) * slots]
                stage[pl.ds(m + k, pairs, stride=kept), :] = part * factor(p, m + k) if forward else part
        part = pl.ds(p * rows, rows)
        mine[part, :] = stage[...].astype(BF)
        for d in range(1, slabs):
            n = p * (slabs - 1) + d - 1
            copy = pltpu.make_async_remote_copy(
                src_ref=mine.at[part], dst_ref=recv_ref.at[slab, part], send_sem=g_send.at[n], recv_sem=g_recv.at[n],
                device_id=slab_peer[d - 1], device_id_type=MESH,
            )
            copy.start()
            third.append(copy)
    recv_ref[slab] = mine[...]
    if filler is not None:
        filler()
    for copy in third:
        copy.wait_recv()
    for copy in sum(first, []) + sum(second, []) + third:
        copy.wait_send()


def front_kernel(slabs, groups, field_hbm, forcing_hbm, slots_hbm, w_hbm, x_down_hbm, x_part_hbm, y_down_hbm, z_down_hbm, recv_ref, merged_ref, wide_ref,
                 plane_ref, own_ref, xs_ref, xf_ref, zt_ref, sp_ref, pick_ref, packed_ref, rx, tx2, rx2, mine, stage, slot_ref, w_ref, x_down_ref, x_part_ref, y_down_ref, z_down_ref,
                 f_packed, f_rx, f_mine, f_rx2, f_sum, in_sem, field_sem, x_send, x_recv, p_send, p_recv, f_send, f_recv, h_send, h_recv, *sems):
    slab, chan, slab_peer, chan_peer = peers_of(slabs, groups)
    channels, planes = merged_ref.shape[:2]
    height = forcing_hbm.shape[1]
    chips = groups // 2
    chip, core = chan // 2, lax.rem(chan, 2)
    partner = (slab, chan + 1 - 2 * core)

    def near(t):
        return 2 * lax.rem(chip + chips + t, chips) + core

    def rows(index, start, count):
        return plane_ref.at[pl.ds(start, count), pl.ds(pl.multiple_of(index * height, height), height), :]

    fields = [pltpu.make_async_copy(field_hbm.at[c], merged_ref.at[c], field_sem.at[c]) for c in range(channels)]
    small = [
        pltpu.make_async_copy(forcing_hbm, own_ref, in_sem.at[0]),
        pltpu.make_async_copy(x_part_hbm.at[chan], x_part_ref, in_sem.at[1]),
        pltpu.make_async_copy(y_down_hbm, y_down_ref, in_sem.at[2]),
        pltpu.make_async_copy(z_down_hbm.at[slab], z_down_ref, in_sem.at[3]),
        pltpu.make_async_copy(slots_hbm, slot_ref, in_sem.at[4]),
        pltpu.make_async_copy(x_down_hbm, x_down_ref, in_sem.at[5]),
    ]
    load_w = pltpu.make_async_copy(w_hbm, w_ref, in_sem.at[6])
    place_own = pltpu.make_async_copy(forcing_hbm, rows(chan, 0, planes), in_sem.at[7])
    for copy in small + fields + [load_w, place_own]:
        copy.start()
    announce(slab_peer + chan_peer)
    for copy in small:
        copy.wait()

    def forcing_body(zz, carry):
        keep_x_rows(xf_ref, zz, dot(x_part_ref[...], own_ref[zz]))
        return carry

    lax.fori_loop(0, planes, forcing_body, 0, unroll=4)
    padded = local_spectra(xf_ref, y_down_ref, z_down_ref[...], zt_ref, sp_ref)
    kept = KZ // PIECES
    block = channels * kept
    forced = jnp.concatenate([padded[n * block : n * block + kept] for n in range(2 * PIECES)], axis=0).astype(BF)
    columns = forced.shape[1]
    capacity = packed_ref.shape[2]
    pairs = [(lax.rem(slab + d, slabs), lax.rem(slab + d + 1, slabs)) for d in range(1, slabs, 2)]
    for i, targets in enumerate(pairs):
        pick = pick_columns(columns, jnp.concatenate([slot_ref[pl.ds(t, 1), :] for t in targets], axis=1))
        pick_ref[i] = pick
        part = dot(forced, pick).astype(BF)
        for n, t in enumerate(targets):
            f_packed[t] = part[:, n * capacity : (n + 1) * capacity]
    await_peers(slab_peer + chan_peer)
    sent = []

    def send(copies):
        for copy in copies:
            copy.start()
            sent.append(copy)
        return copies

    forced_in = send([
        pltpu.make_async_remote_copy(
            src_ref=f_packed.at[slab_peer[d - 1][0]], dst_ref=f_rx.at[d - 1], send_sem=f_send.at[d - 1], recv_sem=f_recv.at[d - 1],
            device_id=slab_peer[d - 1], device_id_type=MESH,
        )
        for d in range(1, slabs)
    ])

    half = planes // 2

    def across(index, start, to, n, source=None):
        return pltpu.make_async_remote_copy(
            src_ref=rows(index, start, half) if source is None else source, dst_ref=rows(index, start, half),
            send_sem=x_send.at[n], recv_sem=x_recv.at[n], device_id=(slab, to), device_id_type=MESH,
        )

    def beside(index, start, count, n, source=None):
        return pltpu.make_async_remote_copy(
            src_ref=rows(index, start, count) if source is None else source, dst_ref=rows(index, start, count),
            send_sem=p_send.at[n], recv_sem=p_recv.at[n], device_id=partner, device_id_type=MESH,
        )

    def x_pass(c):
        fields[c].wait()

        def body(zz, carry):
            keep_x_rows(xs_ref, c * planes + zz, dot(x_down_ref[...], merged_ref[c, zz]))
            return carry

        lax.fori_loop(0, planes, body, 0, unroll=4)

    for c in range(channels // 2):
        x_pass(c)
    total = f_packed[slab].astype(F32)
    for d in range(1, slabs):
        forced_in[d - 1].wait_recv()
        total = total + f_rx[d - 1].astype(F32)
    f_mine[...] = total.astype(BF)
    shared_in = send([
        pltpu.make_async_remote_copy(
            src_ref=f_mine, dst_ref=f_rx2.at[chan], send_sem=h_send.at[d - 1], recv_sem=h_recv.at[d - 1],
            device_id=chan_peer[d - 1], device_id_type=MESH,
        )
        for d in range(1, groups)
    ])
    f_rx2[chan] = f_mine[...]
    low, high = own_ref.at[pl.ds(0, half)], own_ref.at[pl.ds(half, half)]
    right_low, left_high, right_high, left_low = send([
        across(chan, 0, near(1), 0, low), across(chan, half, near(-1), 1, high),
        across(chan, half, near(1), 2, high), across(chan, 0, near(-1), 3, low),
    ])
    beside_all = send([beside(chan, 0, planes, 0, own_ref)])
    for c in range(channels // 2, channels):
        x_pass(c)
    coeffs = local_spectra(xs_ref, y_down_ref, z_down_ref[...], zt_ref, sp_ref).astype(BF)
    first = [[spectra_copy(packed_ref, rx, slab_peer[d - 1], d, p, *sems[:2]) for d in range(1, slabs)] for p in range(PIECES)]
    for i, targets in enumerate(pairs):
        part = dot(coeffs, pick_ref[i]).astype(BF)
        for n, t in enumerate(targets):
            packed_ref[t] = part[:, n * capacity : (n + 1) * capacity]
            if 2 * i + n < slabs - 1:
                first[0][2 * i + n].start()
    for copy in sum(first[1:], []):
        copy.start()
    load_w.wait()
    reorder_weights(w_ref, wide_ref)
    right_low.wait_recv()
    left_high.wait_recv()
    far_low, far_high = send([across(near(-1), 0, near(1), 4), across(near(1), half, near(-1), 5)])
    beside_all += send([beside(near(-1), 0, half, 1), beside(near(1), half, half, 2)])

    def shared():
        for copy in shared_in:
            copy.wait_recv()
        common = f_rx2[0].astype(F32)
        for e in range(1, groups):
            common = common + f_rx2[e].astype(F32)
        f_sum[...] = common
        return f_sum

    def merge():
        more = []
        right_high.wait_recv()
        left_low.wait_recv()
        more += send([beside(near(-1), half, half, 3), beside(near(1), 0, half, 4)])
        far_low.wait_recv()
        far_high.wait_recv()
        more += send([beside(near(2), 0, half, 5), beside(near(2), half, half, 6)])
        place_own.wait()
        for copy in beside_all + more:
            copy.wait_recv()

        def body(zz, carry):
            for c in range(channels):
                merged_ref[c, zz] = merged_ref[c, zz] + plane_ref[zz]
            return carry

        lax.fori_loop(0, planes, body, 0)

    exchange_body(slabs, groups, True, first, packed_ref, wide_ref, recv_ref, rx, tx2, rx2, mine, stage, *sems, shared=shared, filler=merge)
    for copy in sent:
        copy.wait_send()


def whole(shape):
    zeros = (0,) * len(shape)
    return pl.BlockSpec(shape, lambda *_: zeros, pipeline_mode=pl.Buffered(1))


class Sizes:
    def __init__(self, slabs, groups, channels, planes, grid_len, capacity):
        self.slabs, self.groups = slabs, groups
        self.channels, self.planes, self.grid_len = channels, planes, grid_len
        self.capacity = capacity
        planes_all = channels * planes
        x_down, x_up, y_down, y_up = plane_tables(grid_len)
        ones = np.zeros((grid_len, BIAS_ROWS), x_up.dtype)
        ones[:, :2] = 1
        half = bf16_table(0.5 * x_up.astype(np.float32))
        self.x_down, self.x_up, self.y_down, self.y_up = [jnp.asarray(t) for t in (x_down, x_up, y_down, y_up)]
        self.x_part = jnp.asarray(x_down.reshape(2 * KXY, groups, -1).transpose(1, 0, 2))
        self.x_up_half = jnp.asarray(np.concatenate([half, ones], axis=1))
        self.z_down, self.z_up = [jnp.asarray(t) for t in depth_tables(channels, planes, slabs, grid_len)]
        self.per_step = 4
        per_step = self.per_step
        self.steps = planes // per_step
        self.field_spec = pl.BlockSpec((channels, per_step, grid_len, grid_len), lambda i, s: (0, i, 0, 0))
        self.plane_spec = pl.BlockSpec((per_step, grid_len, grid_len), lambda i, s: (i, 0, 0))
        self.z_spec = pl.BlockSpec((1,) + self.z_down.shape[1:], lambda i, s: (s[0], 0, 0), pipeline_mode=pl.Buffered(1))
        self.packed_shape = (slabs, 2 * channels * KZ, capacity)
        self.volume = jax.ShapeDtypeStruct((channels, planes, grid_len, grid_len), BF)
        self.packed_out = jax.ShapeDtypeStruct(self.packed_shape, BF)
        self.wide_scratch = pltpu.VMEM((2 * GROUP * grid_len // LANES, planes_all * KXY // GROUP, LANES), F32)
        dma = pltpu.SemaphoreType.DMA
        self.exchange_sems = [dma((PIECES * n,)) for n in (slabs - 1, slabs - 1, groups - 1, groups - 1, slabs - 1, slabs - 1)]
        self.sp_scratch = pltpu.VMEM((2, (planes_all + planes) * KXY // GROUP, LANES), F32)
        self.zt_scratch = pltpu.VMEM((2 * planes_all, KXY * KXY), BF)
        self.params = pltpu.CompilerParams(dimension_semantics=("arbitrary",), vmem_limit_bytes=30 << 20)


SMEM = pl.BlockSpec(memory_space=pltpu.SMEM)
VMEM = pl.BlockSpec(memory_space=pltpu.VMEM)
HBM = pl.BlockSpec(memory_space=pltpu.HBM)


def front_call(z, field, forcing, slot_column, w_spec):
    block = z.packed_shape[1:]
    pair = (z.groups, 2 * z.channels, z.capacity * KZ)
    tiles = 2 * GROUP * z.grid_len // LANES
    forced = (2 * KZ, z.capacity)
    dma = pltpu.SemaphoreType.DMA
    bf16 = [(z.planes, z.grid_len, z.grid_len), forcing.shape]
    operands = (field, forcing, slot_column, w_spec, z.x_down, z.x_part, z.y_down, z.z_down)
    return pl.pallas_call(
        functools.partial(front_kernel, z.slabs, z.groups),
        out_shape=(z.packed_out, z.volume, jax.ShapeDtypeStruct(w_spec.shape, BF)),
        in_specs=[HBM] * len(operands),
        out_specs=(VMEM, VMEM, VMEM),
        scratch_shapes=[pltpu.VMEM(shape, BF) for shape in bf16]
        + [
            z.wide_scratch,
            pltpu.VMEM((tiles, z.planes * KXY // GROUP, LANES), F32),
            z.zt_scratch,
            z.sp_scratch,
            pltpu.VMEM((z.slabs // 2, KXY * KXY, 2 * z.capacity), BF),
            pltpu.VMEM(z.packed_shape, BF),
            pltpu.VMEM((z.slabs - 1,) + block, BF),
            pltpu.VMEM(pair, BF),
            pltpu.VMEM(pair, BF),
            pltpu.VMEM(block, BF),
            pltpu.VMEM((block[0] // PIECES, block[1]), F32),
            pltpu.VMEM(slot_column.shape, jnp.int32),
            pltpu.VMEM(w_spec.shape, BF),
            pltpu.VMEM(z.x_down.shape, BF),
            pltpu.VMEM(z.x_part.shape[1:], BF),
            pltpu.VMEM(z.y_down.shape, BF),
            pltpu.VMEM(z.z_down.shape[1:], BF),
            pltpu.VMEM((z.slabs,) + forced, BF),
            pltpu.VMEM((z.slabs - 1,) + forced, BF),
            pltpu.VMEM(forced, BF),
            pltpu.VMEM((z.groups,) + forced, BF),
            pltpu.VMEM(forced, F32),
            dma((8,)), dma((z.channels,)), dma((6,)), dma((6,)), dma((7,)), dma((7,)),
        ]
        + [dma((z.slabs - 1,))] * 2
        + [dma((z.groups - 1,))] * 2
        + z.exchange_sems,
        compiler_params=pltpu.CompilerParams(collective_id=1, has_side_effects=True, vmem_limit_bytes=32 << 20),
        name="gather_analyse_mix",
    )(*[pltpu.with_memory_space_constraint(v, pltpu.HBM) for v in operands])


def exchange_call(z, values, wide):
    block = z.packed_shape[1:]
    pair = (z.groups, 2 * z.channels, z.capacity * KZ)
    return pl.pallas_call(
        functools.partial(mix_kernel, z.slabs, z.groups),
        out_shape=z.packed_out,
        in_specs=[VMEM, VMEM],
        out_specs=VMEM,
        scratch_shapes=[
            pltpu.VMEM((z.slabs - 1,) + block, BF),
            pltpu.VMEM(pair, BF),
            pltpu.VMEM(pair, BF),
            pltpu.VMEM(block, BF),
            pltpu.VMEM((block[0] // PIECES, block[1]), F32),
        ]
        + z.exchange_sems,
        compiler_params=pltpu.CompilerParams(collective_id=2, has_side_effects=True, vmem_limit_bytes=8 << 20),
        name="mix_adjoint",
    )(values, wide)


def middle_call(z, where, skip_gain, bias, merged, spectra, slots):
    return pl.pallas_call(
        functools.partial(middle_kernel, z.per_step, 64),
        out_shape=(z.volume, z.volume, z.packed_out),
        grid_spec=pltpu.PrefetchScalarGridSpec(
            num_scalar_prefetch=1, grid=(z.steps,),
            in_specs=[SMEM, SMEM, VMEM, VMEM, whole(slots.shape), whole(z.x_down.shape), whole(z.x_up_half.shape), whole(z.y_down.shape), whole(z.y_up.shape), z.z_spec, z.z_spec],
            out_specs=(z.field_spec, VMEM, VMEM),
            scratch_shapes=[z.wide_scratch, z.wide_scratch, z.zt_scratch, z.sp_scratch] + [pltpu.VMEM((z.grid_len, z.grid_len), F32)] * 2 + [pltpu.VMEM((z.grid_len, z.grid_len), BF)] * 2,
        ),
        compiler_params=z.params,
        name="synth_gelu_analyse",
    )(where, skip_gain, bias, merged, spectra, slots, z.x_down, z.x_up_half, z.y_down, z.y_up, z.z_down, z.z_up)


def final_call(z, where, skip_gain, grad_pre, adjoint, slots):
    return pl.pallas_call(
        functools.partial(final_kernel, z.per_step, 64),
        out_shape=z.volume,
        grid_spec=pltpu.PrefetchScalarGridSpec(
            num_scalar_prefetch=1, grid=(z.steps,),
            in_specs=[SMEM, VMEM, VMEM, whole(slots.shape), whole(z.x_up.shape), whole(z.y_up.shape), z.z_spec],
            out_specs=z.field_spec,
            scratch_shapes=[z.wide_scratch, z.sp_scratch],
        ),
        compiler_params=z.params,
        name="synth_gradient",
    )(where, skip_gain, grad_pre, adjoint, slots, z.x_up, z.y_up, z.z_up)


def per_device(slabs, groups, field, forcing, slot_column, w_spec, skip_gain, bias):
    channels, planes, grid_len, _ = field.shape
    capacity = slot_column.shape[1]
    z = Sizes(slabs, groups, channels, planes, grid_len, capacity)
    slots = slot_column.reshape(1, slabs * capacity)
    where = lax.axis_index("slab").astype(jnp.int32).reshape(1)
    spectra, merged, wide = front_call(z, field, forcing, slot_column, w_spec)
    output, grad_pre, packed_back = middle_call(z, where, skip_gain, bias, merged, spectra, slots)
    adjoint = exchange_call(z, packed_back, wide)
    gradient = final_call(z, where, skip_gain, grad_pre, adjoint, slots)
    return (output, gradient)


def solution(mesh):
    placed = (
        P("chan", "slab", None, None),
        P("slab", "chan", None),
        P(),
        P(None, "chan", None, "slab"),
        P("chan"),
        P("chan"),
    )
    slabs, groups = mesh.shape["slab"], mesh.shape["chan"]
    return jax.shard_map(
        functools.partial(per_device, slabs, groups),
        mesh=mesh,
        in_specs=placed,
        out_specs=(P("chan", "slab", None, None), P("chan", "slab", None, None)),
        check_vma=False,
    )
```

```python
import functools
import math

import jax
import jax.numpy as jnp
import ml_dtypes
import numpy as np
from jax import lax
from jax.experimental import pallas as pl
from jax.experimental.pallas import tpu as pltpu
from jax.sharding import PartitionSpec as P

KXY = 32
KZ = 16
MESH = pl.DeviceIdType.MESH
BF = jnp.bfloat16
F32 = jnp.float32
LANES = 128
SPECTRAL_VMEM = 31 << 20
PIECES = 2
HALVES = 2
BIAS_ROWS = 16
GROUP = LANES // KXY


def bf16_table(values):
    return np.asarray(values, np.float32).astype(ml_dtypes.bfloat16)


def trig(freqs, coords, grid_len):
    angle = (np.outer(freqs, coords) % grid_len) * (2.0 * math.pi / grid_len)
    return np.cos(angle), np.sin(angle)


def plane_tables(grid_len):
    freqs = np.arange(KXY) - KXY // 2
    cos, sin = trig(freqs, np.arange(grid_len), grid_len)
    groups = KXY // GROUP
    scale = float(grid_len) ** -1.5
    x_down = np.zeros((GROUP, 2, groups, grid_len))
    x_up = np.zeros((grid_len, GROUP, 2, groups))
    y_down = np.zeros((GROUP, 2, grid_len, 2, GROUP, KXY))
    y_up = np.zeros((2, GROUP, KXY, GROUP, 2, grid_len))
    for k in range(GROUP):
        for g in range(groups):
            jx = g * GROUP + k
            x_down[k, 0, g], x_down[k, 1, g] = cos[jx], sin[jx]
            x_up[:, k, 0, g], x_up[:, k, 1, g] = scale * cos[jx], -scale * sin[jx]
        y_down[k, 0, :, 0, k], y_down[k, 1, :, 0, k] = cos.T, -sin.T
        y_down[k, 0, :, 1, k], y_down[k, 1, :, 1, k] = -sin.T, -cos.T
        y_up[0, k, :, k, 0], y_up[1, k, :, k, 0] = cos, -sin
        y_up[0, k, :, k, 1], y_up[1, k, :, k, 1] = sin, cos
    rows = 2 * KXY
    return (
        bf16_table(x_down.reshape(rows, grid_len)),
        bf16_table(x_up.reshape(grid_len, rows)),
        bf16_table(y_down.reshape(2 * GROUP * grid_len, 2 * LANES)),
        bf16_table(y_up.reshape(2 * LANES, 2 * GROUP * grid_len)),
    )


def depth_tables(channels, planes, slabs, grid_len):
    scale = float(grid_len) ** -1.5
    down, up = [], []
    for s in range(slabs):
        cos, sin = trig(np.arange(KZ), s * planes + np.arange(planes), grid_len)
        parts = [[cos, sin], [-sin, cos]]
        for store, count in ((down, channels // HALVES), (up, channels)):
            full = np.zeros((2, count, KZ, 2, count, planes))
            for q in range(2):
                for r in range(2):
                    full[q, :, :, r] = np.einsum("cd,mz->cmdz", np.eye(count), parts[q][r])
            full = full.reshape(2, count, PIECES, KZ // PIECES, -1).transpose(2, 0, 1, 3, 4)
            full = full.reshape(2 * count * KZ, 2 * count * planes)
            table = full * scale if store is down else full.T
            high = bf16_table(table)
            low = bf16_table(table - high.astype(np.float64))
            store.append(np.concatenate([high, low], axis=1))
    return np.stack(down), np.stack(up)


def dot(a, b):
    return jnp.dot(a, b, preferred_element_type=F32)


def dot_nt(a, b):
    return lax.dot_general(a, b, (((1,), (1,)), ((), ())), preferred_element_type=F32)


def twice(block):
    return jnp.concatenate([block, block], axis=0)


def tile_rows(plane):
    groups = KXY // GROUP
    return pl.ds(pl.multiple_of(plane * groups, groups), groups)


def keep_x_rows(xs_ref, plane, value):
    groups = KXY // GROUP
    tiles = value.shape[1] // LANES
    for kp in range(2 * GROUP):
        for h in range(tiles):
            xs_ref[kp * tiles + h, tile_rows(plane), :] = value[kp * groups : (kp + 1) * groups, h * LANES : (h + 1) * LANES]


def plane_rows(ws_ref, plane, width):
    tiles = width // LANES
    columns = []
    for h in range(tiles):
        parts = [ws_ref[kp * tiles + h, tile_rows(plane), :] for kp in range(2 * GROUP)]
        columns.append(jnp.concatenate(parts, axis=0))
    return jnp.concatenate(columns, axis=1)


def local_spectra(xs_ref, y_down_ref, z_down, zt_ref, sp_ref, start, count):
    groups = KXY // GROUP
    rows = slice(start * groups, (start + count) * groups)
    half = zt_ref.shape[0] // 2
    lhs = jnp.concatenate([xs_ref[j, rows, :].astype(BF) for j in range(xs_ref.shape[0])], axis=1)
    spectra = dot(lhs, y_down_ref[...])
    for q in range(2):
        sp_ref[q, : count * groups, :] = spectra[:, q * LANES : (q + 1) * LANES]
    if count < half:
        zt_ref[...] = jnp.zeros_like(zt_ref)
    for g in range(groups):
        for q in range(2):
            part = sp_ref[q, pl.ds(g, count, stride=groups), :]
            zt_ref[q * half : q * half + count, g * LANES : (g + 1) * LANES] = part.astype(BF)
    return dot(z_down, twice(zt_ref[...]))


def slot_pairs(slab, slabs):
    return [(lax.rem(slab + d, slabs), lax.rem(slab + d + 1, slabs)) for d in range(1, slabs, 2)]


def pack_half(coeffs, pick_ref, pairs, packed_ref, h, sends):
    rows = coeffs.shape[0]
    capacity = packed_ref.shape[2]
    for i, targets in enumerate(pairs):
        part = dot(coeffs, pick_ref[:, 2 * i * capacity : 2 * (i + 1) * capacity]).astype(BF)
        for n, t in enumerate(targets):
            packed_ref[t, h * rows : (h + 1) * rows, :] = part[:, n * capacity : (n + 1) * capacity]
            if 2 * i + n < len(sends):
                sends[2 * i + n].start()


def synthesis_head(slab, recv_ref, pick_ref, z_up, y_up_ref, sp_ref, ws_ref):
    groups = KXY // GROUP
    rows = ws_ref.shape[1]
    planes_all = rows // groups
    slabs = recv_ref.shape[0]
    by_slot = jnp.concatenate([recv_ref[t] for pair in slot_pairs(slab, slabs) for t in pair], axis=1)
    chunk = 2 * LANES
    for n in range(KXY * KXY // chunk):
        spectra = dot_nt(by_slot, pick_ref[n * chunk : (n + 1) * chunk, :]).astype(BF)
        planes = dot(z_up, twice(spectra))
        for gg in range(2):
            for q in range(2):
                sp_ref[q, pl.ds(2 * n + gg, planes_all, stride=groups), :] = planes[
                    q * planes_all : (q + 1) * planes_all, gg * LANES : (gg + 1) * LANES
                ]
    lhs = jnp.concatenate([sp_ref[q, :rows, :].astype(BF) for q in range(2)], axis=1)
    for j in range(ws_ref.shape[0] // 2):
        wide = dot(lhs, y_up_ref[:, j * chunk : (j + 1) * chunk])
        ws_ref[2 * j] = wide[:, :LANES]
        ws_ref[2 * j + 1] = wide[:, LANES:]


def gelu_pair(half):
    coeff = math.sqrt(2.0 / math.pi)
    square = half * half
    tangent = jnp.tanh(half * (2.0 * coeff + (8.0 * 0.044715 * coeff) * square))
    turned = half * tangent
    value = half + turned
    inner = 0.5 + (half - turned) * (coeff + (12.0 * 0.044715 * coeff) * square)
    return value, (value * (1.0 + tangent)) * inner


def final_kernel(per_step, slab_ref, gain_ref, value_ref, grad_ref, recv_ref, pick_ref, x_up_ref, y_up_ref, z_up_ref, value_hbm, out_ref, ws_ref, sp_ref, value_sem):
    step = pl.program_id(0)
    channels, planes = grad_ref.shape[:2]
    grid_len = grad_ref.shape[2]
    copies = [pltpu.make_async_copy(value_ref.at[c], value_hbm.at[c], value_sem.at[c]) for c in range(channels)]

    @pl.when(step == 0)
    def _():
        for copy in copies:
            copy.start()
        synthesis_head(slab_ref[0], recv_ref, pick_ref, z_up_ref[0], y_up_ref, sp_ref, ws_ref)

    def body(zz, carry):
        for c in range(channels):
            wp = plane_rows(ws_ref, c * planes + step * per_step + zz, grid_len).astype(BF)
            out_ref[c, zz] = (dot(x_up_ref[...], wp) + gain_ref[c] * grad_ref[c, step * per_step + zz].astype(F32)).astype(BF)
        return carry

    lax.fori_loop(0, per_step, body, 0)

    @pl.when(step == pl.num_programs(0) - 1)
    def _():
        for copy in copies:
            copy.wait()


def announce(targets):
    barrier = pltpu.get_barrier_semaphore()
    for target in targets:
        pl.semaphore_signal(barrier, inc=1, device_id=target, device_id_type=MESH)


def await_peers(targets):
    pl.semaphore_wait(pltpu.get_barrier_semaphore(), len(targets))


def reorder_weights(w_ref, wide_ref):
    width = w_ref.shape[3]
    slots = width // KZ
    flat = w_ref[...].reshape(-1, width)
    chunk = 2 * slots

    def body(n, carry):
        source = lax.broadcasted_iota(jnp.int32, (width, chunk), 0)
        lane = lax.broadcasted_iota(jnp.int32, (1, chunk), 1)
        wanted = jnp.where(lane < slots, lane * KZ, (lane - slots) * KZ + 1) + 2 * n
        moved = dot(flat, (source == wanted).astype(F32).astype(BF)).astype(BF)
        wide_ref[:, :, :, pl.ds(pl.multiple_of(n * chunk, chunk), chunk)] = moved.reshape(w_ref.shape[:3] + (chunk,))
        return carry

    lax.fori_loop(0, width // chunk, body, 0)


def peers_of(slabs, groups):
    slab, chan = lax.axis_index("slab"), lax.axis_index("chan")
    slab_peer = [(lax.rem(slab + d, slabs), chan) for d in range(1, slabs)]
    chan_peer = [(slab, lax.rem(chan + d, groups)) for d in range(1, groups)]
    return slab, chan, slab_peer, chan_peer


def spectra_copies(packed_ref, rx, peers, h, s_send, s_recv):
    rows = packed_ref.shape[1] // HALVES
    part = pl.ds(h * rows, rows)
    copies = []
    for d, peer in enumerate(peers):
        n = h * len(peers) + d
        copies.append(pltpu.make_async_remote_copy(
            src_ref=packed_ref.at[peer[0], part], dst_ref=rx.at[d, part], send_sem=s_send.at[n], recv_sem=s_recv.at[n],
            device_id=peer, device_id_type=MESH,
        ))
    return copies


def middle_part(slabs, groups, rows, gain_ref, bias_ref, recv_ref, wide_ref, pick_ref, x_down_ref, x_up_ref, y_down_ref, y_up_ref, z_down_ref, z_up_ref,
                out_ref, grad_ref, adjoint_ref, xs_ref, ws_ref, zt_ref, sp_ref, sa_ref, sb_ref, ga_ref, gb_ref, ma_ref, mb_ref, packed_ref, rx, tx2, rx2, mine, stage, *sems):
    slab, _, slab_peer, _ = peers_of(slabs, groups)
    channels, planes, grid_len, _ = out_ref.shape
    count = channels * planes
    synthesis_head(slab, recv_ref, pick_ref, z_up_ref[...], y_up_ref, sp_ref, ws_ref)

    def synth(t, s_ref, m_ref):
        c = t // planes
        m_ref[...] = out_ref[c, t - c * planes]
        shift = jnp.full((BIAS_ROWS, grid_len), 0.5 * bias_ref[c], F32)
        high = shift.astype(BF).astype(F32)
        row = lax.broadcasted_iota(jnp.int32, shift.shape, 0)
        shift = jnp.where(row == 0, high, jnp.where(row == 1, shift - high, 0.0))
        s_ref[...] = dot(x_up_ref[...], jnp.concatenate([plane_rows(ws_ref, t, grid_len), shift], axis=0).astype(BF))

    def point(t, s_ref, m_ref, g_ref):
        c = t // planes
        zz = t - c * planes
        gain = 0.5 * gain_ref[c]
        for start in range(0, grid_len, rows):
            span = slice(start, start + rows)
            value, grad = gelu_pair(s_ref[span, :] + gain * m_ref[span, :].astype(F32))
            grad = grad.astype(BF)
            out_ref[c, zz, span, :] = value.astype(BF)
            grad_ref[c, zz, span, :] = grad
            g_ref[span, :] = grad

    def down(t, g_ref):
        keep_x_rows(xs_ref, t, dot(x_down_ref[...], g_ref[...]))

    gb_ref[...] = jnp.zeros_like(gb_ref)
    synth(0, sa_ref, ma_ref)

    def body(j, carry):
        t = 2 * j
        synth(t + 1, sb_ref, mb_ref)
        down(jnp.maximum(t - 1, 0), gb_ref)
        point(t, sa_ref, ma_ref, ga_ref)
        synth(jnp.minimum(t + 2, count - 1), sa_ref, ma_ref)
        down(t, ga_ref)
        point(t + 1, sb_ref, mb_ref, gb_ref)
        return carry

    part = count // HALVES
    first = [spectra_copies(packed_ref, rx, slab_peer, h, *sems[:2]) for h in range(HALVES)]
    for h in range(HALVES):
        lax.fori_loop(h * part // 2, (h + 1) * part // 2, body, 0)
        down((h + 1) * part - 1, gb_ref)
        coeffs = local_spectra(xs_ref, y_down_ref, z_down_ref[...], zt_ref, sp_ref, h * part, part).astype(BF)
        pack_half(coeffs, pick_ref, slot_pairs(slab, slabs), packed_ref, h, first[h])
    exchange_body(slabs, groups, False, first, packed_ref, wide_ref, adjoint_ref, rx, tx2, rx2, mine, stage, *sems)


def exchange_body(slabs, groups, forward, first, packed_ref, wide_ref, recv_ref, rx, tx2, rx2, mine, stage, s_send, s_recv, c_send, c_recv, g_send, g_recv, shared=None, filler=None):
    slab, chan, slab_peer, chan_peer = peers_of(slabs, groups)
    rows, slots = packed_ref.shape[1] // PIECES, packed_ref.shape[2]
    kept = KZ // PIECES
    own = rx2.shape[1] // 2
    some = own // HALVES
    pairs = 2 * own
    outputs = own * groups
    wide = kept * slots
    step = min(kept, 4)

    def factor(piece, m):
        return 1.0 if piece == 0 and m == 0 else 2.0

    def at_m(piece, m, count=1):
        return slice((piece * kept + m) * slots, (piece * kept + m + count) * slots)

    def part_rows(h, q):
        return slice((2 * h + q) * some, (2 * h + q + 1) * some)

    half = packed_ref.shape[1] // HALVES
    for h in range(HALVES):
        span = slice(h * half, (h + 1) * half)
        total = packed_ref[slab, span, :].astype(F32)
        for d in range(1, slabs):
            first[h][d - 1].wait_recv()
            total = total + rx[d - 1, span, :].astype(F32)
        stage[span, :] = total
    common = None if shared is None else shared()
    second = []
    for p in range(PIECES):
        tiles = []
        for m in range(kept):
            base = [h * half + p * (half // PIECES) + m for h in range(HALVES)]
            tile = jnp.concatenate([stage[pl.ds(at, 2 * some, stride=kept), :] for at in base], axis=0)
            if common is not None:
                both = [common[(2 * p + q) * kept + m : (2 * p + q) * kept + m + 1, :] for q in range(2)]
                tile = tile + jnp.concatenate([jnp.broadcast_to(b, (some, slots)) for b in both] * HALVES, axis=0)
            tiles.append(tile)
        if forward:
            for m in range(0, kept, step):
                at = at_m(p, m, step)
                u = jnp.concatenate(tiles[m : m + step], axis=1)
                real = jnp.zeros((outputs, step * slots), F32)
                imag = jnp.zeros((outputs, step * slots), F32)
                for c in range(own):
                    w0, w1 = wide_ref[0, c, :, at].astype(F32), wide_ref[1, c, :, at].astype(F32)
                    h, k = c // some, c % some
                    ur, ui = u[2 * h * some + k : 2 * h * some + k + 1], u[(2 * h + 1) * some + k : (2 * h + 1) * some + k + 1]
                    real = real + (w0 * ur - w1 * ui)
                    imag = imag + (w1 * ur + w0 * ui)
                for e in range(groups):
                    mine_rows = slice(e * own, (e + 1) * own)
                    tx2[e, :, at] = jnp.concatenate([real[mine_rows], imag[mine_rows]], axis=0).astype(BF)
        else:
            for m in range(kept):
                tx2[0, :, at_m(p, m)] = (tiles[m] * factor(p, m)).astype(BF)
        lanes = pl.ds(p * wide, wide)
        copies = []
        for d in range(1, groups):
            peer = chan_peer[d - 1]
            n = p * (groups - 1) + d - 1
            copy = pltpu.make_async_remote_copy(
                src_ref=tx2.at[peer[1] if forward else 0, :, lanes], dst_ref=rx2.at[chan, :, lanes], send_sem=c_send.at[n], recv_sem=c_recv.at[n],
                device_id=peer, device_id_type=MESH,
            )
            copy.start()
            copies.append(copy)
        rx2[chan, :, lanes] = tx2[chan if forward else 0, :, lanes]
        second.append(copies)
    third = []
    for p in range(PIECES):
        for copy in second[p]:
            copy.wait_recv()
        for m in range(0, kept, step):
            at = at_m(p, m, step)
            if forward:
                result = rx2[0, :, at].astype(F32)
                for e in range(1, groups):
                    result = result + rx2[e, :, at].astype(F32)
            else:
                blocks = [rx2[e, :, at].astype(F32) for e in range(groups)]
                real = jnp.concatenate([b[part_rows(h, 0)] for b in blocks for h in range(HALVES)], axis=0)
                imag = jnp.concatenate([b[part_rows(h, 1)] for b in blocks for h in range(HALVES)], axis=0)
                reals, imags = [], []
                for c in range(own):
                    w0, w1 = wide_ref[0, c, :, at].astype(F32), wide_ref[1, c, :, at].astype(F32)
                    reals.append(jnp.sum(w0 * real + w1 * imag, axis=0, keepdims=True))
                    imags.append(jnp.sum(w0 * imag - w1 * real, axis=0, keepdims=True))
                result = jnp.concatenate(reals + imags, axis=0)
            for k in range(step):
                part = result[:, k * slots : (k + 1) * slots]
                stage[pl.ds(p * rows + m + k, pairs, stride=kept), :] = part * factor(p, m + k) if forward else part
        part = pl.ds(p * rows, rows)
        mine[part, :] = stage[part, :].astype(BF)
        for d in range(1, slabs):
            n = p * (slabs - 1) + d - 1
            copy = pltpu.make_async_remote_copy(
                src_ref=mine.at[part], dst_ref=recv_ref.at[slab, part], send_sem=g_send.at[n], recv_sem=g_recv.at[n],
                device_id=slab_peer[d - 1], device_id_type=MESH,
            )
            copy.start()
            third.append(copy)
    recv_ref[slab] = mine[...]
    if filler is not None:
        filler()
    for copy in third:
        copy.wait_recv()
    for copy in sum(first, []) + sum(second, []) + third:
        copy.wait_send()


def front_part(slabs, groups, field_hbm, forcing_hbm, slots_hbm, w_hbm, x_down_hbm, x_part_hbm, y_down_hbm, z_down_hbm, later, recv_ref, merged_ref, wide_ref, pick_ref,
               plane_ref, own_ref, xs_ref, xf_ref, zt_ref, sp_ref, packed_ref, rx, tx2, rx2, mine, stage, slot_ref, w_ref, x_down_ref, x_part_ref, y_down_ref, z_down_ref,
                 f_packed, f_rx, f_mine, f_rx2, f_sum, in_sem, field_sem, x_send, x_recv, p_send, p_recv, f_send, f_recv, h_send, h_recv, *sems):
    slab, chan, slab_peer, chan_peer = peers_of(slabs, groups)
    channels, planes = merged_ref.shape[:2]
    height = forcing_hbm.shape[1]
    chips = groups // 2
    chip, core = chan // 2, lax.rem(chan, 2)
    partner = (slab, chan + 1 - 2 * core)

    def near(t):
        return 2 * lax.rem(chip + chips + t, chips) + core

    def rows(index, start, count):
        return plane_ref.at[pl.ds(start, count), pl.ds(pl.multiple_of(index * height, height), height), :]

    fields = [pltpu.make_async_copy(field_hbm.at[c], merged_ref.at[c], field_sem.at[c]) for c in range(channels)]
    small = [
        pltpu.make_async_copy(forcing_hbm, own_ref, in_sem.at[0]),
        pltpu.make_async_copy(x_part_hbm.at[chan], x_part_ref, in_sem.at[1]),
        pltpu.make_async_copy(y_down_hbm, y_down_ref, in_sem.at[2]),
        pltpu.make_async_copy(z_down_hbm.at[slab], z_down_ref, in_sem.at[3]),
        pltpu.make_async_copy(slots_hbm, slot_ref, in_sem.at[4]),
        pltpu.make_async_copy(x_down_hbm, x_down_ref, in_sem.at[5]),
    ]
    load_w = pltpu.make_async_copy(w_hbm, w_ref, in_sem.at[6])
    place_own = pltpu.make_async_copy(forcing_hbm, rows(chan, 0, planes), in_sem.at[7])
    for copy in small + fields + [load_w, place_own] + later:
        copy.start()
    announce(slab_peer + chan_peer)
    for copy in small:
        copy.wait()

    def forcing_body(zz, carry):
        keep_x_rows(xf_ref, zz, dot(x_part_ref[...], own_ref[zz]))
        return carry

    lax.fori_loop(0, planes, forcing_body, 0, unroll=4)
    padded = local_spectra(xf_ref, y_down_ref, z_down_ref[...], zt_ref, sp_ref, 0, planes)
    kept = KZ // PIECES
    block = channels // HALVES * kept
    forced = jnp.concatenate([padded[n * block : n * block + kept] for n in range(2 * PIECES)], axis=0).astype(BF)
    columns = forced.shape[1]
    capacity = packed_ref.shape[2]
    pairs = slot_pairs(slab, slabs)
    for i, targets in enumerate(pairs):
        column = lax.broadcasted_iota(jnp.int32, (columns, 2 * capacity), 0)
        pick = (column == jnp.concatenate([slot_ref[pl.ds(t, 1), :] for t in targets], axis=1)).astype(F32).astype(BF)
        pick_ref[:, 2 * i * capacity : 2 * (i + 1) * capacity] = pick
        part = dot(forced, pick).astype(BF)
        for n, t in enumerate(targets):
            f_packed[t] = part[:, n * capacity : (n + 1) * capacity]
    await_peers(slab_peer + chan_peer)
    sent = []

    def send(copies):
        for copy in copies:
            copy.start()
            sent.append(copy)
        return copies

    forced_in = send([
        pltpu.make_async_remote_copy(
            src_ref=f_packed.at[slab_peer[d - 1][0]], dst_ref=f_rx.at[d - 1], send_sem=f_send.at[d - 1], recv_sem=f_recv.at[d - 1],
            device_id=slab_peer[d - 1], device_id_type=MESH,
        )
        for d in range(1, slabs)
    ])

    half = planes // 2

    def across(index, start, to, n, source=None):
        return pltpu.make_async_remote_copy(
            src_ref=rows(index, start, half) if source is None else source, dst_ref=rows(index, start, half),
            send_sem=x_send.at[n], recv_sem=x_recv.at[n], device_id=(slab, to), device_id_type=MESH,
        )

    def beside(index, start, count, n, source=None):
        return pltpu.make_async_remote_copy(
            src_ref=rows(index, start, count) if source is None else source, dst_ref=rows(index, start, count),
            send_sem=p_send.at[n], recv_sem=p_recv.at[n], device_id=partner, device_id_type=MESH,
        )

    def x_pass(c):
        fields[c].wait()

        def body(zz, carry):
            keep_x_rows(xs_ref, c * planes + zz, dot(x_down_ref[...], merged_ref[c, zz]))
            return carry

        lax.fori_loop(0, planes, body, 0, unroll=4)

    first = [spectra_copies(packed_ref, rx, slab_peer, h, *sems[:2]) for h in range(HALVES)]
    part = channels // HALVES

    def send_half(h):
        for c in range(h * part, (h + 1) * part):
            x_pass(c)
        coeffs = local_spectra(xs_ref, y_down_ref, z_down_ref[...], zt_ref, sp_ref, h * part * planes, part * planes).astype(BF)
        pack_half(coeffs, pick_ref, pairs, packed_ref, h, first[h])

    send_half(0)
    total = f_packed[slab].astype(F32)
    for d in range(1, slabs):
        forced_in[d - 1].wait_recv()
        total = total + f_rx[d - 1].astype(F32)
    f_mine[...] = total.astype(BF)
    shared_in = send([
        pltpu.make_async_remote_copy(
            src_ref=f_mine, dst_ref=f_rx2.at[chan], send_sem=h_send.at[d - 1], recv_sem=h_recv.at[d - 1],
            device_id=chan_peer[d - 1], device_id_type=MESH,
        )
        for d in range(1, groups)
    ])
    f_rx2[chan] = f_mine[...]
    low, high = own_ref.at[pl.ds(0, half)], own_ref.at[pl.ds(half, half)]
    right_low, left_high, right_high, left_low = send([
        across(chan, 0, near(1), 0, low), across(chan, half, near(-1), 1, high),
        across(chan, half, near(1), 2, high), across(chan, 0, near(-1), 3, low),
    ])
    beside_all = send([beside(chan, 0, planes, 0, own_ref)])
    for h in range(1, HALVES):
        send_half(h)
    load_w.wait()
    reorder_weights(w_ref, wide_ref)
    right_low.wait_recv()
    left_high.wait_recv()
    far_low, far_high = send([across(near(-1), 0, near(1), 4), across(near(1), half, near(-1), 5)])
    beside_all += send([beside(near(-1), 0, half, 1), beside(near(1), half, half, 2)])

    def shared():
        for copy in shared_in:
            copy.wait_recv()
        common = f_rx2[0].astype(F32)
        for e in range(1, groups):
            common = common + f_rx2[e].astype(F32)
        f_sum[...] = common
        return f_sum

    def merge():
        more = []
        right_high.wait_recv()
        left_low.wait_recv()
        more += send([beside(near(-1), half, half, 3), beside(near(1), 0, half, 4)])
        far_low.wait_recv()
        far_high.wait_recv()
        more += send([beside(near(2), 0, half, 5), beside(near(2), half, half, 6)])
        place_own.wait()
        for copy in beside_all + more:
            copy.wait_recv()

        def body(zz, carry):
            for c in range(channels):
                merged_ref[c, zz] = merged_ref[c, zz] + plane_ref[zz]
            return carry

        lax.fori_loop(0, planes, body, 0)

    exchange_body(slabs, groups, True, first, packed_ref, wide_ref, recv_ref, rx, tx2, rx2, mine, stage, *sems, shared=shared, filler=merge)
    for copy in sent:
        copy.wait_send()
    for copy in later:
        copy.wait()


def spectral_kernel(slabs, groups, rows, gain_ref, bias_ref, field_hbm, forcing_hbm, slots_hbm, w_hbm, x_down_hbm, x_part_hbm, y_down_hbm, z_down_hbm, x_up_hbm, y_up_hbm, z_up_hbm,
                    out_ref, grad_ref, adjoint_ref, pick_ref, recv_ref, wide_ref, x_down_ref, x_up_ref, y_down_ref, y_up_ref, z_down_ref, z_up_ref,
                    xs_ref, ws_ref, zt_ref, sp_ref, sa_ref, sb_ref, ga_ref, gb_ref, ma_ref, mb_ref,
                    plane_ref, own_ref, xf_ref, slot_ref, w_ref, x_part_ref, f_packed, f_rx, f_mine, f_rx2, f_sum, later_sem, in_sem, field_sem, x_send, x_recv, p_send, p_recv, f_send, f_recv, h_send, h_recv, *rest):
    forward, adjoint = rest[:12], rest[12:]
    later = [
        pltpu.make_async_copy(x_up_hbm, x_up_ref, later_sem.at[0]),
        pltpu.make_async_copy(y_up_hbm, y_up_ref, later_sem.at[1]),
        pltpu.make_async_copy(z_up_hbm.at[lax.axis_index("slab")], z_up_ref, later_sem.at[2]),
    ]
    packed_ref, rx, tx2, rx2, mine, stage = forward[:6]
    front_part(slabs, groups, field_hbm, forcing_hbm, slots_hbm, w_hbm, x_down_hbm, x_part_hbm, y_down_hbm, z_down_hbm, later, recv_ref, out_ref, wide_ref, pick_ref,
               plane_ref, own_ref, xs_ref, xf_ref, zt_ref, sp_ref, packed_ref, rx, tx2, rx2, mine, stage, slot_ref, w_ref, x_down_ref, x_part_ref, y_down_ref, z_down_ref,
               f_packed, f_rx, f_mine, f_rx2, f_sum, in_sem, field_sem, x_send, x_recv, p_send, p_recv, f_send, f_recv, h_send, h_recv, *forward[6:])
    middle_part(slabs, groups, rows, gain_ref, bias_ref, recv_ref, wide_ref, pick_ref, x_down_ref, x_up_ref, y_down_ref, y_up_ref, z_down_ref, z_up_ref,
                out_ref, grad_ref, adjoint_ref, xs_ref, ws_ref, zt_ref, sp_ref, sa_ref, sb_ref, ga_ref, gb_ref, ma_ref, mb_ref, *adjoint)


def whole(shape):
    zeros = (0,) * len(shape)
    return pl.BlockSpec(shape, lambda *_: zeros, pipeline_mode=pl.Buffered(1))


class Sizes:
    def __init__(self, slabs, groups, channels, planes, grid_len, capacity):
        self.slabs, self.groups = slabs, groups
        self.channels, self.planes, self.grid_len = channels, planes, grid_len
        self.capacity = capacity
        planes_all = channels * planes
        x_down, x_up, y_down, y_up = plane_tables(grid_len)
        ones = np.zeros((grid_len, BIAS_ROWS), x_up.dtype)
        ones[:, :2] = 1
        half = bf16_table(0.5 * x_up.astype(np.float32))
        self.x_down, self.x_up, self.y_down, self.y_up = [jnp.asarray(t) for t in (x_down, x_up, y_down, y_up)]
        self.x_part = jnp.asarray(x_down.reshape(2 * KXY, groups, -1).transpose(1, 0, 2))
        self.x_up_half = jnp.asarray(np.concatenate([half, ones], axis=1))
        self.z_down, self.z_up = [jnp.asarray(t) for t in depth_tables(channels, planes, slabs, grid_len)]
        self.per_step = 4
        per_step = self.per_step
        self.steps = planes // per_step
        self.field_spec = pl.BlockSpec((channels, per_step, grid_len, grid_len), lambda i, s: (0, i, 0, 0))
        self.plane_spec = pl.BlockSpec((per_step, grid_len, grid_len), lambda i, s: (i, 0, 0))
        self.z_spec = pl.BlockSpec((1,) + self.z_up.shape[1:], lambda i, s: (s[0], 0, 0), pipeline_mode=pl.Buffered(1))
        self.packed_shape = (slabs, 2 * channels * KZ, capacity)
        self.volume = jax.ShapeDtypeStruct((channels, planes, grid_len, grid_len), BF)
        self.packed_out = jax.ShapeDtypeStruct(self.packed_shape, BF)
        self.wide_scratch = pltpu.VMEM((2 * GROUP * grid_len // LANES, planes_all * KXY // GROUP, LANES), F32)
        dma = pltpu.SemaphoreType.DMA
        self.exchange_sems = [dma((n,)) for n in [HALVES * (slabs - 1)] * 2 + [PIECES * (groups - 1)] * 2 + [PIECES * (slabs - 1)] * 2]
        self.sp_scratch = pltpu.VMEM((2, planes_all * KXY // GROUP, LANES), F32)
        self.zt_scratch = pltpu.VMEM((2 * planes_all // HALVES, KXY * KXY), BF)
        self.params = pltpu.CompilerParams(dimension_semantics=("arbitrary",), vmem_limit_bytes=14 << 20)


SMEM = pl.BlockSpec(memory_space=pltpu.SMEM)
VMEM = pl.BlockSpec(memory_space=pltpu.VMEM)
HBM = pl.BlockSpec(memory_space=pltpu.HBM)


def spectral_call(z, field, forcing, slot_column, w_spec, skip_gain, bias):
    block = z.packed_shape[1:]
    pair = (z.groups, 2 * z.channels, z.capacity * KZ)
    tiles = 2 * GROUP * z.grid_len // LANES
    forced = (2 * KZ, z.capacity)
    plane = (z.grid_len, z.grid_len)
    dma = pltpu.SemaphoreType.DMA
    operands = (field, forcing, slot_column, w_spec, z.x_down, z.x_part, z.y_down, z.z_down, z.x_up_half, z.y_up, z.z_up)

    def scratch(kind, *shapes):
        return [pltpu.VMEM(shape, kind) for shape in shapes]

    exchange = scratch(BF, z.packed_shape, (z.slabs - 1,) + block, pair, pair, block) + scratch(F32, block) + z.exchange_sems
    return pl.pallas_call(
        functools.partial(spectral_kernel, z.slabs, z.groups, 64),
        out_shape=(z.volume, z.volume, z.packed_out, jax.ShapeDtypeStruct((KXY * KXY, slot_column.size), BF)),
        in_specs=[SMEM, SMEM] + [HBM] * len(operands),
        out_specs=(VMEM, VMEM, VMEM, VMEM),
        scratch_shapes=scratch(BF, z.packed_shape, w_spec.shape, z.x_down.shape, z.x_up_half.shape, z.y_down.shape, z.y_up.shape, z.z_down.shape[1:], z.z_up.shape[1:])
        + [z.wide_scratch, z.wide_scratch, z.zt_scratch, z.sp_scratch]
        + scratch(F32, plane, plane)
        + scratch(BF, plane, plane, plane, plane)
        + scratch(BF, (z.planes,) + plane, forcing.shape)
        + scratch(F32, (tiles, z.planes * KXY // GROUP, LANES))
        + scratch(jnp.int32, slot_column.shape)
        + scratch(BF, w_spec.shape, z.x_part.shape[1:], (z.slabs,) + forced, (z.slabs - 1,) + forced, forced, (z.groups,) + forced)
        + scratch(F32, forced)
        + [dma((n,)) for n in [3, 8, z.channels, 6, 6, 7, 7] + [z.slabs - 1] * 2 + [z.groups - 1] * 2]
        + exchange
        + exchange,
        compiler_params=pltpu.CompilerParams(collective_id=1, has_side_effects=True, vmem_limit_bytes=SPECTRAL_VMEM),
        name="spectral",
    )(skip_gain, bias, *[pltpu.with_memory_space_constraint(v, pltpu.HBM) for v in operands])


def final_call(z, where, skip_gain, value, grad_pre, adjoint, picks):
    return pl.pallas_call(
        functools.partial(final_kernel, z.per_step),
        out_shape=(z.volume, z.volume),
        grid_spec=pltpu.PrefetchScalarGridSpec(
            num_scalar_prefetch=1, grid=(z.steps,),
            in_specs=[SMEM, VMEM, VMEM, VMEM, VMEM, whole(z.x_up.shape), whole(z.y_up.shape), z.z_spec],
            out_specs=(HBM, z.field_spec),
            scratch_shapes=[z.wide_scratch, z.sp_scratch, pltpu.SemaphoreType.DMA((z.channels,))],
        ),
        compiler_params=z.params,
        name="synth_gradient",
    )(where, skip_gain, value, grad_pre, adjoint, picks, z.x_up, z.y_up, z.z_up)


def per_device(slabs, groups, field, forcing, slot_column, w_spec, skip_gain, bias):
    channels, planes, grid_len, _ = field.shape
    capacity = slot_column.shape[1]
    z = Sizes(slabs, groups, channels, planes, grid_len, capacity)
    where = lax.axis_index("slab").astype(jnp.int32).reshape(1)
    value, grad_pre, adjoint, picks = spectral_call(z, field, forcing, slot_column, w_spec, skip_gain, bias)
    return final_call(z, where, skip_gain, value, grad_pre, adjoint, picks)


def solution(mesh):
    placed = (
        P("chan", "slab", None, None),
        P("slab", "chan", None),
        P(),
        P(None, "chan", None, "slab"),
        P("chan"),
        P("chan"),
    )
    slabs, groups = mesh.shape["slab"], mesh.shape["chan"]
    return jax.shard_map(
        functools.partial(per_device, slabs, groups),
        mesh=mesh,
        in_specs=placed,
        out_specs=(P("chan", "slab", None, None), P("chan", "slab", None, None)),
        check_vma=False,
    )
```

```python
import functools
import math

import jax
import jax.numpy as jnp
import ml_dtypes
import numpy as np
from jax import lax
from jax.experimental import pallas as pl
from jax.experimental.pallas import tpu as pltpu
from jax.sharding import PartitionSpec as P

KXY = 32
KZ = 16
MESH = pl.DeviceIdType.MESH
BF = jnp.bfloat16
F32 = jnp.float32
LANES = 128
SPECTRAL_VMEM = 31 << 20
PIECES = 4
HALVES = 2
BIAS_ROWS = 16
GROUP = LANES // KXY


def bf16_table(values):
    return np.asarray(values, np.float32).astype(ml_dtypes.bfloat16)


def trig(freqs, coords, grid_len):
    angle = (np.outer(freqs, coords) % grid_len) * (2.0 * math.pi / grid_len)
    return np.cos(angle), np.sin(angle)


def plane_tables(grid_len):
    freqs = np.arange(KXY) - KXY // 2
    cos, sin = trig(freqs, np.arange(grid_len), grid_len)
    groups = KXY // GROUP
    scale = float(grid_len) ** -1.5
    x_down = np.zeros((GROUP, 2, groups, grid_len))
    x_up = np.zeros((grid_len, GROUP, 2, groups))
    y_down = np.zeros((GROUP, 2, grid_len, 2, GROUP, KXY))
    y_up = np.zeros((2, GROUP, KXY, GROUP, 2, grid_len))
    for k in range(GROUP):
        for g in range(groups):
            jx = g * GROUP + k
            x_down[k, 0, g], x_down[k, 1, g] = cos[jx], sin[jx]
            x_up[:, k, 0, g], x_up[:, k, 1, g] = scale * cos[jx], -scale * sin[jx]
        y_down[k, 0, :, 0, k], y_down[k, 1, :, 0, k] = cos.T, -sin.T
        y_down[k, 0, :, 1, k], y_down[k, 1, :, 1, k] = -sin.T, -cos.T
        y_up[0, k, :, k, 0], y_up[1, k, :, k, 0] = cos, -sin
        y_up[0, k, :, k, 1], y_up[1, k, :, k, 1] = sin, cos
    rows = 2 * KXY
    return (
        bf16_table(x_down.reshape(rows, grid_len)),
        bf16_table(x_up.reshape(grid_len, rows)),
        bf16_table(y_down.reshape(2 * GROUP * grid_len, 2 * LANES)),
        bf16_table(y_up.reshape(2 * LANES, 2 * GROUP * grid_len)),
    )


def depth_tables(channels, planes, slabs, grid_len):
    scale = float(grid_len) ** -1.5
    down, up = [], []
    for s in range(slabs):
        cos, sin = trig(np.arange(KZ), s * planes + np.arange(planes), grid_len)
        parts = [[cos, sin], [-sin, cos]]
        for store, count in ((down, channels // HALVES), (up, channels)):
            full = np.zeros((2, count, KZ, 2, count, planes))
            for q in range(2):
                for r in range(2):
                    full[q, :, :, r] = np.einsum("cd,mz->cmdz", np.eye(count), parts[q][r])
            full = full.reshape(2, count, PIECES, KZ // PIECES, -1).transpose(2, 0, 1, 3, 4)
            full = full.reshape(2 * count * KZ, 2 * count * planes)
            table = full * scale if store is down else full.T
            high = bf16_table(table)
            low = bf16_table(table - high.astype(np.float64))
            store.append(np.concatenate([high, low], axis=1))
    return np.stack(down), np.stack(up)


def dot(a, b):
    return jnp.dot(a, b, preferred_element_type=F32)


def dot_nt(a, b):
    return lax.dot_general(a, b, (((1,), (1,)), ((), ())), preferred_element_type=F32)


def twice(block):
    return jnp.concatenate([block, block], axis=0)


def tile_rows(plane):
    groups = KXY // GROUP
    return pl.ds(pl.multiple_of(plane * groups, groups), groups)


def keep_x_rows(xs_ref, plane, value):
    groups = KXY // GROUP
    tiles = value.shape[1] // LANES
    for kp in range(2 * GROUP):
        for h in range(tiles):
            xs_ref[kp * tiles + h, tile_rows(plane), :] = value[kp * groups : (kp + 1) * groups, h * LANES : (h + 1) * LANES]


def plane_rows(ws_ref, plane, width):
    tiles = width // LANES
    columns = []
    for h in range(tiles):
        parts = [ws_ref[kp * tiles + h, tile_rows(plane), :] for kp in range(2 * GROUP)]
        columns.append(jnp.concatenate(parts, axis=0))
    return jnp.concatenate(columns, axis=1)


def local_spectra(xs_ref, y_down_ref, z_down, zt_ref, sp_ref, start, count):
    groups = KXY // GROUP
    rows = slice(start * groups, (start + count) * groups)
    half = zt_ref.shape[0] // 2
    lhs = jnp.concatenate([xs_ref[j, rows, :].astype(BF) for j in range(xs_ref.shape[0])], axis=1)
    spectra = dot(lhs, y_down_ref[...])
    for q in range(2):
        sp_ref[q, : count * groups, :] = spectra[:, q * LANES : (q + 1) * LANES]
    if count < half:
        zt_ref[...] = jnp.zeros_like(zt_ref)
    for g in range(groups):
        for q in range(2):
            part = sp_ref[q, pl.ds(g, count, stride=groups), :]
            zt_ref[q * half : q * half + count, g * LANES : (g + 1) * LANES] = part.astype(BF)
    return dot(z_down, twice(zt_ref[...]))


def slot_pairs(slab, slabs):
    return [(lax.rem(slab + d, slabs), lax.rem(slab + d + 1, slabs)) for d in range(1, slabs, 2)]


def pack_half(coeffs, pick_ref, pairs, packed_ref, h, sends):
    rows = coeffs.shape[0]
    capacity = packed_ref.shape[2]
    for i, targets in enumerate(pairs):
        part = dot(coeffs, pick_ref[:, 2 * i * capacity : 2 * (i + 1) * capacity]).astype(BF)
        for n, t in enumerate(targets):
            packed_ref[t, h * rows : (h + 1) * rows, :] = part[:, n * capacity : (n + 1) * capacity]
            if 2 * i + n < len(sends):
                sends[2 * i + n].start()


def synthesis_head(slab, recv_ref, pick_ref, z_up, y_up_ref, sp_ref, ws_ref):
    groups = KXY // GROUP
    rows = ws_ref.shape[1]
    planes_all = rows // groups
    slabs = recv_ref.shape[0]
    by_slot = jnp.concatenate([recv_ref[t] for pair in slot_pairs(slab, slabs) for t in pair], axis=1)
    chunk = 2 * LANES
    spectra = dot_nt(pick_ref[...], by_slot).astype(BF)
    spectra = jnp.concatenate([spectra, spectra], axis=1)
    for n in range(KXY * KXY // chunk):
        planes = dot_nt(z_up, spectra[n * chunk : (n + 1) * chunk])
        for gg in range(2):
            for q in range(2):
                sp_ref[q, pl.ds(2 * n + gg, planes_all, stride=groups), :] = planes[
                    q * planes_all : (q + 1) * planes_all, gg * LANES : (gg + 1) * LANES
                ]
    lhs = jnp.concatenate([sp_ref[q, :rows, :].astype(BF) for q in range(2)], axis=1)
    for j in range(ws_ref.shape[0] // 2):
        wide = dot(lhs, y_up_ref[:, j * chunk : (j + 1) * chunk])
        ws_ref[2 * j] = wide[:, :LANES]
        ws_ref[2 * j + 1] = wide[:, LANES:]


def gelu_pair(half):
    coeff = math.sqrt(2.0 / math.pi)
    square = half * half
    tangent = jnp.tanh(half * (2.0 * coeff + (8.0 * 0.044715 * coeff) * square))
    turned = half * tangent
    value = half + turned
    inner = 0.5 + (half - turned) * (coeff + (12.0 * 0.044715 * coeff) * square)
    return value, (value * (1.0 + tangent)) * inner


def final_kernel(per_step, slab_ref, gain_ref, value_ref, grad_ref, recv_ref, pick_ref, x_up_ref, y_up_ref, z_up_ref, value_hbm, out_ref, ws_ref, sp_ref, value_sem):
    step = pl.program_id(0)
    channels, planes = grad_ref.shape[:2]
    grid_len = grad_ref.shape[2]
    copies = [pltpu.make_async_copy(value_ref.at[c], value_hbm.at[c], value_sem.at[c]) for c in range(channels)]

    @pl.when(step == 0)
    def _():
        for copy in copies:
            copy.start()
        synthesis_head(slab_ref[0], recv_ref, pick_ref, z_up_ref[0], y_up_ref, sp_ref, ws_ref)

    def body(zz, carry):
        for c in range(channels):
            wp = plane_rows(ws_ref, c * planes + step * per_step + zz, grid_len).astype(BF)
            out_ref[c, zz] = (dot(x_up_ref[...], wp) + gain_ref[c] * grad_ref[c, step * per_step + zz].astype(F32)).astype(BF)
        return carry

    lax.fori_loop(0, per_step, body, 0)

    @pl.when(step == pl.num_programs(0) - 1)
    def _():
        for copy in copies:
            copy.wait()


def announce(targets):
    barrier = pltpu.get_barrier_semaphore()
    for target in targets:
        pl.semaphore_signal(barrier, inc=1, device_id=target, device_id_type=MESH)


def await_peers(targets):
    pl.semaphore_wait(pltpu.get_barrier_semaphore(), len(targets))


def reorder_weights(w_ref, wide_ref):
    width = w_ref.shape[3]
    slots = width // KZ
    flat = w_ref[...].reshape(-1, width)
    chunk = 2 * slots

    def body(n, carry):
        source = lax.broadcasted_iota(jnp.int32, (width, chunk), 0)
        lane = lax.broadcasted_iota(jnp.int32, (1, chunk), 1)
        wanted = jnp.where(lane < slots, lane * KZ, (lane - slots) * KZ + 1) + 2 * n
        moved = dot(flat, (source == wanted).astype(F32).astype(BF)).astype(BF)
        wide_ref[:, :, :, pl.ds(pl.multiple_of(n * chunk, chunk), chunk)] = moved.reshape(w_ref.shape[:3] + (chunk,))
        return carry

    lax.fori_loop(0, width // chunk, body, 0)


def peers_of(slabs, groups):
    slab, chan = lax.axis_index("slab"), lax.axis_index("chan")
    slab_peer = [(lax.rem(slab + d, slabs), chan) for d in range(1, slabs)]
    chan_peer = [(slab, lax.rem(chan + d, groups)) for d in range(1, groups)]
    return slab, chan, slab_peer, chan_peer


def spectra_copies(packed_ref, rx, peers, h, s_send, s_recv):
    rows = packed_ref.shape[1] // HALVES
    part = pl.ds(h * rows, rows)
    copies = []
    for d, peer in enumerate(peers):
        n = h * len(peers) + d
        copies.append(pltpu.make_async_remote_copy(
            src_ref=packed_ref.at[peer[0], part], dst_ref=rx.at[d, part], send_sem=s_send.at[n], recv_sem=s_recv.at[n],
            device_id=peer, device_id_type=MESH,
        ))
    return copies


def middle_part(slabs, groups, rows, gain_ref, bias_ref, recv_ref, wide_ref, pick_ref, x_down_ref, x_up_ref, y_down_ref, y_up_ref, z_down_ref, z_up_ref,
                out_ref, grad_ref, adjoint_ref, xs_ref, ws_ref, zt_ref, sp_ref, sa_ref, sb_ref, ga_ref, gb_ref, ma_ref, mb_ref, packed_ref, rx, tx2, rx2, mine, stage, *sems):
    slab, _, slab_peer, _ = peers_of(slabs, groups)
    channels, planes, grid_len, _ = out_ref.shape
    count = channels * planes
    synthesis_head(slab, recv_ref, pick_ref, z_up_ref[...], y_up_ref, sp_ref, ws_ref)

    def synth(t, s_ref, m_ref):
        c = t // planes
        m_ref[...] = out_ref[c, t - c * planes]
        shift = jnp.full((BIAS_ROWS, grid_len), 0.5 * bias_ref[c], F32)
        high = shift.astype(BF).astype(F32)
        row = lax.broadcasted_iota(jnp.int32, shift.shape, 0)
        shift = jnp.where(row == 0, high, jnp.where(row == 1, shift - high, 0.0))
        s_ref[...] = dot(x_up_ref[...], jnp.concatenate([plane_rows(ws_ref, t, grid_len), shift], axis=0).astype(BF))

    def point(t, s_ref, m_ref, g_ref):
        c = t // planes
        zz = t - c * planes
        gain = 0.5 * gain_ref[c]
        for start in range(0, grid_len, rows):
            span = slice(start, start + rows)
            value, grad = gelu_pair(s_ref[span, :] + gain * m_ref[span, :].astype(F32))
            grad = grad.astype(BF)
            out_ref[c, zz, span, :] = value.astype(BF)
            grad_ref[c, zz, span, :] = grad
            g_ref[span, :] = grad

    def down(t, g_ref):
        keep_x_rows(xs_ref, t, dot(x_down_ref[...], g_ref[...]))

    gb_ref[...] = jnp.zeros_like(gb_ref)
    synth(0, sa_ref, ma_ref)

    def body(j, carry):
        t = 2 * j
        synth(t + 1, sb_ref, mb_ref)
        down(jnp.maximum(t - 1, 0), gb_ref)
        point(t, sa_ref, ma_ref, ga_ref)
        synth(jnp.minimum(t + 2, count - 1), sa_ref, ma_ref)
        down(t, ga_ref)
        point(t + 1, sb_ref, mb_ref, gb_ref)
        return carry

    part = count // HALVES
    first = [spectra_copies(packed_ref, rx, slab_peer, h, *sems[:2]) for h in range(HALVES)]
    for h in range(HALVES):
        lax.fori_loop(h * part // 2, (h + 1) * part // 2, body, 0)
        down((h + 1) * part - 1, gb_ref)
        coeffs = local_spectra(xs_ref, y_down_ref, z_down_ref[...], zt_ref, sp_ref, h * part, part).astype(BF)
        pack_half(coeffs, pick_ref, slot_pairs(slab, slabs), packed_ref, h, first[h])
    exchange_body(slabs, groups, False, first, packed_ref, wide_ref, adjoint_ref, rx, tx2, rx2, mine, stage, *sems)


def exchange_body(slabs, groups, forward, first, packed_ref, wide_ref, recv_ref, rx, tx2, rx2, mine, stage, s_send, s_recv, c_send, c_recv, g_send, g_recv, shared=None, filler=None):
    slab, chan, slab_peer, chan_peer = peers_of(slabs, groups)
    rows, slots = packed_ref.shape[1] // PIECES, packed_ref.shape[2]
    kept = KZ // PIECES
    own = rx2.shape[1] // 2
    some = own // HALVES
    pairs = 2 * own
    outputs = own * groups
    wide = kept * slots
    step = min(kept, 4)

    def factor(piece, m):
        return 1.0 if piece == 0 and m == 0 else 2.0

    def at_m(piece, m, count=1):
        return slice((piece * kept + m) * slots, (piece * kept + m + count) * slots)

    def part_rows(h, q):
        return slice((2 * h + q) * some, (2 * h + q + 1) * some)

    half = packed_ref.shape[1] // HALVES
    for h in range(HALVES):
        span = slice(h * half, (h + 1) * half)
        total = packed_ref[slab, span, :].astype(F32)
        for d in range(1, slabs):
            first[h][d - 1].wait_recv()
            total = total + rx[d - 1, span, :].astype(F32)
        stage[span, :] = total
    common = None if shared is None else shared()
    second = []
    for p in range(PIECES):
        tiles = []
        for m in range(kept):
            base = [h * half + p * (half // PIECES) + m for h in range(HALVES)]
            tile = jnp.concatenate([stage[pl.ds(at, 2 * some, stride=kept), :] for at in base], axis=0)
            if common is not None:
                both = [common[(2 * p + q) * kept + m : (2 * p + q) * kept + m + 1, :] for q in range(2)]
                tile = tile + jnp.concatenate([jnp.broadcast_to(b, (some, slots)) for b in both] * HALVES, axis=0)
            tiles.append(tile)
        if forward:
            for m in range(0, kept, step):
                at = at_m(p, m, step)
                u = jnp.concatenate(tiles[m : m + step], axis=1)
                real = jnp.zeros((outputs, step * slots), F32)
                imag = jnp.zeros((outputs, step * slots), F32)
                for c in range(own):
                    w0, w1 = wide_ref[0, c, :, at].astype(F32), wide_ref[1, c, :, at].astype(F32)
                    h, k = c // some, c % some
                    ur, ui = u[2 * h * some + k : 2 * h * some + k + 1], u[(2 * h + 1) * some + k : (2 * h + 1) * some + k + 1]
                    real = real + (w0 * ur - w1 * ui)
                    imag = imag + (w1 * ur + w0 * ui)
                for e in range(groups):
                    mine_rows = slice(e * own, (e + 1) * own)
                    tx2[e, :, at] = jnp.concatenate([real[mine_rows], imag[mine_rows]], axis=0).astype(BF)
        else:
            for m in range(kept):
                tx2[0, :, at_m(p, m)] = (tiles[m] * factor(p, m)).astype(BF)
        lanes = pl.ds(p * wide, wide)
        copies = []
        for d in range(1, groups):
            peer = chan_peer[d - 1]
            n = p * (groups - 1) + d - 1
            copy = pltpu.make_async_remote_copy(
                src_ref=tx2.at[peer[1] if forward else 0, :, lanes], dst_ref=rx2.at[chan, :, lanes], send_sem=c_send.at[n], recv_sem=c_recv.at[n],
                device_id=peer, device_id_type=MESH,
            )
            copy.start()
            copies.append(copy)
        rx2[chan, :, lanes] = tx2[chan if forward else 0, :, lanes]
        second.append(copies)
    third = []
    for p in range(PIECES):
        for copy in second[p]:
            copy.wait_recv()
        for m in range(0, kept, step):
            at = at_m(p, m, step)
            if forward:
                result = rx2[0, :, at].astype(F32)
                for e in range(1, groups):
                    result = result + rx2[e, :, at].astype(F32)
            else:
                blocks = [rx2[e, :, at].astype(F32) for e in range(groups)]
                real = jnp.concatenate([b[part_rows(h, 0)] for b in blocks for h in range(HALVES)], axis=0)
                imag = jnp.concatenate([b[part_rows(h, 1)] for b in blocks for h in range(HALVES)], axis=0)
                reals, imags = [], []
                for c in range(own):
                    w0, w1 = wide_ref[0, c, :, at].astype(F32), wide_ref[1, c, :, at].astype(F32)
                    reals.append(jnp.sum(w0 * real + w1 * imag, axis=0, keepdims=True))
                    imags.append(jnp.sum(w0 * imag - w1 * real, axis=0, keepdims=True))
                result = jnp.concatenate(reals + imags, axis=0)
            for k in range(step):
                part = result[:, k * slots : (k + 1) * slots]
                stage[pl.ds(p * rows + m + k, pairs, stride=kept), :] = part * factor(p, m + k) if forward else part
        part = pl.ds(p * rows, rows)
        mine[part, :] = stage[part, :].astype(BF)
        for d in range(1, slabs):
            n = p * (slabs - 1) + d - 1
            copy = pltpu.make_async_remote_copy(
                src_ref=mine.at[part], dst_ref=recv_ref.at[slab, part], send_sem=g_send.at[n], recv_sem=g_recv.at[n],
                device_id=slab_peer[d - 1], device_id_type=MESH,
            )
            copy.start()
            third.append(copy)
    recv_ref[slab] = mine[...]
    if filler is not None:
        filler()
    for copy in third:
        copy.wait_recv()
    for copy in sum(first, []) + sum(second, []) + third:
        copy.wait_send()


def front_part(slabs, groups, field_hbm, forcing_hbm, slots_hbm, w_hbm, x_down_hbm, x_part_hbm, y_down_hbm, z_down_hbm, later, recv_ref, merged_ref, wide_ref, pick_ref,
               plane_ref, own_ref, xs_ref, xf_ref, zt_ref, sp_ref, packed_ref, rx, tx2, rx2, mine, stage, slot_ref, w_ref, x_down_ref, x_part_ref, y_down_ref, z_down_ref,
                 f_packed, f_rx, f_mine, f_rx2, f_sum, in_sem, field_sem, x_send, x_recv, p_send, p_recv, f_send, f_recv, h_send, h_recv, *sems):
    slab, chan, slab_peer, chan_peer = peers_of(slabs, groups)
    channels, planes = merged_ref.shape[:2]
    height = forcing_hbm.shape[1]
    chips = groups // 2
    chip, core = chan // 2, lax.rem(chan, 2)
    partner = (slab, chan + 1 - 2 * core)

    def near(t):
        return 2 * lax.rem(chip + chips + t, chips) + core

    def rows(index, start, count):
        return plane_ref.at[pl.ds(start, count), pl.ds(pl.multiple_of(index * height, height), height), :]

    fields = [pltpu.make_async_copy(field_hbm.at[c], merged_ref.at[c], field_sem.at[c]) for c in range(channels)]
    small = [
        pltpu.make_async_copy(forcing_hbm, own_ref, in_sem.at[0]),
        pltpu.make_async_copy(x_part_hbm.at[chan], x_part_ref, in_sem.at[1]),
        pltpu.make_async_copy(y_down_hbm, y_down_ref, in_sem.at[2]),
        pltpu.make_async_copy(z_down_hbm.at[slab], z_down_ref, in_sem.at[3]),
        pltpu.make_async_copy(slots_hbm, slot_ref, in_sem.at[4]),
        pltpu.make_async_copy(x_down_hbm, x_down_ref, in_sem.at[5]),
    ]
    load_w = pltpu.make_async_copy(w_hbm, w_ref, in_sem.at[6])
    place_own = pltpu.make_async_copy(forcing_hbm, rows(chan, 0, planes), in_sem.at[7])
    for copy in small + fields + [load_w, place_own] + later:
        copy.start()
    announce(slab_peer + chan_peer)
    for copy in small:
        copy.wait()

    def forcing_body(zz, carry):
        keep_x_rows(xf_ref, zz, dot(x_part_ref[...], own_ref[zz]))
        return carry

    lax.fori_loop(0, planes, forcing_body, 0, unroll=4)
    padded = local_spectra(xf_ref, y_down_ref, z_down_ref[...], zt_ref, sp_ref, 0, planes)
    kept = KZ // PIECES
    block = channels // HALVES * kept
    forced = jnp.concatenate([padded[n * block : n * block + kept] for n in range(2 * PIECES)], axis=0).astype(BF)
    columns = forced.shape[1]
    capacity = packed_ref.shape[2]
    pairs = slot_pairs(slab, slabs)
    for i, targets in enumerate(pairs):
        column = lax.broadcasted_iota(jnp.int32, (columns, 2 * capacity), 0)
        pick = (column == jnp.concatenate([slot_ref[pl.ds(t, 1), :] for t in targets], axis=1)).astype(F32).astype(BF)
        pick_ref[:, 2 * i * capacity : 2 * (i + 1) * capacity] = pick
        part = dot(forced, pick).astype(BF)
        for n, t in enumerate(targets):
            f_packed[t] = part[:, n * capacity : (n + 1) * capacity]
    await_peers(slab_peer + chan_peer)
    sent = []

    def send(copies):
        for copy in copies:
            copy.start()
            sent.append(copy)
        return copies

    forced_in = send([
        pltpu.make_async_remote_copy(
            src_ref=f_packed.at[slab_peer[d - 1][0]], dst_ref=f_rx.at[d - 1], send_sem=f_send.at[d - 1], recv_sem=f_recv.at[d - 1],
            device_id=slab_peer[d - 1], device_id_type=MESH,
        )
        for d in range(1, slabs)
    ])

    half = planes // 2

    def across(index, start, to, n, source=None):
        return pltpu.make_async_remote_copy(
            src_ref=rows(index, start, half) if source is None else source, dst_ref=rows(index, start, half),
            send_sem=x_send.at[n], recv_sem=x_recv.at[n], device_id=(slab, to), device_id_type=MESH,
        )

    def beside(index, start, count, n, source=None):
        return pltpu.make_async_remote_copy(
            src_ref=rows(index, start, count) if source is None else source, dst_ref=rows(index, start, count),
            send_sem=p_send.at[n], recv_sem=p_recv.at[n], device_id=partner, device_id_type=MESH,
        )

    def x_pass(c):
        fields[c].wait()

        def body(zz, carry):
            keep_x_rows(xs_ref, c * planes + zz, dot(x_down_ref[...], merged_ref[c, zz]))
            return carry

        lax.fori_loop(0, planes, body, 0, unroll=4)

    low, high = own_ref.at[pl.ds(0, half)], own_ref.at[pl.ds(half, half)]
    right_low, left_high, right_high, left_low = send([
        across(chan, 0, near(1), 0, low), across(chan, half, near(-1), 1, high),
        across(chan, half, near(1), 2, high), across(chan, 0, near(-1), 3, low),
    ])
    beside_all = send([beside(chan, 0, planes, 0, own_ref)])
    first = [spectra_copies(packed_ref, rx, slab_peer, h, *sems[:2]) for h in range(HALVES)]
    part = channels // HALVES

    def send_half(h):
        for c in range(h * part, (h + 1) * part):
            x_pass(c)
        coeffs = local_spectra(xs_ref, y_down_ref, z_down_ref[...], zt_ref, sp_ref, h * part * planes, part * planes).astype(BF)
        pack_half(coeffs, pick_ref, pairs, packed_ref, h, first[h])

    send_half(0)
    total = f_packed[slab].astype(F32)
    for d in range(1, slabs):
        forced_in[d - 1].wait_recv()
        total = total + f_rx[d - 1].astype(F32)
    f_mine[...] = total.astype(BF)
    shared_in = send([
        pltpu.make_async_remote_copy(
            src_ref=f_mine, dst_ref=f_rx2.at[chan], send_sem=h_send.at[d - 1], recv_sem=h_recv.at[d - 1],
            device_id=chan_peer[d - 1], device_id_type=MESH,
        )
        for d in range(1, groups)
    ])
    f_rx2[chan] = f_mine[...]
    right_low.wait_recv()
    left_high.wait_recv()
    far_low, far_high = send([across(near(-1), 0, near(1), 4), across(near(1), half, near(-1), 5)])
    beside_all += send([beside(near(-1), 0, half, 1), beside(near(1), half, half, 2)])
    for h in range(1, HALVES):
        send_half(h)
    right_high.wait_recv()
    left_low.wait_recv()
    beside_all += send([beside(near(-1), half, half, 3), beside(near(1), 0, half, 4)])
    load_w.wait()
    reorder_weights(w_ref, wide_ref)
    far_low.wait_recv()
    far_high.wait_recv()
    beside_all += send([beside(near(2), 0, half, 5), beside(near(2), half, half, 6)])

    def shared():
        for copy in shared_in:
            copy.wait_recv()
        common = f_rx2[0].astype(F32)
        for e in range(1, groups):
            common = common + f_rx2[e].astype(F32)
        f_sum[...] = common
        return f_sum

    def merge():
        place_own.wait()
        for copy in beside_all:
            copy.wait_recv()

        def body(zz, carry):
            for c in range(channels):
                merged_ref[c, zz] = merged_ref[c, zz] + plane_ref[zz]
            return carry

        lax.fori_loop(0, planes, body, 0)

    exchange_body(slabs, groups, True, first, packed_ref, wide_ref, recv_ref, rx, tx2, rx2, mine, stage, *sems, shared=shared, filler=merge)
    for copy in sent:
        copy.wait_send()
    for copy in later:
        copy.wait()


def spectral_kernel(slabs, groups, rows, gain_hbm, bias_hbm, field_hbm, forcing_hbm, slots_hbm, w_hbm, x_down_hbm, x_part_hbm, y_down_hbm, z_down_hbm, x_up_hbm, y_up_hbm, z_up_hbm,
                    out_ref, grad_ref, adjoint_ref, pick_ref, recv_ref, wide_ref, x_down_ref, x_up_ref, y_down_ref, y_up_ref, z_down_ref, z_up_ref,
                    xs_ref, ws_ref, zt_ref, sp_ref, sa_ref, sb_ref, ga_ref, gb_ref, ma_ref, mb_ref,
                    plane_ref, own_ref, xf_ref, slot_ref, w_ref, x_part_ref, f_packed, f_rx, f_mine, f_rx2, f_sum, gain_ref, bias_ref, later_sem, in_sem, field_sem, x_send, x_recv, p_send, p_recv, f_send, f_recv, h_send, h_recv, *rest):
    forward, adjoint = rest[:12], rest[12:]
    later = [
        pltpu.make_async_copy(x_up_hbm, x_up_ref, later_sem.at[0]),
        pltpu.make_async_copy(y_up_hbm, y_up_ref, later_sem.at[1]),
        pltpu.make_async_copy(z_up_hbm.at[lax.axis_index("slab")], z_up_ref, later_sem.at[2]),
        pltpu.make_async_copy(gain_hbm, gain_ref, later_sem.at[3]),
        pltpu.make_async_copy(bias_hbm, bias_ref, later_sem.at[4]),
    ]
    packed_ref, rx, tx2, rx2, mine, stage = forward[:6]
    front_part(slabs, groups, field_hbm, forcing_hbm, slots_hbm, w_hbm, x_down_hbm, x_part_hbm, y_down_hbm, z_down_hbm, later, recv_ref, out_ref, wide_ref, pick_ref,
               plane_ref, own_ref, xs_ref, xf_ref, zt_ref, sp_ref, packed_ref, rx, tx2, rx2, mine, stage, slot_ref, w_ref, x_down_ref, x_part_ref, y_down_ref, z_down_ref,
               f_packed, f_rx, f_mine, f_rx2, f_sum, in_sem, field_sem, x_send, x_recv, p_send, p_recv, f_send, f_recv, h_send, h_recv, *forward[6:])
    middle_part(slabs, groups, rows, gain_ref, bias_ref, recv_ref, wide_ref, pick_ref, x_down_ref, x_up_ref, y_down_ref, y_up_ref, z_down_ref, z_up_ref,
                out_ref, grad_ref, adjoint_ref, xs_ref, ws_ref, zt_ref, sp_ref, sa_ref, sb_ref, ga_ref, gb_ref, ma_ref, mb_ref, *adjoint)


def whole(shape):
    zeros = (0,) * len(shape)
    return pl.BlockSpec(shape, lambda *_: zeros, pipeline_mode=pl.Buffered(1))


class Sizes:
    def __init__(self, slabs, groups, channels, planes, grid_len, capacity):
        self.slabs, self.groups = slabs, groups
        self.channels, self.planes, self.grid_len = channels, planes, grid_len
        self.capacity = capacity
        planes_all = channels * planes
        x_down, x_up, y_down, y_up = plane_tables(grid_len)
        ones = np.zeros((grid_len, BIAS_ROWS), x_up.dtype)
        ones[:, :2] = 1
        half = bf16_table(0.5 * x_up.astype(np.float32))
        self.x_down, self.x_up, self.y_down, self.y_up = [jnp.asarray(t) for t in (x_down, x_up, y_down, y_up)]
        self.x_part = jnp.asarray(x_down.reshape(2 * KXY, groups, -1).transpose(1, 0, 2))
        self.x_up_half = jnp.asarray(np.concatenate([half, ones], axis=1))
        self.z_down, self.z_up = [jnp.asarray(t) for t in depth_tables(channels, planes, slabs, grid_len)]
        self.per_step = 4
        per_step = self.per_step
        self.steps = planes // per_step
        self.field_spec = pl.BlockSpec((channels, per_step, grid_len, grid_len), lambda i, s: (0, i, 0, 0))
        self.z_spec = pl.BlockSpec((1,) + self.z_up.shape[1:], lambda i, s: (s[0], 0, 0), pipeline_mode=pl.Buffered(1))
        self.packed_shape = (slabs, 2 * channels * KZ, capacity)
        self.volume = jax.ShapeDtypeStruct((channels, planes, grid_len, grid_len), BF)
        self.packed_out = jax.ShapeDtypeStruct(self.packed_shape, BF)
        self.wide_scratch = pltpu.VMEM((2 * GROUP * grid_len // LANES, planes_all * KXY // GROUP, LANES), F32)
        dma = pltpu.SemaphoreType.DMA
        self.exchange_sems = [dma((n,)) for n in [HALVES * (slabs - 1)] * 2 + [PIECES * (groups - 1)] * 2 + [PIECES * (slabs - 1)] * 2]
        self.sp_scratch = pltpu.VMEM((2, planes_all * KXY // GROUP, LANES), F32)
        self.zt_scratch = pltpu.VMEM((2 * planes_all // HALVES, KXY * KXY), BF)
        self.params = pltpu.CompilerParams(dimension_semantics=("arbitrary",), vmem_limit_bytes=14 << 20)


SMEM = pl.BlockSpec(memory_space=pltpu.SMEM)
VMEM = pl.BlockSpec(memory_space=pltpu.VMEM)
HBM = pl.BlockSpec(memory_space=pltpu.HBM)


def spectral_call(z, field, forcing, slot_column, w_spec, skip_gain, bias):
    block = z.packed_shape[1:]
    pair = (z.groups, 2 * z.channels, z.capacity * KZ)
    tiles = 2 * GROUP * z.grid_len // LANES
    forced = (2 * KZ, z.capacity)
    plane = (z.grid_len, z.grid_len)
    dma = pltpu.SemaphoreType.DMA
    operands = (skip_gain, bias, field, forcing, slot_column, w_spec, z.x_down, z.x_part, z.y_down, z.z_down, z.x_up_half, z.y_up, z.z_up)

    def scratch(kind, *shapes):
        return [pltpu.VMEM(shape, kind) for shape in shapes]

    exchange = scratch(BF, z.packed_shape, (z.slabs - 1,) + block, pair, pair, block) + scratch(F32, block) + z.exchange_sems
    return pl.pallas_call(
        functools.partial(spectral_kernel, z.slabs, z.groups, 64),
        out_shape=(z.volume, z.volume, z.packed_out, jax.ShapeDtypeStruct((KXY * KXY, slot_column.size), BF)),
        in_specs=[HBM] * len(operands),
        out_specs=(VMEM, VMEM, VMEM, VMEM),
        scratch_shapes=scratch(BF, z.packed_shape, w_spec.shape, z.x_down.shape, z.x_up_half.shape, z.y_down.shape, z.y_up.shape, z.z_down.shape[1:], z.z_up.shape[1:])
        + [z.wide_scratch, z.wide_scratch, z.zt_scratch, z.sp_scratch]
        + scratch(F32, plane, plane)
        + scratch(BF, plane, plane, plane, plane)
        + scratch(BF, (z.planes,) + plane, forcing.shape)
        + scratch(F32, (tiles, z.planes * KXY // GROUP, LANES))
        + scratch(jnp.int32, slot_column.shape)
        + scratch(BF, w_spec.shape, z.x_part.shape[1:], (z.slabs,) + forced, (z.slabs - 1,) + forced, forced, (z.groups,) + forced)
        + scratch(F32, forced)
        + [pltpu.SMEM((z.channels,), F32)] * 2
        + [dma((n,)) for n in [5, 8, z.channels, 6, 6, 7, 7] + [z.slabs - 1] * 2 + [z.groups - 1] * 2]
        + exchange
        + exchange,
        compiler_params=pltpu.CompilerParams(collective_id=1, has_side_effects=True, vmem_limit_bytes=SPECTRAL_VMEM),
        name="spectral",
    )(*[pltpu.with_memory_space_constraint(v, pltpu.HBM) for v in operands])


def final_call(z, where, skip_gain, value, grad_pre, adjoint, picks):
    return pl.pallas_call(
        functools.partial(final_kernel, z.per_step),
        out_shape=(z.volume, z.volume),
        grid_spec=pltpu.PrefetchScalarGridSpec(
            num_scalar_prefetch=1, grid=(z.steps,),
            in_specs=[SMEM, VMEM, VMEM, VMEM, VMEM, whole(z.x_up.shape), whole(z.y_up.shape), z.z_spec],
            out_specs=(HBM, z.field_spec),
            scratch_shapes=[z.wide_scratch, z.sp_scratch, pltpu.SemaphoreType.DMA((z.channels,))],
        ),
        compiler_params=z.params,
        name="synth_gradient",
    )(where, skip_gain, value, grad_pre, adjoint, picks, z.x_up, z.y_up, z.z_up)


def per_device(slabs, groups, field, forcing, slot_column, w_spec, skip_gain, bias):
    channels, planes, grid_len, _ = field.shape
    capacity = slot_column.shape[1]
    z = Sizes(slabs, groups, channels, planes, grid_len, capacity)
    where = lax.axis_index("slab").astype(jnp.int32).reshape(1)
    value, grad_pre, adjoint, picks = spectral_call(z, field, forcing, slot_column, w_spec, skip_gain, bias)
    return final_call(z, where, skip_gain, value, grad_pre, adjoint, picks)


def solution(mesh):
    placed = (
        P("chan", "slab", None, None),
        P("slab", "chan", None),
        P(),
        P(None, "chan", None, "slab"),
        P("chan"),
        P("chan"),
    )
    slabs, groups = mesh.shape["slab"], mesh.shape["chan"]
    return jax.shard_map(
        functools.partial(per_device, slabs, groups),
        mesh=mesh,
        in_specs=placed,
        out_specs=(P("chan", "slab", None, None), P("chan", "slab", None, None)),
        check_vma=False,
    )
```

```python
import functools
import math

import jax
import jax.numpy as jnp
import ml_dtypes
import numpy as np
from jax import lax
from jax.experimental import pallas as pl
from jax.experimental.pallas import tpu as pltpu
from jax.sharding import PartitionSpec as P

KXY = 32
KZ = 16
MESH = pl.DeviceIdType.MESH
BF = jnp.bfloat16
F32 = jnp.float32
LANES = 128
SPECTRAL_VMEM = 31 << 20
PIECES = 4
HALVES = 2
BIAS_ROWS = 16
GROUP = LANES // KXY


def bf16_table(values):
    return np.asarray(values, np.float32).astype(ml_dtypes.bfloat16)


def trig(freqs, coords, grid_len):
    angle = (np.outer(freqs, coords) % grid_len) * (2.0 * math.pi / grid_len)
    return np.cos(angle), np.sin(angle)


def plane_tables(grid_len):
    freqs = np.arange(KXY) - KXY // 2
    cos, sin = trig(freqs, np.arange(grid_len), grid_len)
    groups = KXY // GROUP
    scale = float(grid_len) ** -1.5
    x_down = np.zeros((GROUP, 2, groups, grid_len))
    x_up = np.zeros((grid_len, GROUP, 2, groups))
    y_down = np.zeros((GROUP, 2, grid_len, 2, GROUP, KXY))
    y_up = np.zeros((2, GROUP, KXY, GROUP, 2, grid_len))
    for k in range(GROUP):
        for g in range(groups):
            jx = g * GROUP + k
            x_down[k, 0, g], x_down[k, 1, g] = cos[jx], sin[jx]
            x_up[:, k, 0, g], x_up[:, k, 1, g] = scale * cos[jx], -scale * sin[jx]
        y_down[k, 0, :, 0, k], y_down[k, 1, :, 0, k] = cos.T, -sin.T
        y_down[k, 0, :, 1, k], y_down[k, 1, :, 1, k] = -sin.T, -cos.T
        y_up[0, k, :, k, 0], y_up[1, k, :, k, 0] = cos, -sin
        y_up[0, k, :, k, 1], y_up[1, k, :, k, 1] = sin, cos
    rows = 2 * KXY
    return (
        bf16_table(x_down.reshape(rows, grid_len)),
        bf16_table(x_up.reshape(grid_len, rows)),
        bf16_table(y_down.reshape(2 * GROUP * grid_len, 2 * LANES)),
        bf16_table(y_up.reshape(2 * LANES, 2 * GROUP * grid_len)),
    )


def depth_tables(channels, planes, slabs, grid_len):
    scale = float(grid_len) ** -1.5
    down, up = [], []
    for s in range(slabs):
        cos, sin = trig(np.arange(KZ), s * planes + np.arange(planes), grid_len)
        parts = [[cos, sin], [-sin, cos]]
        for store, count in ((down, channels // HALVES), (up, channels)):
            full = np.zeros((2, count, KZ, 2, count, planes))
            for q in range(2):
                for r in range(2):
                    full[q, :, :, r] = np.einsum("cd,mz->cmdz", np.eye(count), parts[q][r])
            full = full.reshape(2, count, PIECES, KZ // PIECES, -1).transpose(2, 0, 1, 3, 4)
            full = full.reshape(2 * count * KZ, 2 * count * planes)
            table = full * scale if store is down else full.T
            high = bf16_table(table)
            low = bf16_table(table - high.astype(np.float64))
            store.append(np.concatenate([high, low], axis=1))
    return np.stack(down), np.stack(up)


def dot(a, b):
    return jnp.dot(a, b, preferred_element_type=F32)


def dot_nt(a, b):
    return lax.dot_general(a, b, (((1,), (1,)), ((), ())), preferred_element_type=F32)


def twice(block):
    return jnp.concatenate([block, block], axis=0)


def tile_rows(plane):
    groups = KXY // GROUP
    return pl.ds(pl.multiple_of(plane * groups, groups), groups)


def keep_x_rows(xs_ref, plane, value):
    groups = KXY // GROUP
    tiles = value.shape[1] // LANES
    for kp in range(2 * GROUP):
        for h in range(tiles):
            xs_ref[kp * tiles + h, tile_rows(plane), :] = value[kp * groups : (kp + 1) * groups, h * LANES : (h + 1) * LANES]


def plane_rows(ws_ref, plane, width):
    tiles = width // LANES
    columns = []
    for h in range(tiles):
        parts = [ws_ref[kp * tiles + h, tile_rows(plane), :] for kp in range(2 * GROUP)]
        columns.append(jnp.concatenate(parts, axis=0))
    return jnp.concatenate(columns, axis=1)


def local_spectra(xs_ref, y_down_ref, z_down, zt_ref, sp_ref, start, count):
    groups = KXY // GROUP
    rows = slice(start * groups, (start + count) * groups)
    half = zt_ref.shape[0] // 2
    lhs = jnp.concatenate([xs_ref[j, rows, :].astype(BF) for j in range(xs_ref.shape[0])], axis=1)
    spectra = dot(lhs, y_down_ref[...])
    for q in range(2):
        sp_ref[q, : count * groups, :] = spectra[:, q * LANES : (q + 1) * LANES]
    if count < half:
        zt_ref[...] = jnp.zeros_like(zt_ref)
    for g in range(groups):
        for q in range(2):
            part = sp_ref[q, pl.ds(g, count, stride=groups), :]
            zt_ref[q * half : q * half + count, g * LANES : (g + 1) * LANES] = part.astype(BF)
    return dot(z_down, twice(zt_ref[...]))


def slot_pairs(slab, slabs):
    return [(lax.rem(slab + d, slabs), lax.rem(slab + d + 1, slabs)) for d in range(1, slabs, 2)]


def pack_half(coeffs, pick_ref, pairs, packed_ref, h, sends):
    rows = coeffs.shape[0]
    capacity = packed_ref.shape[2]
    for i, targets in enumerate(pairs):
        part = dot(coeffs, pick_ref[:, 2 * i * capacity : 2 * (i + 1) * capacity]).astype(BF)
        for n, t in enumerate(targets):
            packed_ref[t, h * rows : (h + 1) * rows, :] = part[:, n * capacity : (n + 1) * capacity]
            if 2 * i + n < len(sends):
                sends[2 * i + n].start()


def synthesis_head(slab, recv_ref, pick_ref, z_up, y_up_ref, sp_ref, ws_ref):
    groups = KXY // GROUP
    rows = ws_ref.shape[1]
    planes_all = rows // groups
    slabs = recv_ref.shape[0]
    by_slot = jnp.concatenate([recv_ref[t] for pair in slot_pairs(slab, slabs) for t in pair], axis=1)
    chunk = 2 * LANES
    spectra = dot_nt(pick_ref[...], by_slot).astype(BF)
    spectra = jnp.concatenate([spectra, spectra], axis=1)
    for n in range(KXY * KXY // chunk):
        planes = dot_nt(z_up, spectra[n * chunk : (n + 1) * chunk])
        for gg in range(2):
            for q in range(2):
                sp_ref[q, pl.ds(2 * n + gg, planes_all, stride=groups), :] = planes[
                    q * planes_all : (q + 1) * planes_all, gg * LANES : (gg + 1) * LANES
                ]
    lhs = jnp.concatenate([sp_ref[q, :rows, :].astype(BF) for q in range(2)], axis=1)
    for j in range(ws_ref.shape[0] // 2):
        wide = dot(lhs, y_up_ref[:, j * chunk : (j + 1) * chunk])
        ws_ref[2 * j] = wide[:, :LANES]
        ws_ref[2 * j + 1] = wide[:, LANES:]


def gelu_pair(half):
    coeff = math.sqrt(2.0 / math.pi)
    square = half * half
    tangent = jnp.tanh(half * (2.0 * coeff + (8.0 * 0.044715 * coeff) * square))
    turned = half * tangent
    value = half + turned
    inner = 0.5 + (half - turned) * (coeff + (12.0 * 0.044715 * coeff) * square)
    return value, (value * (1.0 + tangent)) * inner


def final_kernel(per_step, slab_ref, gain_ref, value_ref, grad_ref, recv_ref, pick_ref, x_up_ref, y_up_ref, z_up_ref, value_hbm, out_ref, ws_ref, sp_ref, value_sem):
    step = pl.program_id(0)
    channels, planes = grad_ref.shape[:2]
    grid_len = grad_ref.shape[2]
    copies = [pltpu.make_async_copy(value_ref.at[c], value_hbm.at[c], value_sem.at[c]) for c in range(channels)]

    @pl.when(step == 0)
    def _():
        for copy in copies:
            copy.start()
        synthesis_head(slab_ref[0], recv_ref, pick_ref, z_up_ref[0], y_up_ref, sp_ref, ws_ref)

    def body(zz, carry):
        for c in range(channels):
            wp = plane_rows(ws_ref, c * planes + step * per_step + zz, grid_len).astype(BF)
            out_ref[c, zz] = (dot(x_up_ref[...], wp) + gain_ref[c] * grad_ref[c, step * per_step + zz].astype(F32)).astype(BF)
        return carry

    lax.fori_loop(0, per_step, body, 0)

    @pl.when(step == pl.num_programs(0) - 1)
    def _():
        for copy in copies:
            copy.wait()


def announce(targets):
    barrier = pltpu.get_barrier_semaphore()
    for target in targets:
        pl.semaphore_signal(barrier, inc=1, device_id=target, device_id_type=MESH)


def await_peers(targets):
    pl.semaphore_wait(pltpu.get_barrier_semaphore(), len(targets))


def reorder_weights(w_ref, wide_ref):
    width = w_ref.shape[3]
    slots = width // KZ
    flat = w_ref[...].reshape(-1, width)
    chunk = 2 * slots

    def body(n, carry):
        source = lax.broadcasted_iota(jnp.int32, (width, chunk), 0)
        lane = lax.broadcasted_iota(jnp.int32, (1, chunk), 1)
        wanted = jnp.where(lane < slots, lane * KZ, (lane - slots) * KZ + 1) + 2 * n
        moved = dot(flat, (source == wanted).astype(F32).astype(BF)).astype(BF)
        wide_ref[:, :, :, pl.ds(pl.multiple_of(n * chunk, chunk), chunk)] = moved.reshape(w_ref.shape[:3] + (chunk,))
        return carry

    lax.fori_loop(0, width // chunk, body, 0)


def peers_of(slabs, groups):
    slab, chan = lax.axis_index("slab"), lax.axis_index("chan")
    slab_peer = [(lax.rem(slab + d, slabs), chan) for d in range(1, slabs)]
    chan_peer = [(slab, lax.rem(chan + d, groups)) for d in range(1, groups)]
    return slab, chan, slab_peer, chan_peer


def spectra_copies(packed_ref, rx, peers, h, s_send, s_recv):
    rows = packed_ref.shape[1] // HALVES
    part = pl.ds(h * rows, rows)
    copies = []
    for d, peer in enumerate(peers):
        n = h * len(peers) + d
        copies.append(pltpu.make_async_remote_copy(
            src_ref=packed_ref.at[peer[0], part], dst_ref=rx.at[d, part], send_sem=s_send.at[n], recv_sem=s_recv.at[n],
            device_id=peer, device_id_type=MESH,
        ))
    return copies


def middle_part(slabs, groups, rows, gain_ref, bias_ref, recv_ref, wide_ref, pick_ref, x_down_ref, x_up_ref, y_down_ref, y_up_ref, z_down_ref, z_up_ref,
                out_ref, grad_ref, adjoint_ref, xs_ref, ws_ref, zt_ref, sp_ref, sa_ref, sb_ref, ga_ref, gb_ref, ma_ref, mb_ref, packed_ref, rx, tx2, rx2, mine, stage, *sems):
    slab, _, slab_peer, _ = peers_of(slabs, groups)
    channels, planes, grid_len, _ = out_ref.shape
    count = channels * planes
    synthesis_head(slab, recv_ref, pick_ref, z_up_ref[...], y_up_ref, sp_ref, ws_ref)

    def synth(t, s_ref, m_ref):
        c = t // planes
        m_ref[...] = out_ref[c, t - c * planes]
        shift = jnp.full((BIAS_ROWS, grid_len), 0.5 * bias_ref[c], F32)
        high = shift.astype(BF).astype(F32)
        row = lax.broadcasted_iota(jnp.int32, shift.shape, 0)
        shift = jnp.where(row == 0, high, jnp.where(row == 1, shift - high, 0.0))
        s_ref[...] = dot(x_up_ref[...], jnp.concatenate([plane_rows(ws_ref, t, grid_len), shift], axis=0).astype(BF))

    def point(t, s_ref, m_ref, g_ref):
        c = t // planes
        zz = t - c * planes
        gain = 0.5 * gain_ref[c]
        for start in range(0, grid_len, rows):
            span = slice(start, start + rows)
            value, grad = gelu_pair(s_ref[span, :] + gain * m_ref[span, :].astype(F32))
            grad = grad.astype(BF)
            out_ref[c, zz, span, :] = value.astype(BF)
            grad_ref[c, zz, span, :] = grad
            g_ref[span, :] = grad

    def down(t, g_ref):
        keep_x_rows(xs_ref, t, dot(x_down_ref[...], g_ref[...]))

    gb_ref[...] = jnp.zeros_like(gb_ref)
    synth(0, sa_ref, ma_ref)

    def body(j, carry):
        t = 2 * j
        synth(t + 1, sb_ref, mb_ref)
        down(jnp.maximum(t - 1, 0), gb_ref)
        point(t, sa_ref, ma_ref, ga_ref)
        synth(jnp.minimum(t + 2, count - 1), sa_ref, ma_ref)
        down(t, ga_ref)
        point(t + 1, sb_ref, mb_ref, gb_ref)
        return carry

    part = count // HALVES
    first = [spectra_copies(packed_ref, rx, slab_peer, h, *sems[:2]) for h in range(HALVES)]
    for h in range(HALVES):
        lax.fori_loop(h * part // 2, (h + 1) * part // 2, body, 0)
        down((h + 1) * part - 1, gb_ref)
        coeffs = local_spectra(xs_ref, y_down_ref, z_down_ref[...], zt_ref, sp_ref, h * part, part).astype(BF)
        pack_half(coeffs, pick_ref, slot_pairs(slab, slabs), packed_ref, h, first[h])
    exchange_body(slabs, groups, False, first, packed_ref, wide_ref, adjoint_ref, rx, tx2, rx2, mine, stage, *sems)


def exchange_body(slabs, groups, forward, first, packed_ref, wide_ref, recv_ref, rx, tx2, rx2, mine, stage, s_send, s_recv, c_send, c_recv, g_send, g_recv, shared=None, filler=None):
    slab, chan, slab_peer, chan_peer = peers_of(slabs, groups)
    rows, slots = packed_ref.shape[1] // PIECES, packed_ref.shape[2]
    kept = KZ // PIECES
    own = rx2.shape[1] // 2
    some = own // HALVES
    pairs = 2 * own
    outputs = own * groups
    wide = kept * slots
    step = min(kept, 4)

    def factor(piece, m):
        return 1.0 if piece == 0 and m == 0 else 2.0

    def at_m(piece, m, count=1):
        return slice((piece * kept + m) * slots, (piece * kept + m + count) * slots)

    def part_rows(h, q):
        return slice((2 * h + q) * some, (2 * h + q + 1) * some)

    half = packed_ref.shape[1] // HALVES
    for h in range(HALVES):
        span = slice(h * half, (h + 1) * half)
        total = packed_ref[slab, span, :].astype(F32)
        for d in range(1, slabs):
            first[h][d - 1].wait_recv()
            total = total + rx[d - 1, span, :].astype(F32)
        stage[span, :] = total
    common = None if shared is None else shared()
    second = []
    for p in range(PIECES):
        tiles = []
        for m in range(kept):
            base = [h * half + p * (half // PIECES) + m for h in range(HALVES)]
            tile = jnp.concatenate([stage[pl.ds(at, 2 * some, stride=kept), :] for at in base], axis=0)
            if common is not None:
                both = [common[(2 * p + q) * kept + m : (2 * p + q) * kept + m + 1, :] for q in range(2)]
                tile = tile + jnp.concatenate([jnp.broadcast_to(b, (some, slots)) for b in both] * HALVES, axis=0)
            tiles.append(tile)
        if forward:
            for m in range(0, kept, step):
                at = at_m(p, m, step)
                u = jnp.concatenate(tiles[m : m + step], axis=1)
                real = jnp.zeros((outputs, step * slots), F32)
                imag = jnp.zeros((outputs, step * slots), F32)
                for c in range(own):
                    w0, w1 = wide_ref[0, c, :, at].astype(F32), wide_ref[1, c, :, at].astype(F32)
                    h, k = c // some, c % some
                    ur, ui = u[2 * h * some + k : 2 * h * some + k + 1], u[(2 * h + 1) * some + k : (2 * h + 1) * some + k + 1]
                    real = real + (w0 * ur - w1 * ui)
                    imag = imag + (w1 * ur + w0 * ui)
                for e in range(groups):
                    mine_rows = slice(e * own, (e + 1) * own)
                    tx2[e, :, at] = jnp.concatenate([real[mine_rows], imag[mine_rows]], axis=0).astype(BF)
        else:
            for m in range(kept):
                tx2[0, :, at_m(p, m)] = (tiles[m] * factor(p, m)).astype(BF)
        lanes = pl.ds(p * wide, wide)
        copies = []
        for d in range(1, groups):
            peer = chan_peer[d - 1]
            n = p * (groups - 1) + d - 1
            copy = pltpu.make_async_remote_copy(
                src_ref=tx2.at[peer[1] if forward else 0, :, lanes], dst_ref=rx2.at[chan, :, lanes], send_sem=c_send.at[n], recv_sem=c_recv.at[n],
                device_id=peer, device_id_type=MESH,
            )
            copy.start()
            copies.append(copy)
        rx2[chan, :, lanes] = tx2[chan if forward else 0, :, lanes]
        second.append(copies)
    third, steps = [], []
    side = math.isqrt(slabs)
    y, z = slab // side, lax.rem(slab, side)

    def ring(axis, d):
        return lax.rem(y + d, side) * side + z if axis == 0 else y * side + lax.rem(z + d, side)

    def hand_on(source, index, part, to, n):
        copy = pltpu.make_async_remote_copy(
            src_ref=source, dst_ref=recv_ref.at[index, part], send_sem=g_send.at[n], recv_sem=g_recv.at[n],
            device_id=(to, chan), device_id_type=MESH,
        )
        copy.start()
        third.append(copy)
        return copy

    def spread_piece(p, part):
        n = p * (slabs - 1)
        along = [hand_on(mine.at[part], slab, part, ring(p % 2, d), n + d - 1) for d in range(1, side)]
        for d in range(1, side):
            hand_on(mine.at[part], slab, part, ring(1 - p % 2, d), n + side - 1 + d - 1)
        return p, part, along

    def forward_piece(p, part, along):
        n = p * (slabs - 1) + 2 * (side - 1)
        for a in range(1, side):
            along[a - 1].wait_recv()
            taken.append(along[a - 1])
            source = ring(p % 2, side - a)
            for d in range(1, side):
                hand_on(recv_ref.at[source, part], source, part, ring(1 - p % 2, d), n + (a - 1) * (side - 1) + d - 1)

    taken = []
    for p in range(PIECES):
        for copy in second[p]:
            copy.wait_recv()
        for m in range(0, kept, step):
            at = at_m(p, m, step)
            if forward:
                result = rx2[0, :, at].astype(F32)
                for e in range(1, groups):
                    result = result + rx2[e, :, at].astype(F32)
            else:
                blocks = [rx2[e, :, at].astype(F32) for e in range(groups)]
                real = jnp.concatenate([b[part_rows(h, 0)] for b in blocks for h in range(HALVES)], axis=0)
                imag = jnp.concatenate([b[part_rows(h, 1)] for b in blocks for h in range(HALVES)], axis=0)
                reals, imags = [], []
                for c in range(own):
                    w0, w1 = wide_ref[0, c, :, at].astype(F32), wide_ref[1, c, :, at].astype(F32)
                    reals.append(jnp.sum(w0 * real + w1 * imag, axis=0, keepdims=True))
                    imags.append(jnp.sum(w0 * imag - w1 * real, axis=0, keepdims=True))
                result = jnp.concatenate(reals + imags, axis=0)
            for k in range(step):
                part = result[:, k * slots : (k + 1) * slots]
                stage[pl.ds(p * rows + m + k, pairs, stride=kept), :] = part * factor(p, m + k) if forward else part
        part = pl.ds(p * rows, rows)
        mine[part, :] = stage[part, :].astype(BF)
        steps.append(spread_piece(p, part))
        if p > 0:
            forward_piece(*steps[p - 1])
    forward_piece(*steps[-1])
    recv_ref[slab] = mine[...]
    if filler is not None:
        filler()
    for copy in third:
        if not any(copy is other for other in taken):
            copy.wait_recv()
    for copy in sum(first, []) + sum(second, []) + third:
        copy.wait_send()


def front_part(slabs, groups, field_hbm, forcing_hbm, slots_hbm, w_hbm, x_down_hbm, x_part_hbm, y_down_hbm, z_down_hbm, later, recv_ref, merged_ref, wide_ref, pick_ref,
               plane_ref, own_ref, xs_ref, xf_ref, zt_ref, sp_ref, packed_ref, rx, tx2, rx2, mine, stage, slot_ref, w_ref, x_down_ref, x_part_ref, y_down_ref, z_down_ref,
                 f_packed, f_rx, f_mine, f_rx2, f_sum, in_sem, field_sem, x_send, x_recv, p_send, p_recv, f_send, f_recv, h_send, h_recv, *sems):
    slab, chan, slab_peer, chan_peer = peers_of(slabs, groups)
    channels, planes = merged_ref.shape[:2]
    height = forcing_hbm.shape[1]
    chips = groups // 2
    chip, core = chan // 2, lax.rem(chan, 2)
    partner = (slab, chan + 1 - 2 * core)

    def near(t):
        return 2 * lax.rem(chip + chips + t, chips) + core

    def rows(index, start, count):
        return plane_ref.at[pl.ds(start, count), pl.ds(pl.multiple_of(index * height, height), height), :]

    fields = [pltpu.make_async_copy(field_hbm.at[c], merged_ref.at[c], field_sem.at[c]) for c in range(channels)]
    small = [
        pltpu.make_async_copy(forcing_hbm, own_ref, in_sem.at[0]),
        pltpu.make_async_copy(x_part_hbm.at[chan], x_part_ref, in_sem.at[1]),
        pltpu.make_async_copy(y_down_hbm, y_down_ref, in_sem.at[2]),
        pltpu.make_async_copy(z_down_hbm.at[slab], z_down_ref, in_sem.at[3]),
        pltpu.make_async_copy(slots_hbm, slot_ref, in_sem.at[4]),
        pltpu.make_async_copy(x_down_hbm, x_down_ref, in_sem.at[5]),
    ]
    load_w = pltpu.make_async_copy(w_hbm, w_ref, in_sem.at[6])
    place_own = pltpu.make_async_copy(forcing_hbm, rows(chan, 0, planes), in_sem.at[7])
    for copy in small + fields + [load_w, place_own] + later:
        copy.start()
    announce(slab_peer + chan_peer)
    for copy in small:
        copy.wait()

    def forcing_body(zz, carry):
        keep_x_rows(xf_ref, zz, dot(x_part_ref[...], own_ref[zz]))
        return carry

    lax.fori_loop(0, planes, forcing_body, 0, unroll=4)
    padded = local_spectra(xf_ref, y_down_ref, z_down_ref[...], zt_ref, sp_ref, 0, planes)
    kept = KZ // PIECES
    block = channels // HALVES * kept
    forced = jnp.concatenate([padded[n * block : n * block + kept] for n in range(2 * PIECES)], axis=0).astype(BF)
    columns = forced.shape[1]
    capacity = packed_ref.shape[2]
    pairs = slot_pairs(slab, slabs)
    for i, targets in enumerate(pairs):
        column = lax.broadcasted_iota(jnp.int32, (columns, 2 * capacity), 0)
        pick = (column == jnp.concatenate([slot_ref[pl.ds(t, 1), :] for t in targets], axis=1)).astype(F32).astype(BF)
        pick_ref[:, 2 * i * capacity : 2 * (i + 1) * capacity] = pick
        part = dot(forced, pick).astype(BF)
        for n, t in enumerate(targets):
            f_packed[t] = part[:, n * capacity : (n + 1) * capacity]
    await_peers(slab_peer + chan_peer)
    sent = []

    def send(copies):
        for copy in copies:
            copy.start()
            sent.append(copy)
        return copies

    forced_in = send([
        pltpu.make_async_remote_copy(
            src_ref=f_packed.at[slab_peer[d - 1][0]], dst_ref=f_rx.at[d - 1], send_sem=f_send.at[d - 1], recv_sem=f_recv.at[d - 1],
            device_id=slab_peer[d - 1], device_id_type=MESH,
        )
        for d in range(1, slabs)
    ])

    half = planes // 2

    def across(index, start, to, n, source=None):
        return pltpu.make_async_remote_copy(
            src_ref=rows(index, start, half) if source is None else source, dst_ref=rows(index, start, half),
            send_sem=x_send.at[n], recv_sem=x_recv.at[n], device_id=(slab, to), device_id_type=MESH,
        )

    def beside(index, start, count, n, source=None):
        return pltpu.make_async_remote_copy(
            src_ref=rows(index, start, count) if source is None else source, dst_ref=rows(index, start, count),
            send_sem=p_send.at[n], recv_sem=p_recv.at[n], device_id=partner, device_id_type=MESH,
        )

    def x_pass(c):
        fields[c].wait()

        def body(zz, carry):
            keep_x_rows(xs_ref, c * planes + zz, dot(x_down_ref[...], merged_ref[c, zz]))
            return carry

        lax.fori_loop(0, planes, body, 0, unroll=4)

    low, high = own_ref.at[pl.ds(0, half)], own_ref.at[pl.ds(half, half)]
    right_low, left_high, right_high, left_low = send([
        across(chan, 0, near(1), 0, low), across(chan, half, near(-1), 1, high),
        across(chan, half, near(1), 2, high), across(chan, 0, near(-1), 3, low),
    ])
    beside_all = send([beside(chan, 0, planes, 0, own_ref)])
    first = [spectra_copies(packed_ref, rx, slab_peer, h, *sems[:2]) for h in range(HALVES)]
    part = channels // HALVES

    def send_half(h):
        for c in range(h * part, (h + 1) * part):
            x_pass(c)
        coeffs = local_spectra(xs_ref, y_down_ref, z_down_ref[...], zt_ref, sp_ref, h * part * planes, part * planes).astype(BF)
        pack_half(coeffs, pick_ref, pairs, packed_ref, h, first[h])

    send_half(0)
    total = f_packed[slab].astype(F32)
    for d in range(1, slabs):
        forced_in[d - 1].wait_recv()
        total = total + f_rx[d - 1].astype(F32)
    f_mine[...] = total.astype(BF)
    shared_in = send([
        pltpu.make_async_remote_copy(
            src_ref=f_mine, dst_ref=f_rx2.at[chan], send_sem=h_send.at[d - 1], recv_sem=h_recv.at[d - 1],
            device_id=chan_peer[d - 1], device_id_type=MESH,
        )
        for d in range(1, groups)
    ])
    f_rx2[chan] = f_mine[...]
    right_low.wait_recv()
    left_high.wait_recv()
    far_low, far_high = send([across(near(-1), 0, near(1), 4), across(near(1), half, near(-1), 5)])
    beside_all += send([beside(near(-1), 0, half, 1), beside(near(1), half, half, 2)])
    for h in range(1, HALVES):
        send_half(h)
    right_high.wait_recv()
    left_low.wait_recv()
    beside_all += send([beside(near(-1), half, half, 3), beside(near(1), 0, half, 4)])
    load_w.wait()
    reorder_weights(w_ref, wide_ref)
    far_low.wait_recv()
    far_high.wait_recv()
    beside_all += send([beside(near(2), 0, half, 5), beside(near(2), half, half, 6)])

    def shared():
        for copy in shared_in:
            copy.wait_recv()
        common = f_rx2[0].astype(F32)
        for e in range(1, groups):
            common = common + f_rx2[e].astype(F32)
        f_sum[...] = common
        return f_sum

    def merge():
        place_own.wait()
        for copy in beside_all:
            copy.wait_recv()

        def body(zz, carry):
            for c in range(channels):
                merged_ref[c, zz] = merged_ref[c, zz] + plane_ref[zz]
            return carry

        lax.fori_loop(0, planes, body, 0)

    exchange_body(slabs, groups, True, first, packed_ref, wide_ref, recv_ref, rx, tx2, rx2, mine, stage, *sems, shared=shared, filler=merge)
    for copy in sent:
        copy.wait_send()
    for copy in later:
        copy.wait()


def spectral_kernel(slabs, groups, rows, gain_hbm, bias_hbm, field_hbm, forcing_hbm, slots_hbm, w_hbm, x_down_hbm, x_part_hbm, y_down_hbm, z_down_hbm, x_up_hbm, y_up_hbm, z_up_hbm,
                    out_ref, grad_ref, adjoint_ref, pick_ref, recv_ref, wide_ref, x_down_ref, x_up_ref, y_down_ref, y_up_ref, z_down_ref, z_up_ref,
                    xs_ref, ws_ref, zt_ref, sp_ref, sa_ref, sb_ref, ga_ref, gb_ref, ma_ref, mb_ref,
                    plane_ref, own_ref, xf_ref, slot_ref, w_ref, x_part_ref, f_packed, f_rx, f_mine, f_rx2, f_sum, gain_ref, bias_ref, later_sem, in_sem, field_sem, x_send, x_recv, p_send, p_recv, f_send, f_recv, h_send, h_recv, *rest):
    forward, adjoint = rest[:12], rest[12:]
    later = [
        pltpu.make_async_copy(x_up_hbm, x_up_ref, later_sem.at[0]),
        pltpu.make_async_copy(y_up_hbm, y_up_ref, later_sem.at[1]),
        pltpu.make_async_copy(z_up_hbm.at[lax.axis_index("slab")], z_up_ref, later_sem.at[2]),
        pltpu.make_async_copy(gain_hbm, gain_ref, later_sem.at[3]),
        pltpu.make_async_copy(bias_hbm, bias_ref, later_sem.at[4]),
    ]
    packed_ref, rx, tx2, rx2, mine, stage = forward[:6]
    front_part(slabs, groups, field_hbm, forcing_hbm, slots_hbm, w_hbm, x_down_hbm, x_part_hbm, y_down_hbm, z_down_hbm, later, recv_ref, out_ref, wide_ref, pick_ref,
               plane_ref, own_ref, xs_ref, xf_ref, zt_ref, sp_ref, packed_ref, rx, tx2, rx2, mine, stage, slot_ref, w_ref, x_down_ref, x_part_ref, y_down_ref, z_down_ref,
               f_packed, f_rx, f_mine, f_rx2, f_sum, in_sem, field_sem, x_send, x_recv, p_send, p_recv, f_send, f_recv, h_send, h_recv, *forward[6:])
    middle_part(slabs, groups, rows, gain_ref, bias_ref, recv_ref, wide_ref, pick_ref, x_down_ref, x_up_ref, y_down_ref, y_up_ref, z_down_ref, z_up_ref,
                out_ref, grad_ref, adjoint_ref, xs_ref, ws_ref, zt_ref, sp_ref, sa_ref, sb_ref, ga_ref, gb_ref, ma_ref, mb_ref, *adjoint)


def whole(shape):
    zeros = (0,) * len(shape)
    return pl.BlockSpec(shape, lambda *_: zeros, pipeline_mode=pl.Buffered(1))


class Sizes:
    def __init__(self, slabs, groups, channels, planes, grid_len, capacity):
        self.slabs, self.groups = slabs, groups
        self.channels, self.planes, self.grid_len = channels, planes, grid_len
        self.capacity = capacity
        planes_all = channels * planes
        x_down, x_up, y_down, y_up = plane_tables(grid_len)
        ones = np.zeros((grid_len, BIAS_ROWS), x_up.dtype)
        ones[:, :2] = 1
        half = bf16_table(0.5 * x_up.astype(np.float32))
        self.x_down, self.x_up, self.y_down, self.y_up = [jnp.asarray(t) for t in (x_down, x_up, y_down, y_up)]
        self.x_part = jnp.asarray(x_down.reshape(2 * KXY, groups, -1).transpose(1, 0, 2))
        self.x_up_half = jnp.asarray(np.concatenate([half, ones], axis=1))
        self.z_down, self.z_up = [jnp.asarray(t) for t in depth_tables(channels, planes, slabs, grid_len)]
        self.per_step = 4
        per_step = self.per_step
        self.steps = planes // per_step
        self.field_spec = pl.BlockSpec((channels, per_step, grid_len, grid_len), lambda i, s: (0, i, 0, 0))
        self.z_spec = pl.BlockSpec((1,) + self.z_up.shape[1:], lambda i, s: (s[0], 0, 0), pipeline_mode=pl.Buffered(1))
        self.packed_shape = (slabs, 2 * channels * KZ, capacity)
        self.volume = jax.ShapeDtypeStruct((channels, planes, grid_len, grid_len), BF)
        self.packed_out = jax.ShapeDtypeStruct(self.packed_shape, BF)
        self.wide_scratch = pltpu.VMEM((2 * GROUP * grid_len // LANES, planes_all * KXY // GROUP, LANES), F32)
        dma = pltpu.SemaphoreType.DMA
        self.exchange_sems = [dma((n,)) for n in [HALVES * (slabs - 1)] * 2 + [PIECES * (groups - 1)] * 2 + [PIECES * (slabs - 1)] * 2]
        self.sp_scratch = pltpu.VMEM((2, planes_all * KXY // GROUP, LANES), F32)
        self.zt_scratch = pltpu.VMEM((2 * planes_all // HALVES, KXY * KXY), BF)
        self.params = pltpu.CompilerParams(dimension_semantics=("arbitrary",), vmem_limit_bytes=14 << 20)


SMEM = pl.BlockSpec(memory_space=pltpu.SMEM)
VMEM = pl.BlockSpec(memory_space=pltpu.VMEM)
HBM = pl.BlockSpec(memory_space=pltpu.HBM)


def spectral_call(z, field, forcing, slot_column, w_spec, skip_gain, bias):
    block = z.packed_shape[1:]
    pair = (z.groups, 2 * z.channels, z.capacity * KZ)
    tiles = 2 * GROUP * z.grid_len // LANES
    forced = (2 * KZ, z.capacity)
    plane = (z.grid_len, z.grid_len)
    dma = pltpu.SemaphoreType.DMA
    operands = (skip_gain, bias, field, forcing, slot_column, w_spec, z.x_down, z.x_part, z.y_down, z.z_down, z.x_up_half, z.y_up, z.z_up)

    def scratch(kind, *shapes):
        return [pltpu.VMEM(shape, kind) for shape in shapes]

    exchange = scratch(BF, z.packed_shape, (z.slabs - 1,) + block, pair, pair, block) + scratch(F32, block) + z.exchange_sems
    return pl.pallas_call(
        functools.partial(spectral_kernel, z.slabs, z.groups, 64),
        out_shape=(z.volume, z.volume, z.packed_out, jax.ShapeDtypeStruct((KXY * KXY, slot_column.size), BF)),
        in_specs=[HBM] * len(operands),
        out_specs=(VMEM, VMEM, VMEM, VMEM),
        scratch_shapes=scratch(BF, z.packed_shape, w_spec.shape, z.x_down.shape, z.x_up_half.shape, z.y_down.shape, z.y_up.shape, z.z_down.shape[1:], z.z_up.shape[1:])
        + [z.wide_scratch, z.wide_scratch, z.zt_scratch, z.sp_scratch]
        + scratch(F32, plane, plane)
        + scratch(BF, plane, plane, plane, plane)
        + scratch(BF, (z.planes,) + plane, forcing.shape)
        + scratch(F32, (tiles, z.planes * KXY // GROUP, LANES))
        + scratch(jnp.int32, slot_column.shape)
        + scratch(BF, w_spec.shape, z.x_part.shape[1:], (z.slabs,) + forced, (z.slabs - 1,) + forced, forced, (z.groups,) + forced)
        + scratch(F32, forced)
        + [pltpu.SMEM((z.channels,), F32)] * 2
        + [dma((n,)) for n in [5, 8, z.channels, 6, 6, 7, 7] + [z.slabs - 1] * 2 + [z.groups - 1] * 2]
        + exchange
        + exchange,
        compiler_params=pltpu.CompilerParams(collective_id=1, has_side_effects=True, vmem_limit_bytes=SPECTRAL_VMEM),
        name="spectral",
    )(*[pltpu.with_memory_space_constraint(v, pltpu.HBM) for v in operands])


def final_call(z, where, skip_gain, value, grad_pre, adjoint, picks):
    return pl.pallas_call(
        functools.partial(final_kernel, z.per_step),
        out_shape=(z.volume, z.volume),
        grid_spec=pltpu.PrefetchScalarGridSpec(
            num_scalar_prefetch=1, grid=(z.steps,),
            in_specs=[SMEM, VMEM, VMEM, VMEM, VMEM, whole(z.x_up.shape), whole(z.y_up.shape), z.z_spec],
            out_specs=(HBM, z.field_spec),
            scratch_shapes=[z.wide_scratch, z.sp_scratch, pltpu.SemaphoreType.DMA((z.channels,))],
        ),
        compiler_params=z.params,
        name="synth_gradient",
    )(where, skip_gain, value, grad_pre, adjoint, picks, z.x_up, z.y_up, z.z_up)


def per_device(slabs, groups, field, forcing, slot_column, w_spec, skip_gain, bias):
    channels, planes, grid_len, _ = field.shape
    capacity = slot_column.shape[1]
    z = Sizes(slabs, groups, channels, planes, grid_len, capacity)
    where = lax.axis_index("slab").astype(jnp.int32).reshape(1)
    value, grad_pre, adjoint, picks = spectral_call(z, field, forcing, slot_column, w_spec, skip_gain, bias)
    return final_call(z, where, skip_gain, value, grad_pre, adjoint, picks)


def solution(mesh):
    placed = (
        P("chan", "slab", None, None),
        P("slab", "chan", None),
        P(),
        P(None, "chan", None, "slab"),
        P("chan"),
        P("chan"),
    )
    slabs, groups = mesh.shape["slab"], mesh.shape["chan"]
    return jax.shard_map(
        functools.partial(per_device, slabs, groups),
        mesh=mesh,
        in_specs=placed,
        out_specs=(P("chan", "slab", None, None), P("chan", "slab", None, None)),
        check_vma=False,
    )
```

```python
import functools
import math

import jax
import jax.numpy as jnp
import ml_dtypes
import numpy as np
from jax import lax
from jax.experimental import pallas as pl
from jax.experimental.pallas import tpu as pltpu
from jax.sharding import PartitionSpec as P

KXY = 32
KZ = 16
MESH = pl.DeviceIdType.MESH
BF = jnp.bfloat16
F32 = jnp.float32
LANES = 128
SPECTRAL_VMEM = 31 << 20
PIECES = 2
HALVES = 2
BIAS_ROWS = 16
GROUP = LANES // KXY


def bf16_table(values):
    return np.asarray(values, np.float32).astype(ml_dtypes.bfloat16)


def trig(freqs, coords, grid_len):
    angle = (np.outer(freqs, coords) % grid_len) * (2.0 * math.pi / grid_len)
    return np.cos(angle), np.sin(angle)


def plane_tables(grid_len):
    freqs = np.arange(KXY) - KXY // 2
    cos, sin = trig(freqs, np.arange(grid_len), grid_len)
    groups = KXY // GROUP
    scale = float(grid_len) ** -1.5
    x_down = np.zeros((GROUP, 2, groups, grid_len))
    x_up = np.zeros((grid_len, GROUP, 2, groups))
    y_down = np.zeros((GROUP, 2, grid_len, 2, GROUP, KXY))
    y_up = np.zeros((2, GROUP, KXY, GROUP, 2, grid_len))
    for k in range(GROUP):
        for g in range(groups):
            jx = g * GROUP + k
            x_down[k, 0, g], x_down[k, 1, g] = cos[jx], sin[jx]
            x_up[:, k, 0, g], x_up[:, k, 1, g] = scale * cos[jx], -scale * sin[jx]
        y_down[k, 0, :, 0, k], y_down[k, 1, :, 0, k] = cos.T, -sin.T
        y_down[k, 0, :, 1, k], y_down[k, 1, :, 1, k] = -sin.T, -cos.T
        y_up[0, k, :, k, 0], y_up[1, k, :, k, 0] = cos, -sin
        y_up[0, k, :, k, 1], y_up[1, k, :, k, 1] = sin, cos
    rows = 2 * KXY
    return (
        bf16_table(x_down.reshape(rows, grid_len)),
        bf16_table(x_up.reshape(grid_len, rows)),
        bf16_table(y_down.reshape(2 * GROUP * grid_len, 2 * LANES)),
        bf16_table(y_up.reshape(2 * LANES, 2 * GROUP * grid_len)),
    )


def depth_tables(channels, planes, slabs, grid_len):
    scale = float(grid_len) ** -1.5
    down, up = [], []
    for s in range(slabs):
        cos, sin = trig(np.arange(KZ), s * planes + np.arange(planes), grid_len)
        parts = [[cos, sin], [-sin, cos]]
        for store, count in ((down, channels // HALVES), (up, channels)):
            full = np.zeros((2, count, KZ, 2, count, planes))
            for q in range(2):
                for r in range(2):
                    full[q, :, :, r] = np.einsum("cd,mz->cmdz", np.eye(count), parts[q][r])
            full = full.reshape(2, count, PIECES, KZ // PIECES, -1).transpose(2, 0, 1, 3, 4)
            full = full.reshape(2 * count * KZ, 2 * count * planes)
            table = full * scale if store is down else full.T
            high = bf16_table(table)
            low = bf16_table(table - high.astype(np.float64))
            store.append(np.concatenate([high, low], axis=1))
    return np.stack(down), np.stack(up)


def dot(a, b):
    return jnp.dot(a, b, preferred_element_type=F32)


def dot_nt(a, b):
    return lax.dot_general(a, b, (((1,), (1,)), ((), ())), preferred_element_type=F32)


def twice(block):
    return jnp.concatenate([block, block], axis=0)


def tile_rows(plane):
    groups = KXY // GROUP
    return pl.ds(pl.multiple_of(plane * groups, groups), groups)


def keep_x_rows(xs_ref, plane, value):
    groups = KXY // GROUP
    tiles = value.shape[1] // LANES
    for kp in range(2 * GROUP):
        for h in range(tiles):
            xs_ref[kp * tiles + h, tile_rows(plane), :] = value[kp * groups : (kp + 1) * groups, h * LANES : (h + 1) * LANES]


def plane_rows(ws_ref, plane, width):
    tiles = width // LANES
    columns = []
    for h in range(tiles):
        parts = [ws_ref[kp * tiles + h, tile_rows(plane), :] for kp in range(2 * GROUP)]
        columns.append(jnp.concatenate(parts, axis=0))
    return jnp.concatenate(columns, axis=1)


def local_spectra(xs_ref, y_down_ref, z_down, zt_ref, sp_ref, start, count):
    groups = KXY // GROUP
    rows = slice(start * groups, (start + count) * groups)
    half = zt_ref.shape[0] // 2
    lhs = jnp.concatenate([xs_ref[j, rows, :].astype(BF) for j in range(xs_ref.shape[0])], axis=1)
    spectra = dot(lhs, y_down_ref[...])
    for q in range(2):
        sp_ref[q, : count * groups, :] = spectra[:, q * LANES : (q + 1) * LANES]
    if count < half:
        zt_ref[...] = jnp.zeros_like(zt_ref)
    for g in range(groups):
        for q in range(2):
            part = sp_ref[q, pl.ds(g, count, stride=groups), :]
            zt_ref[q * half : q * half + count, g * LANES : (g + 1) * LANES] = part.astype(BF)
    return dot(z_down, twice(zt_ref[...]))


def slot_pairs(slab, slabs):
    return [(lax.rem(slab + d, slabs), lax.rem(slab + d + 1, slabs)) for d in range(1, slabs, 2)]


def pack_half(coeffs, pick_ref, pairs, packed_ref, h, sends):
    rows = coeffs.shape[0]
    capacity = packed_ref.shape[2]
    for i, targets in enumerate(pairs):
        part = dot(coeffs, pick_ref[:, 2 * i * capacity : 2 * (i + 1) * capacity]).astype(BF)
        for n, t in enumerate(targets):
            packed_ref[t, h * rows : (h + 1) * rows, :] = part[:, n * capacity : (n + 1) * capacity]
            if 2 * i + n < len(sends):
                sends[2 * i + n].start()


def synthesis_head(slab, recv_ref, pick_ref, z_up, y_up_ref, sp_ref, ws_ref):
    groups = KXY // GROUP
    rows = ws_ref.shape[1]
    planes_all = rows // groups
    slabs = recv_ref.shape[0]
    by_slot = jnp.concatenate([recv_ref[t] for pair in slot_pairs(slab, slabs) for t in pair], axis=1)
    chunk = 2 * LANES
    spectra = dot_nt(pick_ref[...], by_slot).astype(BF)
    spectra = jnp.concatenate([spectra, spectra], axis=1)
    for n in range(KXY * KXY // chunk):
        planes = dot_nt(z_up, spectra[n * chunk : (n + 1) * chunk])
        for gg in range(2):
            for q in range(2):
                sp_ref[q, pl.ds(2 * n + gg, planes_all, stride=groups), :] = planes[
                    q * planes_all : (q + 1) * planes_all, gg * LANES : (gg + 1) * LANES
                ]
    lhs = jnp.concatenate([sp_ref[q, :rows, :].astype(BF) for q in range(2)], axis=1)
    for j in range(ws_ref.shape[0] // 2):
        wide = dot(lhs, y_up_ref[:, j * chunk : (j + 1) * chunk])
        ws_ref[2 * j] = wide[:, :LANES]
        ws_ref[2 * j + 1] = wide[:, LANES:]


def gelu_pair(half):
    coeff = math.sqrt(2.0 / math.pi)
    square = half * half
    tangent = jnp.tanh(half * (2.0 * coeff + (8.0 * 0.044715 * coeff) * square))
    turned = half * tangent
    value = half + turned
    inner = 0.5 + (half - turned) * (coeff + (12.0 * 0.044715 * coeff) * square)
    return value, (value * (1.0 + tangent)) * inner


def final_kernel(per_step, slab_ref, gain_ref, value_ref, grad_ref, recv_ref, pick_ref, x_up_ref, y_up_ref, z_up_ref, value_hbm, out_ref, ws_ref, sp_ref, value_sem):
    step = pl.program_id(0)
    channels, planes = grad_ref.shape[:2]
    grid_len = grad_ref.shape[2]
    copies = [pltpu.make_async_copy(value_ref.at[c], value_hbm.at[c], value_sem.at[c]) for c in range(channels)]

    @pl.when(step == 0)
    def _():
        for copy in copies:
            copy.start()
        synthesis_head(slab_ref[0], recv_ref, pick_ref, z_up_ref[0], y_up_ref, sp_ref, ws_ref)

    def body(zz, carry):
        for c in range(channels):
            wp = plane_rows(ws_ref, c * planes + step * per_step + zz, grid_len).astype(BF)
            out_ref[c, zz] = (dot(x_up_ref[...], wp) + gain_ref[c] * grad_ref[c, step * per_step + zz].astype(F32)).astype(BF)
        return carry

    lax.fori_loop(0, per_step, body, 0)

    @pl.when(step == pl.num_programs(0) - 1)
    def _():
        for copy in copies:
            copy.wait()


def announce(targets):
    barrier = pltpu.get_barrier_semaphore()
    for target in targets:
        pl.semaphore_signal(barrier, inc=1, device_id=target, device_id_type=MESH)


def await_peers(targets):
    pl.semaphore_wait(pltpu.get_barrier_semaphore(), len(targets))


def reorder_weights(w_ref, wide_ref):
    width = w_ref.shape[3]
    slots = width // KZ
    flat = w_ref[...].reshape(-1, width)
    chunk = 2 * slots

    def body(n, carry):
        source = lax.broadcasted_iota(jnp.int32, (width, chunk), 0)
        lane = lax.broadcasted_iota(jnp.int32, (1, chunk), 1)
        wanted = jnp.where(lane < slots, lane * KZ, (lane - slots) * KZ + 1) + 2 * n
        moved = dot(flat, (source == wanted).astype(F32).astype(BF)).astype(BF)
        wide_ref[:, :, :, pl.ds(pl.multiple_of(n * chunk, chunk), chunk)] = moved.reshape(w_ref.shape[:3] + (chunk,))
        return carry

    lax.fori_loop(0, width // chunk, body, 0)


def peers_of(slabs, groups):
    slab, chan = lax.axis_index("slab"), lax.axis_index("chan")
    slab_peer = [(lax.rem(slab + d, slabs), chan) for d in range(1, slabs)]
    chan_peer = [(slab, lax.rem(chan + d, groups)) for d in range(1, groups)]
    return slab, chan, slab_peer, chan_peer


def spectra_copies(packed_ref, rx, peers, h, s_send, s_recv):
    rows = packed_ref.shape[1] // HALVES
    part = pl.ds(h * rows, rows)
    copies = []
    for d, peer in enumerate(peers):
        n = h * len(peers) + d
        copies.append(pltpu.make_async_remote_copy(
            src_ref=packed_ref.at[peer[0], part], dst_ref=rx.at[d, part], send_sem=s_send.at[n], recv_sem=s_recv.at[n],
            device_id=peer, device_id_type=MESH,
        ))
    return copies


def middle_part(slabs, groups, rows, gain_ref, bias_ref, recv_ref, wide_ref, pick_ref, x_down_ref, x_up_ref, y_down_ref, y_up_ref, z_down_ref, z_up_ref,
                out_ref, grad_ref, adjoint_ref, xs_ref, ws_ref, zt_ref, sp_ref, sa_ref, sb_ref, ga_ref, gb_ref, ma_ref, mb_ref, packed_ref, rx, tx2, rx2, mine, stage, *sems):
    slab, _, slab_peer, _ = peers_of(slabs, groups)
    channels, planes, grid_len, _ = out_ref.shape
    count = channels * planes
    synthesis_head(slab, recv_ref, pick_ref, z_up_ref[...], y_up_ref, sp_ref, ws_ref)

    def synth(t, s_ref, m_ref):
        c = t // planes
        m_ref[...] = out_ref[c, t - c * planes]
        shift = jnp.full((BIAS_ROWS, grid_len), 0.5 * bias_ref[c], F32)
        high = shift.astype(BF).astype(F32)
        row = lax.broadcasted_iota(jnp.int32, shift.shape, 0)
        shift = jnp.where(row == 0, high, jnp.where(row == 1, shift - high, 0.0))
        s_ref[...] = dot(x_up_ref[...], jnp.concatenate([plane_rows(ws_ref, t, grid_len), shift], axis=0).astype(BF))

    def point(t, s_ref, m_ref, g_ref):
        c = t // planes
        zz = t - c * planes
        gain = 0.5 * gain_ref[c]
        for start in range(0, grid_len, rows):
            span = slice(start, start + rows)
            value, grad = gelu_pair(s_ref[span, :] + gain * m_ref[span, :].astype(F32))
            grad = grad.astype(BF)
            out_ref[c, zz, span, :] = value.astype(BF)
            grad_ref[c, zz, span, :] = grad
            g_ref[span, :] = grad

    def down(t, g_ref):
        keep_x_rows(xs_ref, t, dot(x_down_ref[...], g_ref[...]))

    gb_ref[...] = jnp.zeros_like(gb_ref)
    synth(0, sa_ref, ma_ref)

    def body(j, carry):
        t = 2 * j
        synth(t + 1, sb_ref, mb_ref)
        down(jnp.maximum(t - 1, 0), gb_ref)
        point(t, sa_ref, ma_ref, ga_ref)
        synth(jnp.minimum(t + 2, count - 1), sa_ref, ma_ref)
        down(t, ga_ref)
        point(t + 1, sb_ref, mb_ref, gb_ref)
        return carry

    part = count // HALVES
    first = [spectra_copies(packed_ref, rx, slab_peer, h, *sems[:2]) for h in range(HALVES)]
    for h in range(HALVES):
        lax.fori_loop(h * part // 2, (h + 1) * part // 2, body, 0)
        down((h + 1) * part - 1, gb_ref)
        coeffs = local_spectra(xs_ref, y_down_ref, z_down_ref[...], zt_ref, sp_ref, h * part, part).astype(BF)
        pack_half(coeffs, pick_ref, slot_pairs(slab, slabs), packed_ref, h, first[h])
    exchange_body(slabs, groups, False, first, packed_ref, wide_ref, adjoint_ref, rx, tx2, rx2, mine, stage, *sems)


def exchange_body(slabs, groups, forward, first, packed_ref, wide_ref, recv_ref, rx, tx2, rx2, mine, stage, s_send, s_recv, c_send, c_recv, g_send, g_recv, shared=None, filler=None):
    slab, chan, slab_peer, chan_peer = peers_of(slabs, groups)
    rows, slots = packed_ref.shape[1] // PIECES, packed_ref.shape[2]
    kept = KZ // PIECES
    own = rx2.shape[1] // 2
    some = own // HALVES
    pairs = 2 * own
    outputs = own * groups
    wide = kept * slots
    step = min(kept, 4)

    def factor(piece, m):
        return 1.0 if piece == 0 and m == 0 else 2.0

    def at_m(piece, m, count=1):
        return slice((piece * kept + m) * slots, (piece * kept + m + count) * slots)

    def part_rows(h, q):
        return slice((2 * h + q) * some, (2 * h + q + 1) * some)

    half = packed_ref.shape[1] // HALVES
    for h in range(HALVES):
        span = slice(h * half, (h + 1) * half)
        total = packed_ref[slab, span, :].astype(F32)
        for d in range(1, slabs):
            first[h][d - 1].wait_recv()
            total = total + rx[d - 1, span, :].astype(F32)
        stage[span, :] = total
    common = None if shared is None else shared()
    second = []
    for p in range(PIECES):
        tiles = []
        for m in range(kept):
            base = [h * half + p * (half // PIECES) + m for h in range(HALVES)]
            tile = jnp.concatenate([stage[pl.ds(at, 2 * some, stride=kept), :] for at in base], axis=0)
            if common is not None:
                both = [common[(2 * p + q) * kept + m : (2 * p + q) * kept + m + 1, :] for q in range(2)]
                tile = tile + jnp.concatenate([jnp.broadcast_to(b, (some, slots)) for b in both] * HALVES, axis=0)
            tiles.append(tile)
        if forward:
            for m in range(0, kept, step):
                at = at_m(p, m, step)
                u = jnp.concatenate(tiles[m : m + step], axis=1)
                real = jnp.zeros((outputs, step * slots), F32)
                imag = jnp.zeros((outputs, step * slots), F32)
                for c in range(own):
                    w0, w1 = wide_ref[0, c, :, at].astype(F32), wide_ref[1, c, :, at].astype(F32)
                    h, k = c // some, c % some
                    ur, ui = u[2 * h * some + k : 2 * h * some + k + 1], u[(2 * h + 1) * some + k : (2 * h + 1) * some + k + 1]
                    real = real + (w0 * ur - w1 * ui)
                    imag = imag + (w1 * ur + w0 * ui)
                for e in range(groups):
                    mine_rows = slice(e * own, (e + 1) * own)
                    tx2[e, :, at] = jnp.concatenate([real[mine_rows], imag[mine_rows]], axis=0).astype(BF)
        else:
            for m in range(kept):
                tx2[0, :, at_m(p, m)] = (tiles[m] * factor(p, m)).astype(BF)
        lanes = pl.ds(p * wide, wide)
        copies = []
        for d in range(1, groups):
            peer = chan_peer[d - 1]
            n = p * (groups - 1) + d - 1
            copy = pltpu.make_async_remote_copy(
                src_ref=tx2.at[peer[1] if forward else 0, :, lanes], dst_ref=rx2.at[chan, :, lanes], send_sem=c_send.at[n], recv_sem=c_recv.at[n],
                device_id=peer, device_id_type=MESH,
            )
            copy.start()
            copies.append(copy)
        rx2[chan, :, lanes] = tx2[chan if forward else 0, :, lanes]
        second.append(copies)
    third = []
    for p in range(PIECES):
        for copy in second[p]:
            copy.wait_recv()
        for m in range(0, kept, step):
            at = at_m(p, m, step)
            if forward:
                result = rx2[0, :, at].astype(F32)
                for e in range(1, groups):
                    result = result + rx2[e, :, at].astype(F32)
            else:
                blocks = [rx2[e, :, at].astype(F32) for e in range(groups)]
                real = jnp.concatenate([b[part_rows(h, 0)] for b in blocks for h in range(HALVES)], axis=0)
                imag = jnp.concatenate([b[part_rows(h, 1)] for b in blocks for h in range(HALVES)], axis=0)
                reals, imags = [], []
                for c in range(own):
                    w0, w1 = wide_ref[0, c, :, at].astype(F32), wide_ref[1, c, :, at].astype(F32)
                    reals.append(jnp.sum(w0 * real + w1 * imag, axis=0, keepdims=True))
                    imags.append(jnp.sum(w0 * imag - w1 * real, axis=0, keepdims=True))
                result = jnp.concatenate(reals + imags, axis=0)
            for k in range(step):
                part = result[:, k * slots : (k + 1) * slots]
                stage[pl.ds(p * rows + m + k, pairs, stride=kept), :] = part * factor(p, m + k) if forward else part
        part = pl.ds(p * rows, rows)
        mine[part, :] = stage[part, :].astype(BF)
        for d in range(1, slabs):
            n = p * (slabs - 1) + d - 1
            copy = pltpu.make_async_remote_copy(
                src_ref=mine.at[part], dst_ref=recv_ref.at[slab, part], send_sem=g_send.at[n], recv_sem=g_recv.at[n],
                device_id=slab_peer[d - 1], device_id_type=MESH,
            )
            copy.start()
            third.append(copy)
    recv_ref[slab] = mine[...]
    if filler is not None:
        filler()
    for copy in third:
        copy.wait_recv()
    for copy in sum(first, []) + sum(second, []) + third:
        copy.wait_send()


def front_part(slabs, groups, field_hbm, forcing_hbm, slots_hbm, w_hbm, x_down_hbm, x_part_hbm, y_down_hbm, z_down_hbm, later, recv_ref, merged_ref, wide_ref, pick_ref,
               plane_ref, own_ref, xs_ref, xf_ref, zt_ref, sp_ref, packed_ref, rx, tx2, rx2, mine, stage, slot_ref, w_ref, x_down_ref, x_part_ref, y_down_ref, z_down_ref,
                 f_packed, f_rx, f_mine, f_rx2, f_sum, in_sem, field_sem, x_send, x_recv, p_send, p_recv, f_send, f_recv, h_send, h_recv, *sems):
    slab, chan, slab_peer, chan_peer = peers_of(slabs, groups)
    channels, planes = merged_ref.shape[:2]
    height = forcing_hbm.shape[1]
    chips = groups // 2
    chip, core = chan // 2, lax.rem(chan, 2)
    partner = (slab, chan + 1 - 2 * core)

    def near(t):
        return 2 * lax.rem(chip + chips + t, chips) + core

    def rows(index, start, count):
        return plane_ref.at[pl.ds(start, count), pl.ds(pl.multiple_of(index * height, height), height), :]

    fields = [pltpu.make_async_copy(field_hbm.at[c], merged_ref.at[c], field_sem.at[c]) for c in range(channels)]
    small = [
        pltpu.make_async_copy(forcing_hbm, own_ref, in_sem.at[0]),
        pltpu.make_async_copy(x_part_hbm.at[chan], x_part_ref, in_sem.at[1]),
        pltpu.make_async_copy(y_down_hbm, y_down_ref, in_sem.at[2]),
        pltpu.make_async_copy(z_down_hbm.at[slab], z_down_ref, in_sem.at[3]),
        pltpu.make_async_copy(slots_hbm, slot_ref, in_sem.at[4]),
        pltpu.make_async_copy(x_down_hbm, x_down_ref, in_sem.at[5]),
    ]
    load_w = pltpu.make_async_copy(w_hbm, w_ref, in_sem.at[6])
    place_own = pltpu.make_async_copy(forcing_hbm, rows(chan, 0, planes), in_sem.at[7])
    for copy in small + fields + [load_w, place_own] + later:
        copy.start()
    announce(slab_peer + chan_peer)
    for copy in small:
        copy.wait()

    def forcing_body(zz, carry):
        keep_x_rows(xf_ref, zz, dot(x_part_ref[...], own_ref[zz]))
        return carry

    lax.fori_loop(0, planes, forcing_body, 0, unroll=4)
    padded = local_spectra(xf_ref, y_down_ref, z_down_ref[...], zt_ref, sp_ref, 0, planes)
    kept = KZ // PIECES
    block = channels // HALVES * kept
    forced = jnp.concatenate([padded[n * block : n * block + kept] for n in range(2 * PIECES)], axis=0).astype(BF)
    columns = forced.shape[1]
    capacity = packed_ref.shape[2]
    pairs = slot_pairs(slab, slabs)
    for i, targets in enumerate(pairs):
        column = lax.broadcasted_iota(jnp.int32, (columns, 2 * capacity), 0)
        pick = (column == jnp.concatenate([slot_ref[pl.ds(t, 1), :] for t in targets], axis=1)).astype(F32).astype(BF)
        pick_ref[:, 2 * i * capacity : 2 * (i + 1) * capacity] = pick
        part = dot(forced, pick).astype(BF)
        for n, t in enumerate(targets):
            f_packed[t] = part[:, n * capacity : (n + 1) * capacity]
    await_peers(slab_peer + chan_peer)
    sent = []

    def send(copies):
        for copy in copies:
            copy.start()
            sent.append(copy)
        return copies

    forced_in = send([
        pltpu.make_async_remote_copy(
            src_ref=f_packed.at[slab_peer[d - 1][0]], dst_ref=f_rx.at[d - 1], send_sem=f_send.at[d - 1], recv_sem=f_recv.at[d - 1],
            device_id=slab_peer[d - 1], device_id_type=MESH,
        )
        for d in range(1, slabs)
    ])

    half = planes // 2

    def across(index, start, to, n, source=None):
        return pltpu.make_async_remote_copy(
            src_ref=rows(index, start, half) if source is None else source, dst_ref=rows(index, start, half),
            send_sem=x_send.at[n], recv_sem=x_recv.at[n], device_id=(slab, to), device_id_type=MESH,
        )

    def beside(index, start, count, n, source=None):
        return pltpu.make_async_remote_copy(
            src_ref=rows(index, start, count) if source is None else source, dst_ref=rows(index, start, count),
            send_sem=p_send.at[n], recv_sem=p_recv.at[n], device_id=partner, device_id_type=MESH,
        )

    def x_pass(c):
        fields[c].wait()

        def body(zz, carry):
            keep_x_rows(xs_ref, c * planes + zz, dot(x_down_ref[...], merged_ref[c, zz]))
            return carry

        lax.fori_loop(0, planes, body, 0, unroll=4)

    low, high = own_ref.at[pl.ds(0, half)], own_ref.at[pl.ds(half, half)]
    right_low, left_high, right_high, left_low = send([
        across(chan, 0, near(1), 0, low), across(chan, half, near(-1), 1, high),
        across(chan, half, near(1), 2, high), across(chan, 0, near(-1), 3, low),
    ])
    beside_all = send([beside(chan, 0, planes, 0, own_ref)])
    first = [spectra_copies(packed_ref, rx, slab_peer, h, *sems[:2]) for h in range(HALVES)]
    part = channels // HALVES

    def send_half(h):
        for c in range(h * part, (h + 1) * part):
            x_pass(c)
        coeffs = local_spectra(xs_ref, y_down_ref, z_down_ref[...], zt_ref, sp_ref, h * part * planes, part * planes).astype(BF)
        pack_half(coeffs, pick_ref, pairs, packed_ref, h, first[h])

    send_half(0)
    total = f_packed[slab].astype(F32)
    for d in range(1, slabs):
        forced_in[d - 1].wait_recv()
        total = total + f_rx[d - 1].astype(F32)
    f_mine[...] = total.astype(BF)
    shared_in = send([
        pltpu.make_async_remote_copy(
            src_ref=f_mine, dst_ref=f_rx2.at[chan], send_sem=h_send.at[d - 1], recv_sem=h_recv.at[d - 1],
            device_id=chan_peer[d - 1], device_id_type=MESH,
        )
        for d in range(1, groups)
    ])
    f_rx2[chan] = f_mine[...]
    right_low.wait_recv()
    left_high.wait_recv()
    far_low, far_high = send([across(near(-1), 0, near(1), 4), across(near(1), half, near(-1), 5)])
    beside_all += send([beside(near(-1), 0, half, 1), beside(near(1), half, half, 2)])
    for h in range(1, HALVES):
        send_half(h)
    right_high.wait_recv()
    left_low.wait_recv()
    beside_all += send([beside(near(-1), half, half, 3), beside(near(1), 0, half, 4)])
    load_w.wait()
    reorder_weights(w_ref, wide_ref)
    far_low.wait_recv()
    far_high.wait_recv()
    beside_all += send([beside(near(2), 0, half, 5), beside(near(2), half, half, 6)])

    def shared():
        for copy in shared_in:
            copy.wait_recv()
        common = f_rx2[0].astype(F32)
        for e in range(1, groups):
            common = common + f_rx2[e].astype(F32)
        f_sum[...] = common
        return f_sum

    def merge():
        place_own.wait()
        for copy in beside_all:
            copy.wait_recv()

        def body(zz, carry):
            for c in range(channels):
                merged_ref[c, zz] = merged_ref[c, zz] + plane_ref[zz]
            return carry

        lax.fori_loop(0, planes, body, 0)

    exchange_body(slabs, groups, True, first, packed_ref, wide_ref, recv_ref, rx, tx2, rx2, mine, stage, *sems, shared=shared, filler=merge)
    for copy in sent:
        copy.wait_send()
    for copy in later:
        copy.wait()


def spectral_kernel(slabs, groups, rows, gain_hbm, bias_hbm, field_hbm, forcing_hbm, slots_hbm, w_hbm, x_down_hbm, x_part_hbm, y_down_hbm, z_down_hbm, x_up_hbm, y_up_hbm, z_up_hbm,
                    out_ref, grad_ref, adjoint_ref, pick_ref, recv_ref, wide_ref, x_down_ref, x_up_ref, y_down_ref, y_up_ref, z_down_ref, z_up_ref,
                    xs_ref, ws_ref, zt_ref, sp_ref, sa_ref, sb_ref, ga_ref, gb_ref, ma_ref, mb_ref,
                    plane_ref, own_ref, xf_ref, slot_ref, w_ref, x_part_ref, f_packed, f_rx, f_mine, f_rx2, f_sum, gain_ref, bias_ref, later_sem, in_sem, field_sem, x_send, x_recv, p_send, p_recv, f_send, f_recv, h_send, h_recv, *rest):
    forward, adjoint = rest[:12], rest[12:]
    later = [
        pltpu.make_async_copy(x_up_hbm, x_up_ref, later_sem.at[0]),
        pltpu.make_async_copy(y_up_hbm, y_up_ref, later_sem.at[1]),
        pltpu.make_async_copy(z_up_hbm.at[lax.axis_index("slab")], z_up_ref, later_sem.at[2]),
        pltpu.make_async_copy(gain_hbm, gain_ref, later_sem.at[3]),
        pltpu.make_async_copy(bias_hbm, bias_ref, later_sem.at[4]),
    ]
    packed_ref, rx, tx2, rx2, mine, stage = forward[:6]
    front_part(slabs, groups, field_hbm, forcing_hbm, slots_hbm, w_hbm, x_down_hbm, x_part_hbm, y_down_hbm, z_down_hbm, later, recv_ref, out_ref, wide_ref, pick_ref,
               plane_ref, own_ref, xs_ref, xf_ref, zt_ref, sp_ref, packed_ref, rx, tx2, rx2, mine, stage, slot_ref, w_ref, x_down_ref, x_part_ref, y_down_ref, z_down_ref,
               f_packed, f_rx, f_mine, f_rx2, f_sum, in_sem, field_sem, x_send, x_recv, p_send, p_recv, f_send, f_recv, h_send, h_recv, *forward[6:])
    middle_part(slabs, groups, rows, gain_ref, bias_ref, recv_ref, wide_ref, pick_ref, x_down_ref, x_up_ref, y_down_ref, y_up_ref, z_down_ref, z_up_ref,
                out_ref, grad_ref, adjoint_ref, xs_ref, ws_ref, zt_ref, sp_ref, sa_ref, sb_ref, ga_ref, gb_ref, ma_ref, mb_ref, *adjoint)


def whole(shape):
    zeros = (0,) * len(shape)
    return pl.BlockSpec(shape, lambda *_: zeros, pipeline_mode=pl.Buffered(1))


class Sizes:
    def __init__(self, slabs, groups, channels, planes, grid_len, capacity):
        self.slabs, self.groups = slabs, groups
        self.channels, self.planes, self.grid_len = channels, planes, grid_len
        self.capacity = capacity
        planes_all = channels * planes
        x_down, x_up, y_down, y_up = plane_tables(grid_len)
        ones = np.zeros((grid_len, BIAS_ROWS), x_up.dtype)
        ones[:, :2] = 1
        half = bf16_table(0.5 * x_up.astype(np.float32))
        self.x_down, self.x_up, self.y_down, self.y_up = [jnp.asarray(t) for t in (x_down, x_up, y_down, y_up)]
        self.x_part = jnp.asarray(x_down.reshape(2 * KXY, groups, -1).transpose(1, 0, 2))
        self.x_up_half = jnp.asarray(np.concatenate([half, ones], axis=1))
        self.z_down, self.z_up = [jnp.asarray(t) for t in depth_tables(channels, planes, slabs, grid_len)]
        self.per_step = 4
        per_step = self.per_step
        self.steps = planes // per_step
        self.field_spec = pl.BlockSpec((channels, per_step, grid_len, grid_len), lambda i, s: (0, i, 0, 0))
        self.z_spec = pl.BlockSpec((1,) + self.z_up.shape[1:], lambda i, s: (s[0], 0, 0), pipeline_mode=pl.Buffered(1))
        self.packed_shape = (slabs, 2 * channels * KZ, capacity)
        self.volume = jax.ShapeDtypeStruct((channels, planes, grid_len, grid_len), BF)
        self.packed_out = jax.ShapeDtypeStruct(self.packed_shape, BF)
        self.wide_scratch = pltpu.VMEM((2 * GROUP * grid_len // LANES, planes_all * KXY // GROUP, LANES), F32)
        dma = pltpu.SemaphoreType.DMA
        self.exchange_sems = [dma((n,)) for n in [HALVES * (slabs - 1)] * 2 + [PIECES * (groups - 1)] * 2 + [PIECES * (slabs - 1)] * 2]
        self.sp_scratch = pltpu.VMEM((2, planes_all * KXY // GROUP, LANES), F32)
        self.zt_scratch = pltpu.VMEM((2 * planes_all // HALVES, KXY * KXY), BF)
        self.params = pltpu.CompilerParams(dimension_semantics=("arbitrary",), vmem_limit_bytes=14 << 20)


SMEM = pl.BlockSpec(memory_space=pltpu.SMEM)
VMEM = pl.BlockSpec(memory_space=pltpu.VMEM)
HBM = pl.BlockSpec(memory_space=pltpu.HBM)


def spectral_call(z, field, forcing, slot_column, w_spec, skip_gain, bias):
    block = z.packed_shape[1:]
    pair = (z.groups, 2 * z.channels, z.capacity * KZ)
    tiles = 2 * GROUP * z.grid_len // LANES
    forced = (2 * KZ, z.capacity)
    plane = (z.grid_len, z.grid_len)
    dma = pltpu.SemaphoreType.DMA
    operands = (skip_gain, bias, field, forcing, slot_column, w_spec, z.x_down, z.x_part, z.y_down, z.z_down, z.x_up_half, z.y_up, z.z_up)

    def scratch(kind, *shapes):
        return [pltpu.VMEM(shape, kind) for shape in shapes]

    exchange = scratch(BF, z.packed_shape, (z.slabs - 1,) + block, pair, pair, block) + scratch(F32, block) + z.exchange_sems
    return pl.pallas_call(
        functools.partial(spectral_kernel, z.slabs, z.groups, 64),
        out_shape=(z.volume, z.volume, z.packed_out, jax.ShapeDtypeStruct((KXY * KXY, slot_column.size), BF)),
        in_specs=[HBM] * len(operands),
        out_specs=(VMEM, VMEM, VMEM, VMEM),
        scratch_shapes=scratch(BF, z.packed_shape, w_spec.shape, z.x_down.shape, z.x_up_half.shape, z.y_down.shape, z.y_up.shape, z.z_down.shape[1:], z.z_up.shape[1:])
        + [z.wide_scratch, z.wide_scratch, z.zt_scratch, z.sp_scratch]
        + scratch(F32, plane, plane)
        + scratch(BF, plane, plane, plane, plane)
        + scratch(BF, (z.planes,) + plane, forcing.shape)
        + scratch(F32, (tiles, z.planes * KXY // GROUP, LANES))
        + scratch(jnp.int32, slot_column.shape)
        + scratch(BF, w_spec.shape, z.x_part.shape[1:], (z.slabs,) + forced, (z.slabs - 1,) + forced, forced, (z.groups,) + forced)
        + scratch(F32, forced)
        + [pltpu.SMEM((z.channels,), F32)] * 2
        + [dma((n,)) for n in [5, 8, z.channels, 6, 6, 7, 7] + [z.slabs - 1] * 2 + [z.groups - 1] * 2]
        + exchange
        + exchange,
        compiler_params=pltpu.CompilerParams(collective_id=1, has_side_effects=True, vmem_limit_bytes=SPECTRAL_VMEM),
        name="spectral",
    )(*[pltpu.with_memory_space_constraint(v, pltpu.HBM) for v in operands])


def final_call(z, where, skip_gain, value, grad_pre, adjoint, picks):
    return pl.pallas_call(
        functools.partial(final_kernel, z.per_step),
        out_shape=(z.volume, z.volume),
        grid_spec=pltpu.PrefetchScalarGridSpec(
            num_scalar_prefetch=1, grid=(z.steps,),
            in_specs=[SMEM, VMEM, VMEM, VMEM, VMEM, whole(z.x_up.shape), whole(z.y_up.shape), z.z_spec],
            out_specs=(HBM, z.field_spec),
            scratch_shapes=[z.wide_scratch, z.sp_scratch, pltpu.SemaphoreType.DMA((z.channels,))],
        ),
        compiler_params=z.params,
        name="synth_gradient",
    )(where, skip_gain, value, grad_pre, adjoint, picks, z.x_up, z.y_up, z.z_up)


def per_device(slabs, groups, field, forcing, slot_column, w_spec, skip_gain, bias):
    channels, planes, grid_len, _ = field.shape
    capacity = slot_column.shape[1]
    z = Sizes(slabs, groups, channels, planes, grid_len, capacity)
    where = lax.axis_index("slab").astype(jnp.int32).reshape(1)
    value, grad_pre, adjoint, picks = spectral_call(z, field, forcing, slot_column, w_spec, skip_gain, bias)
    return final_call(z, where, skip_gain, value, grad_pre, adjoint, picks)


def solution(mesh):
    placed = (
        P("chan", "slab", None, None),
        P("slab", "chan", None),
        P(),
        P(None, "chan", None, "slab"),
        P("chan"),
        P("chan"),
    )
    slabs, groups = mesh.shape["slab"], mesh.shape["chan"]
    return jax.shard_map(
        functools.partial(per_device, slabs, groups),
        mesh=mesh,
        in_specs=placed,
        out_specs=(P("chan", "slab", None, None), P("chan", "slab", None, None)),
        check_vma=False,
    )
```

```python
import functools
import math

import jax
import jax.numpy as jnp
import ml_dtypes
import numpy as np
from jax import lax
from jax.experimental import pallas as pl
from jax.experimental.pallas import tpu as pltpu
from jax.sharding import PartitionSpec as P

KXY = 32
KZ = 16
MESH = pl.DeviceIdType.MESH
BF = jnp.bfloat16
F32 = jnp.float32
LANES = 128
SPECTRAL_VMEM = 31 << 20
PIECES = 2
HALVES = 2
BIAS_ROWS = 16
GROUP = LANES // KXY


def bf16_table(values):
    return np.asarray(values, np.float32).astype(ml_dtypes.bfloat16)


def trig(freqs, coords, grid_len):
    angle = (np.outer(freqs, coords) % grid_len) * (2.0 * math.pi / grid_len)
    return np.cos(angle), np.sin(angle)


def plane_tables(grid_len):
    freqs = np.arange(KXY) - KXY // 2
    cos, sin = trig(freqs, np.arange(grid_len), grid_len)
    groups = KXY // GROUP
    scale = float(grid_len) ** -1.5
    x_down = np.zeros((GROUP, 2, groups, grid_len))
    x_up = np.zeros((grid_len, GROUP, 2, groups))
    y_down = np.zeros((GROUP, 2, grid_len, 2, GROUP, KXY))
    y_up = np.zeros((2, GROUP, KXY, GROUP, 2, grid_len))
    for k in range(GROUP):
        for g in range(groups):
            jx = g * GROUP + k
            x_down[k, 0, g], x_down[k, 1, g] = cos[jx], sin[jx]
            x_up[:, k, 0, g], x_up[:, k, 1, g] = scale * cos[jx], -scale * sin[jx]
        y_down[k, 0, :, 0, k], y_down[k, 1, :, 0, k] = cos.T, -sin.T
        y_down[k, 0, :, 1, k], y_down[k, 1, :, 1, k] = -sin.T, -cos.T
        y_up[0, k, :, k, 0], y_up[1, k, :, k, 0] = cos, -sin
        y_up[0, k, :, k, 1], y_up[1, k, :, k, 1] = sin, cos
    rows = 2 * KXY
    return (
        bf16_table(x_down.reshape(rows, grid_len)),
        bf16_table(x_up.reshape(grid_len, rows)),
        bf16_table(y_down.reshape(2 * GROUP * grid_len, 2 * LANES)),
        bf16_table(y_up.reshape(2 * LANES, 2 * GROUP * grid_len)),
    )


def depth_tables(channels, planes, slabs, grid_len):
    scale = float(grid_len) ** -1.5
    down, up = [], []
    for s in range(slabs):
        cos, sin = trig(np.arange(KZ), s * planes + np.arange(planes), grid_len)
        parts = [[cos, sin], [-sin, cos]]
        for store, count in ((down, channels // HALVES), (up, channels)):
            full = np.zeros((2, count, KZ, 2, count, planes))
            for q in range(2):
                for r in range(2):
                    full[q, :, :, r] = np.einsum("cd,mz->cmdz", np.eye(count), parts[q][r])
            full = full.reshape(2, count, PIECES, KZ // PIECES, -1).transpose(2, 0, 1, 3, 4)
            full = full.reshape(2 * count * KZ, 2 * count * planes)
            table = full * scale if store is down else full.T
            high = bf16_table(table)
            low = bf16_table(table - high.astype(np.float64))
            store.append(np.concatenate([high, low], axis=1))
    return np.stack(down), np.stack(up)


def dot(a, b):
    return jnp.dot(a, b, preferred_element_type=F32)


def dot_nt(a, b):
    return lax.dot_general(a, b, (((1,), (1,)), ((), ())), preferred_element_type=F32)


def twice(block):
    return jnp.concatenate([block, block], axis=0)


def tile_rows(plane):
    groups = KXY // GROUP
    return pl.ds(pl.multiple_of(plane * groups, groups), groups)


def keep_x_rows(xs_ref, plane, value):
    groups = KXY // GROUP
    tiles = value.shape[1] // LANES
    for kp in range(2 * GROUP):
        for h in range(tiles):
            xs_ref[kp * tiles + h, tile_rows(plane), :] = value[kp * groups : (kp + 1) * groups, h * LANES : (h + 1) * LANES]


def plane_rows(ws_ref, plane, width):
    tiles = width // LANES
    columns = []
    for h in range(tiles):
        parts = [ws_ref[kp * tiles + h, tile_rows(plane), :] for kp in range(2 * GROUP)]
        columns.append(jnp.concatenate(parts, axis=0))
    return jnp.concatenate(columns, axis=1)


def local_spectra(xs_ref, y_down_ref, z_down, zt_ref, sp_ref, start, count):
    groups = KXY // GROUP
    rows = slice(start * groups, (start + count) * groups)
    half = zt_ref.shape[0] // 2
    lhs = jnp.concatenate([xs_ref[j, rows, :].astype(BF) for j in range(xs_ref.shape[0])], axis=1)
    spectra = dot(lhs, y_down_ref[...])
    for q in range(2):
        sp_ref[q, : count * groups, :] = spectra[:, q * LANES : (q + 1) * LANES]
    if count < half:
        zt_ref[...] = jnp.zeros_like(zt_ref)
    for g in range(groups):
        for q in range(2):
            part = sp_ref[q, pl.ds(g, count, stride=groups), :]
            zt_ref[q * half : q * half + count, g * LANES : (g + 1) * LANES] = part.astype(BF)
    return dot(z_down, twice(zt_ref[...]))


def slot_pairs(slab, slabs):
    return [(lax.rem(slab + d, slabs), lax.rem(slab + d + 1, slabs)) for d in range(1, slabs, 2)]


def pack_half(coeffs, pick_ref, pairs, packed_ref, h, sends):
    rows = coeffs.shape[0]
    capacity = packed_ref.shape[2]
    for i, targets in enumerate(pairs):
        part = dot(coeffs, pick_ref[:, 2 * i * capacity : 2 * (i + 1) * capacity]).astype(BF)
        for n, t in enumerate(targets):
            packed_ref[t, h * rows : (h + 1) * rows, :] = part[:, n * capacity : (n + 1) * capacity]
            if 2 * i + n < len(sends):
                sends[2 * i + n].start()


def synthesis_head(slab, recv_ref, pick_ref, z_up, y_up_ref, sp_ref, ws_ref):
    groups = KXY // GROUP
    rows = ws_ref.shape[1]
    planes_all = rows // groups
    slabs = recv_ref.shape[0]
    by_slot = jnp.concatenate([recv_ref[t] for pair in slot_pairs(slab, slabs) for t in pair], axis=1)
    chunk = 2 * LANES
    spectra = dot_nt(pick_ref[...], by_slot).astype(BF)
    spectra = jnp.concatenate([spectra, spectra], axis=1)
    for n in range(KXY * KXY // chunk):
        planes = dot_nt(z_up, spectra[n * chunk : (n + 1) * chunk])
        for gg in range(2):
            for q in range(2):
                sp_ref[q, pl.ds(2 * n + gg, planes_all, stride=groups), :] = planes[
                    q * planes_all : (q + 1) * planes_all, gg * LANES : (gg + 1) * LANES
                ]
    lhs = jnp.concatenate([sp_ref[q, :rows, :].astype(BF) for q in range(2)], axis=1)
    for j in range(ws_ref.shape[0] // 2):
        wide = dot(lhs, y_up_ref[:, j * chunk : (j + 1) * chunk])
        ws_ref[2 * j] = wide[:, :LANES]
        ws_ref[2 * j + 1] = wide[:, LANES:]


def gelu_pair(half):
    coeff = math.sqrt(2.0 / math.pi)
    square = half * half
    tangent = jnp.tanh(half * (2.0 * coeff + (8.0 * 0.044715 * coeff) * square))
    turned = half * tangent
    value = half + turned
    inner = 0.5 + (half - turned) * (coeff + (12.0 * 0.044715 * coeff) * square)
    return value, (value * (1.0 + tangent)) * inner


def final_kernel(per_step, slab_ref, gain_ref, value_ref, grad_ref, recv_ref, pick_ref, x_up_ref, y_up_ref, z_up_ref, value_hbm, out_ref, ws_ref, sp_ref, value_sem):
    step = pl.program_id(0)
    channels, planes = grad_ref.shape[:2]
    grid_len = grad_ref.shape[2]
    copies = [pltpu.make_async_copy(value_ref.at[c], value_hbm.at[c], value_sem.at[c]) for c in range(channels)]

    @pl.when(step == 0)
    def _():
        for copy in copies:
            copy.start()
        synthesis_head(slab_ref[0], recv_ref, pick_ref, z_up_ref[0], y_up_ref, sp_ref, ws_ref)

    def body(zz, carry):
        for c in range(channels):
            wp = plane_rows(ws_ref, c * planes + step * per_step + zz, grid_len).astype(BF)
            out_ref[c, zz] = (dot(x_up_ref[...], wp) + gain_ref[c] * grad_ref[c, step * per_step + zz].astype(F32)).astype(BF)
        return carry

    lax.fori_loop(0, per_step, body, 0)

    @pl.when(step == pl.num_programs(0) - 1)
    def _():
        for copy in copies:
            copy.wait()


def announce(targets):
    barrier = pltpu.get_barrier_semaphore()
    for target in targets:
        pl.semaphore_signal(barrier, inc=1, device_id=target, device_id_type=MESH)


def await_peers(targets):
    pl.semaphore_wait(pltpu.get_barrier_semaphore(), len(targets))


def reorder_weights(w_ref, wide_ref):
    width = w_ref.shape[3]
    slots = width // KZ
    flat = w_ref[...].reshape(-1, width)
    chunk = 2 * slots

    def body(n, carry):
        source = lax.broadcasted_iota(jnp.int32, (width, chunk), 0)
        lane = lax.broadcasted_iota(jnp.int32, (1, chunk), 1)
        wanted = jnp.where(lane < slots, lane * KZ, (lane - slots) * KZ + 1) + 2 * n
        moved = dot(flat, (source == wanted).astype(F32).astype(BF)).astype(BF)
        wide_ref[:, :, :, pl.ds(pl.multiple_of(n * chunk, chunk), chunk)] = moved.reshape(w_ref.shape[:3] + (chunk,))
        return carry

    lax.fori_loop(0, width // chunk, body, 0)


def peers_of(slabs, groups):
    slab, chan = lax.axis_index("slab"), lax.axis_index("chan")
    slab_peer = [(lax.rem(slab + d, slabs), chan) for d in range(1, slabs)]
    chan_peer = [(slab, lax.rem(chan + d, groups)) for d in range(1, groups)]
    return slab, chan, slab_peer, chan_peer


def spectra_copies(packed_ref, rx, peers, h, s_send, s_recv):
    rows = packed_ref.shape[1] // HALVES
    part = pl.ds(h * rows, rows)
    copies = []
    for d, peer in enumerate(peers):
        n = h * len(peers) + d
        copies.append(pltpu.make_async_remote_copy(
            src_ref=packed_ref.at[peer[0], part], dst_ref=rx.at[d, part], send_sem=s_send.at[n], recv_sem=s_recv.at[n],
            device_id=peer, device_id_type=MESH,
        ))
    return copies


def middle_part(slabs, groups, rows, gain_ref, bias_ref, recv_ref, wide_ref, pick_ref, x_down_ref, x_up_ref, y_down_ref, y_up_ref, z_down_ref, z_up_ref,
                out_ref, grad_ref, adjoint_ref, xs_ref, ws_ref, zt_ref, sp_ref, sa_ref, sb_ref, ga_ref, gb_ref, ma_ref, mb_ref, packed_ref, rx, tx2, rx2, mine, stage, *sems):
    slab, _, slab_peer, _ = peers_of(slabs, groups)
    channels, planes, grid_len, _ = out_ref.shape
    count = channels * planes
    synthesis_head(slab, recv_ref, pick_ref, z_up_ref[...], y_up_ref, sp_ref, ws_ref)

    def synth(t, s_ref, m_ref):
        c = t // planes
        m_ref[...] = out_ref[c, t - c * planes]
        shift = jnp.full((BIAS_ROWS, grid_len), 0.5 * bias_ref[c], F32)
        high = shift.astype(BF).astype(F32)
        row = lax.broadcasted_iota(jnp.int32, shift.shape, 0)
        shift = jnp.where(row == 0, high, jnp.where(row == 1, shift - high, 0.0))
        s_ref[...] = dot(x_up_ref[...], jnp.concatenate([plane_rows(ws_ref, t, grid_len), shift], axis=0).astype(BF))

    def point(t, s_ref, m_ref, g_ref):
        c = t // planes
        zz = t - c * planes
        gain = 0.5 * gain_ref[c]
        for start in range(0, grid_len, rows):
            span = slice(start, start + rows)
            value, grad = gelu_pair(s_ref[span, :] + gain * m_ref[span, :].astype(F32))
            grad = grad.astype(BF)
            out_ref[c, zz, span, :] = value.astype(BF)
            grad_ref[c, zz, span, :] = grad
            g_ref[span, :] = grad

    def down(t, g_ref):
        keep_x_rows(xs_ref, t, dot(x_down_ref[...], g_ref[...]))

    gb_ref[...] = jnp.zeros_like(gb_ref)
    synth(0, sa_ref, ma_ref)

    def body(j, carry):
        t = 2 * j
        synth(t + 1, sb_ref, mb_ref)
        down(jnp.maximum(t - 1, 0), gb_ref)
        point(t, sa_ref, ma_ref, ga_ref)
        synth(jnp.minimum(t + 2, count - 1), sa_ref, ma_ref)
        down(t, ga_ref)
        point(t + 1, sb_ref, mb_ref, gb_ref)
        return carry

    part = count // HALVES
    first = [spectra_copies(packed_ref, rx, slab_peer, h, *sems[:2]) for h in range(HALVES)]
    for h in range(HALVES):
        lax.fori_loop(h * part // 2, (h + 1) * part // 2, body, 0)
        down((h + 1) * part - 1, gb_ref)
        coeffs = local_spectra(xs_ref, y_down_ref, z_down_ref[...], zt_ref, sp_ref, h * part, part).astype(BF)
        pack_half(coeffs, pick_ref, slot_pairs(slab, slabs), packed_ref, h, first[h])
    exchange_body(slabs, groups, False, first, packed_ref, wide_ref, adjoint_ref, rx, tx2, rx2, mine, stage, *sems)


def exchange_body(slabs, groups, forward, first, packed_ref, wide_ref, recv_ref, rx, tx2, rx2, mine, stage, s_send, s_recv, c_send, c_recv, g_send, g_recv, shared=None, filler=None):
    slab, chan, slab_peer, chan_peer = peers_of(slabs, groups)
    rows, slots = packed_ref.shape[1] // PIECES, packed_ref.shape[2]
    kept = KZ // PIECES
    own = rx2.shape[1] // 2
    some = own // HALVES
    pairs = 2 * own
    outputs = own * groups
    wide = kept * slots
    step = min(kept, 4)

    def factor(piece, m):
        return 1.0 if piece == 0 and m == 0 else 2.0

    def at_m(piece, m, count=1):
        return slice((piece * kept + m) * slots, (piece * kept + m + count) * slots)

    def part_rows(h, q):
        return slice((2 * h + q) * some, (2 * h + q + 1) * some)

    half = packed_ref.shape[1] // HALVES
    for h in range(HALVES):
        span = slice(h * half, (h + 1) * half)
        total = packed_ref[slab, span, :].astype(F32)
        for d in range(1, slabs):
            first[h][d - 1].wait_recv()
            total = total + rx[d - 1, span, :].astype(F32)
        stage[span, :] = total
    common = None if shared is None else shared()
    second = []
    for p in range(PIECES):
        tiles = []
        for m in range(kept):
            base = [h * half + p * (half // PIECES) + m for h in range(HALVES)]
            tile = jnp.concatenate([stage[pl.ds(at, 2 * some, stride=kept), :] for at in base], axis=0)
            if common is not None:
                both = [common[(2 * p + q) * kept + m : (2 * p + q) * kept + m + 1, :] for q in range(2)]
                tile = tile + jnp.concatenate([jnp.broadcast_to(b, (some, slots)) for b in both] * HALVES, axis=0)
            tiles.append(tile)
        if forward:
            for m in range(0, kept, step):
                at = at_m(p, m, step)
                u = jnp.concatenate(tiles[m : m + step], axis=1)
                real = jnp.zeros((outputs, step * slots), F32)
                imag = jnp.zeros((outputs, step * slots), F32)
                for c in range(own):
                    w0, w1 = wide_ref[0, c, :, at].astype(F32), wide_ref[1, c, :, at].astype(F32)
                    h, k = c // some, c % some
                    ur, ui = u[2 * h * some + k : 2 * h * some + k + 1], u[(2 * h + 1) * some + k : (2 * h + 1) * some + k + 1]
                    real = real + (w0 * ur - w1 * ui)
                    imag = imag + (w1 * ur + w0 * ui)
                for e in range(groups):
                    mine_rows = slice(e * own, (e + 1) * own)
                    tx2[e, :, at] = jnp.concatenate([real[mine_rows], imag[mine_rows]], axis=0).astype(BF)
        else:
            for m in range(kept):
                tx2[0, :, at_m(p, m)] = (tiles[m] * factor(p, m)).astype(BF)
        lanes = pl.ds(p * wide, wide)
        copies = []
        for d in range(1, groups):
            peer = chan_peer[d - 1]
            n = p * (groups - 1) + d - 1
            copy = pltpu.make_async_remote_copy(
                src_ref=tx2.at[peer[1] if forward else 0, :, lanes], dst_ref=rx2.at[chan, :, lanes], send_sem=c_send.at[n], recv_sem=c_recv.at[n],
                device_id=peer, device_id_type=MESH,
            )
            copy.start()
            copies.append(copy)
        rx2[chan, :, lanes] = tx2[chan if forward else 0, :, lanes]
        second.append(copies)
    side = math.isqrt(slabs)
    y, z = slab // side, lax.rem(slab, side)
    offsets = [(a, b) for a in range(side) for b in range(side) if a or b]
    offsets.sort(key=lambda o: -min(o[0], side - o[0]) - min(o[1], side - o[1]))
    far_first = [lax.rem(y + a, side) * side + lax.rem(z + b, side) for a, b in offsets]
    third = []
    for p in range(PIECES):
        for copy in second[p]:
            copy.wait_recv()
        for m in range(0, kept, step):
            at = at_m(p, m, step)
            if forward:
                result = rx2[0, :, at].astype(F32)
                for e in range(1, groups):
                    result = result + rx2[e, :, at].astype(F32)
            else:
                blocks = [rx2[e, :, at].astype(F32) for e in range(groups)]
                real = jnp.concatenate([b[part_rows(h, 0)] for b in blocks for h in range(HALVES)], axis=0)
                imag = jnp.concatenate([b[part_rows(h, 1)] for b in blocks for h in range(HALVES)], axis=0)
                reals, imags = [], []
                for c in range(own):
                    w0, w1 = wide_ref[0, c, :, at].astype(F32), wide_ref[1, c, :, at].astype(F32)
                    reals.append(jnp.sum(w0 * real + w1 * imag, axis=0, keepdims=True))
                    imags.append(jnp.sum(w0 * imag - w1 * real, axis=0, keepdims=True))
                result = jnp.concatenate(reals + imags, axis=0)
            for k in range(step):
                part = result[:, k * slots : (k + 1) * slots]
                stage[pl.ds(p * rows + m + k, pairs, stride=kept), :] = part * factor(p, m + k) if forward else part
        part = pl.ds(p * rows, rows)
        mine[part, :] = stage[part, :].astype(BF)
        for d, target in enumerate(far_first):
            n = p * (slabs - 1) + d
            copy = pltpu.make_async_remote_copy(
                src_ref=mine.at[part], dst_ref=recv_ref.at[slab, part], send_sem=g_send.at[n], recv_sem=g_recv.at[n],
                device_id=(target, chan), device_id_type=MESH,
            )
            copy.start()
            third.append(copy)
    recv_ref[slab] = mine[...]
    if filler is not None:
        filler()
    for copy in third:
        copy.wait_recv()
    for copy in sum(first, []) + sum(second, []) + third:
        copy.wait_send()


def front_part(slabs, groups, field_hbm, forcing_hbm, slots_hbm, w_hbm, x_down_hbm, x_part_hbm, y_down_hbm, z_down_hbm, later, recv_ref, merged_ref, wide_ref, pick_ref,
               plane_ref, own_ref, xs_ref, xf_ref, zt_ref, sp_ref, packed_ref, rx, tx2, rx2, mine, stage, slot_ref, w_ref, x_down_ref, x_part_ref, y_down_ref, z_down_ref,
                 f_packed, f_rx, f_mine, f_rx2, f_sum, in_sem, field_sem, x_send, x_recv, p_send, p_recv, f_send, f_recv, h_send, h_recv, *sems):
    slab, chan, slab_peer, chan_peer = peers_of(slabs, groups)
    channels, planes = merged_ref.shape[:2]
    height = forcing_hbm.shape[1]
    chips = groups // 2
    chip, core = chan // 2, lax.rem(chan, 2)
    partner = (slab, chan + 1 - 2 * core)

    def near(t):
        return 2 * lax.rem(chip + chips + t, chips) + core

    def rows(index, start, count):
        return plane_ref.at[pl.ds(start, count), pl.ds(pl.multiple_of(index * height, height), height), :]

    fields = [pltpu.make_async_copy(field_hbm.at[c], merged_ref.at[c], field_sem.at[c]) for c in range(channels)]
    small = [
        pltpu.make_async_copy(forcing_hbm, own_ref, in_sem.at[0]),
        pltpu.make_async_copy(x_part_hbm.at[chan], x_part_ref, in_sem.at[1]),
        pltpu.make_async_copy(y_down_hbm, y_down_ref, in_sem.at[2]),
        pltpu.make_async_copy(z_down_hbm.at[slab], z_down_ref, in_sem.at[3]),
        pltpu.make_async_copy(slots_hbm, slot_ref, in_sem.at[4]),
        pltpu.make_async_copy(x_down_hbm, x_down_ref, in_sem.at[5]),
    ]
    load_w = pltpu.make_async_copy(w_hbm, w_ref, in_sem.at[6])
    place_own = pltpu.make_async_copy(forcing_hbm, rows(chan, 0, planes), in_sem.at[7])
    for copy in small + fields + [load_w, place_own] + later:
        copy.start()
    announce(slab_peer + chan_peer)
    for copy in small:
        copy.wait()

    def forcing_body(zz, carry):
        keep_x_rows(xf_ref, zz, dot(x_part_ref[...], own_ref[zz]))
        return carry

    lax.fori_loop(0, planes, forcing_body, 0, unroll=4)
    padded = local_spectra(xf_ref, y_down_ref, z_down_ref[...], zt_ref, sp_ref, 0, planes)
    kept = KZ // PIECES
    block = channels // HALVES * kept
    forced = jnp.concatenate([padded[n * block : n * block + kept] for n in range(2 * PIECES)], axis=0).astype(BF)
    columns = forced.shape[1]
    capacity = packed_ref.shape[2]
    pairs = slot_pairs(slab, slabs)
    for i, targets in enumerate(pairs):
        column = lax.broadcasted_iota(jnp.int32, (columns, 2 * capacity), 0)
        pick = (column == jnp.concatenate([slot_ref[pl.ds(t, 1), :] for t in targets], axis=1)).astype(F32).astype(BF)
        pick_ref[:, 2 * i * capacity : 2 * (i + 1) * capacity] = pick
        part = dot(forced, pick).astype(BF)
        for n, t in enumerate(targets):
            f_packed[t] = part[:, n * capacity : (n + 1) * capacity]
    await_peers(slab_peer + chan_peer)
    sent = []

    def send(copies):
        for copy in copies:
            copy.start()
            sent.append(copy)
        return copies

    forced_in = send([
        pltpu.make_async_remote_copy(
            src_ref=f_packed.at[slab_peer[d - 1][0]], dst_ref=f_rx.at[d - 1], send_sem=f_send.at[d - 1], recv_sem=f_recv.at[d - 1],
            device_id=slab_peer[d - 1], device_id_type=MESH,
        )
        for d in range(1, slabs)
    ])

    half = planes // 2

    def across(index, start, to, n, source=None):
        return pltpu.make_async_remote_copy(
            src_ref=rows(index, start, half) if source is None else source, dst_ref=rows(index, start, half),
            send_sem=x_send.at[n], recv_sem=x_recv.at[n], device_id=(slab, to), device_id_type=MESH,
        )

    def beside(index, start, count, n, source=None):
        return pltpu.make_async_remote_copy(
            src_ref=rows(index, start, count) if source is None else source, dst_ref=rows(index, start, count),
            send_sem=p_send.at[n], recv_sem=p_recv.at[n], device_id=partner, device_id_type=MESH,
        )

    def x_pass(c):
        fields[c].wait()

        def body(zz, carry):
            keep_x_rows(xs_ref, c * planes + zz, dot(x_down_ref[...], merged_ref[c, zz]))
            return carry

        lax.fori_loop(0, planes, body, 0, unroll=4)

    low, high = own_ref.at[pl.ds(0, half)], own_ref.at[pl.ds(half, half)]
    right_low, left_high, right_high, left_low = send([
        across(chan, 0, near(1), 0, low), across(chan, half, near(-1), 1, high),
        across(chan, half, near(1), 2, high), across(chan, 0, near(-1), 3, low),
    ])
    beside_all = send([beside(chan, 0, planes, 0, own_ref)])
    first = [spectra_copies(packed_ref, rx, slab_peer, h, *sems[:2]) for h in range(HALVES)]
    part = channels // HALVES

    def send_half(h):
        for c in range(h * part, (h + 1) * part):
            x_pass(c)
        coeffs = local_spectra(xs_ref, y_down_ref, z_down_ref[...], zt_ref, sp_ref, h * part * planes, part * planes).astype(BF)
        pack_half(coeffs, pick_ref, pairs, packed_ref, h, first[h])

    send_half(0)
    total = f_packed[slab].astype(F32)
    for d in range(1, slabs):
        forced_in[d - 1].wait_recv()
        total = total + f_rx[d - 1].astype(F32)
    f_mine[...] = total.astype(BF)
    shared_in = send([
        pltpu.make_async_remote_copy(
            src_ref=f_mine, dst_ref=f_rx2.at[chan], send_sem=h_send.at[d - 1], recv_sem=h_recv.at[d - 1],
            device_id=chan_peer[d - 1], device_id_type=MESH,
        )
        for d in range(1, groups)
    ])
    f_rx2[chan] = f_mine[...]
    right_low.wait_recv()
    left_high.wait_recv()
    far_low, far_high = send([across(near(-1), 0, near(1), 4), across(near(1), half, near(-1), 5)])
    beside_all += send([beside(near(-1), 0, half, 1), beside(near(1), half, half, 2)])
    for h in range(1, HALVES):
        send_half(h)
    right_high.wait_recv()
    left_low.wait_recv()
    beside_all += send([beside(near(-1), half, half, 3), beside(near(1), 0, half, 4)])
    load_w.wait()
    reorder_weights(w_ref, wide_ref)
    far_low.wait_recv()
    far_high.wait_recv()
    beside_all += send([beside(near(2), 0, half, 5), beside(near(2), half, half, 6)])

    def shared():
        for copy in shared_in:
            copy.wait_recv()
        common = f_rx2[0].astype(F32)
        for e in range(1, groups):
            common = common + f_rx2[e].astype(F32)
        f_sum[...] = common
        return f_sum

    def merge():
        place_own.wait()
        for copy in beside_all:
            copy.wait_recv()

        def body(zz, carry):
            for c in range(channels):
                merged_ref[c, zz] = merged_ref[c, zz] + plane_ref[zz]
            return carry

        lax.fori_loop(0, planes, body, 0)

    exchange_body(slabs, groups, True, first, packed_ref, wide_ref, recv_ref, rx, tx2, rx2, mine, stage, *sems, shared=shared, filler=merge)
    for copy in sent:
        copy.wait_send()
    for copy in later:
        copy.wait()


def spectral_kernel(slabs, groups, rows, gain_hbm, bias_hbm, field_hbm, forcing_hbm, slots_hbm, w_hbm, x_down_hbm, x_part_hbm, y_down_hbm, z_down_hbm, x_up_hbm, y_up_hbm, z_up_hbm,
                    out_ref, grad_ref, adjoint_ref, pick_ref, recv_ref, wide_ref, x_down_ref, x_up_ref, y_down_ref, y_up_ref, z_down_ref, z_up_ref,
                    xs_ref, ws_ref, zt_ref, sp_ref, sa_ref, sb_ref, ga_ref, gb_ref, ma_ref, mb_ref,
                    plane_ref, own_ref, xf_ref, slot_ref, w_ref, x_part_ref, f_packed, f_rx, f_mine, f_rx2, f_sum, gain_ref, bias_ref, later_sem, in_sem, field_sem, x_send, x_recv, p_send, p_recv, f_send, f_recv, h_send, h_recv, *rest):
    forward, adjoint = rest[:12], rest[12:]
    later = [
        pltpu.make_async_copy(x_up_hbm, x_up_ref, later_sem.at[0]),
        pltpu.make_async_copy(y_up_hbm, y_up_ref, later_sem.at[1]),
        pltpu.make_async_copy(z_up_hbm.at[lax.axis_index("slab")], z_up_ref, later_sem.at[2]),
        pltpu.make_async_copy(gain_hbm, gain_ref, later_sem.at[3]),
        pltpu.make_async_copy(bias_hbm, bias_ref, later_sem.at[4]),
    ]
    packed_ref, rx, tx2, rx2, mine, stage = forward[:6]
    front_part(slabs, groups, field_hbm, forcing_hbm, slots_hbm, w_hbm, x_down_hbm, x_part_hbm, y_down_hbm, z_down_hbm, later, recv_ref, out_ref, wide_ref, pick_ref,
               plane_ref, own_ref, xs_ref, xf_ref, zt_ref, sp_ref, packed_ref, rx, tx2, rx2, mine, stage, slot_ref, w_ref, x_down_ref, x_part_ref, y_down_ref, z_down_ref,
               f_packed, f_rx, f_mine, f_rx2, f_sum, in_sem, field_sem, x_send, x_recv, p_send, p_recv, f_send, f_recv, h_send, h_recv, *forward[6:])
    middle_part(slabs, groups, rows, gain_ref, bias_ref, recv_ref, wide_ref, pick_ref, x_down_ref, x_up_ref, y_down_ref, y_up_ref, z_down_ref, z_up_ref,
                out_ref, grad_ref, adjoint_ref, xs_ref, ws_ref, zt_ref, sp_ref, sa_ref, sb_ref, ga_ref, gb_ref, ma_ref, mb_ref, *adjoint)


def whole(shape):
    zeros = (0,) * len(shape)
    return pl.BlockSpec(shape, lambda *_: zeros, pipeline_mode=pl.Buffered(1))


class Sizes:
    def __init__(self, slabs, groups, channels, planes, grid_len, capacity):
        self.slabs, self.groups = slabs, groups
        self.channels, self.planes, self.grid_len = channels, planes, grid_len
        self.capacity = capacity
        planes_all = channels * planes
        x_down, x_up, y_down, y_up = plane_tables(grid_len)
        ones = np.zeros((grid_len, BIAS_ROWS), x_up.dtype)
        ones[:, :2] = 1
        half = bf16_table(0.5 * x_up.astype(np.float32))
        self.x_down, self.x_up, self.y_down, self.y_up = [jnp.asarray(t) for t in (x_down, x_up, y_down, y_up)]
        self.x_part = jnp.asarray(x_down.reshape(2 * KXY, groups, -1).transpose(1, 0, 2))
        self.x_up_half = jnp.asarray(np.concatenate([half, ones], axis=1))
        self.z_down, self.z_up = [jnp.asarray(t) for t in depth_tables(channels, planes, slabs, grid_len)]
        self.per_step = 4
        per_step = self.per_step
        self.steps = planes // per_step
        self.field_spec = pl.BlockSpec((channels, per_step, grid_len, grid_len), lambda i, s: (0, i, 0, 0))
        self.z_spec = pl.BlockSpec((1,) + self.z_up.shape[1:], lambda i, s: (s[0], 0, 0), pipeline_mode=pl.Buffered(1))
        self.packed_shape = (slabs, 2 * channels * KZ, capacity)
        self.volume = jax.ShapeDtypeStruct((channels, planes, grid_len, grid_len), BF)
        self.packed_out = jax.ShapeDtypeStruct(self.packed_shape, BF)
        self.wide_scratch = pltpu.VMEM((2 * GROUP * grid_len // LANES, planes_all * KXY // GROUP, LANES), F32)
        dma = pltpu.SemaphoreType.DMA
        self.exchange_sems = [dma((n,)) for n in [HALVES * (slabs - 1)] * 2 + [PIECES * (groups - 1)] * 2 + [PIECES * (slabs - 1)] * 2]
        self.sp_scratch = pltpu.VMEM((2, planes_all * KXY // GROUP, LANES), F32)
        self.zt_scratch = pltpu.VMEM((2 * planes_all // HALVES, KXY * KXY), BF)
        self.params = pltpu.CompilerParams(dimension_semantics=("arbitrary",), vmem_limit_bytes=14 << 20)


SMEM = pl.BlockSpec(memory_space=pltpu.SMEM)
VMEM = pl.BlockSpec(memory_space=pltpu.VMEM)
HBM = pl.BlockSpec(memory_space=pltpu.HBM)


def spectral_call(z, field, forcing, slot_column, w_spec, skip_gain, bias):
    block = z.packed_shape[1:]
    pair = (z.groups, 2 * z.channels, z.capacity * KZ)
    tiles = 2 * GROUP * z.grid_len // LANES
    forced = (2 * KZ, z.capacity)
    plane = (z.grid_len, z.grid_len)
    dma = pltpu.SemaphoreType.DMA
    operands = (skip_gain, bias, field, forcing, slot_column, w_spec, z.x_down, z.x_part, z.y_down, z.z_down, z.x_up_half, z.y_up, z.z_up)

    def scratch(kind, *shapes):
        return [pltpu.VMEM(shape, kind) for shape in shapes]

    exchange = scratch(BF, z.packed_shape, (z.slabs - 1,) + block, pair, pair, block) + scratch(F32, block) + z.exchange_sems
    return pl.pallas_call(
        functools.partial(spectral_kernel, z.slabs, z.groups, 64),
        out_shape=(z.volume, z.volume, z.packed_out, jax.ShapeDtypeStruct((KXY * KXY, slot_column.size), BF)),
        in_specs=[HBM] * len(operands),
        out_specs=(VMEM, VMEM, VMEM, VMEM),
        scratch_shapes=scratch(BF, z.packed_shape, w_spec.shape, z.x_down.shape, z.x_up_half.shape, z.y_down.shape, z.y_up.shape, z.z_down.shape[1:], z.z_up.shape[1:])
        + [z.wide_scratch, z.wide_scratch, z.zt_scratch, z.sp_scratch]
        + scratch(F32, plane, plane)
        + scratch(BF, plane, plane, plane, plane)
        + scratch(BF, (z.planes,) + plane, forcing.shape)
        + scratch(F32, (tiles, z.planes * KXY // GROUP, LANES))
        + scratch(jnp.int32, slot_column.shape)
        + scratch(BF, w_spec.shape, z.x_part.shape[1:], (z.slabs,) + forced, (z.slabs - 1,) + forced, forced, (z.groups,) + forced)
        + scratch(F32, forced)
        + [pltpu.SMEM((z.channels,), F32)] * 2
        + [dma((n,)) for n in [5, 8, z.channels, 6, 6, 7, 7] + [z.slabs - 1] * 2 + [z.groups - 1] * 2]
        + exchange
        + exchange,
        compiler_params=pltpu.CompilerParams(collective_id=1, has_side_effects=True, vmem_limit_bytes=SPECTRAL_VMEM),
        name="spectral",
    )(*[pltpu.with_memory_space_constraint(v, pltpu.HBM) for v in operands])


def final_call(z, where, skip_gain, value, grad_pre, adjoint, picks):
    return pl.pallas_call(
        functools.partial(final_kernel, z.per_step),
        out_shape=(z.volume, z.volume),
        grid_spec=pltpu.PrefetchScalarGridSpec(
            num_scalar_prefetch=1, grid=(z.steps,),
            in_specs=[SMEM, VMEM, VMEM, VMEM, VMEM, whole(z.x_up.shape), whole(z.y_up.shape), z.z_spec],
            out_specs=(HBM, z.field_spec),
            scratch_shapes=[z.wide_scratch, z.sp_scratch, pltpu.SemaphoreType.DMA((z.channels,))],
        ),
        compiler_params=z.params,
        name="synth_gradient",
    )(where, skip_gain, value, grad_pre, adjoint, picks, z.x_up, z.y_up, z.z_up)


def per_device(slabs, groups, field, forcing, slot_column, w_spec, skip_gain, bias):
    channels, planes, grid_len, _ = field.shape
    capacity = slot_column.shape[1]
    z = Sizes(slabs, groups, channels, planes, grid_len, capacity)
    where = lax.axis_index("slab").astype(jnp.int32).reshape(1)
    value, grad_pre, adjoint, picks = spectral_call(z, field, forcing, slot_column, w_spec, skip_gain, bias)
    return final_call(z, where, skip_gain, value, grad_pre, adjoint, picks)


def solution(mesh):
    placed = (
        P("chan", "slab", None, None),
        P("slab", "chan", None),
        P(),
        P(None, "chan", None, "slab"),
        P("chan"),
        P("chan"),
    )
    slabs, groups = mesh.shape["slab"], mesh.shape["chan"]
    return jax.shard_map(
        functools.partial(per_device, slabs, groups),
        mesh=mesh,
        in_specs=placed,
        out_specs=(P("chan", "slab", None, None), P("chan", "slab", None, None)),
        check_vma=False,
    )
```
